32 devices in a mesh: fsdp: 8 (over z, x), tensor: 4 (over y, core).
Axes of the slice: x: 2, y: 2, z: 4, core: 2. Of those that a mesh axis runs over, the one named last changes fastest.
Arguments:
- hidden_in: bfloat16 [8192, 768], P(('fsdp', 'tensor')), may hold values from -6 to 6
- time_embed: bfloat16 [8, 768], P('fsdp'), may hold values from -6 to 6
- segment_ids: int32 [8, 1024], P('fsdp'), may hold values from -1 to 7, as said below
- cotangent: bfloat16 [8192, 768], P(('fsdp', 'tensor')), may hold values from -6 to 6
- query_weight: bfloat16 [2, 768, 768], P(None, 'fsdp', 'tensor'), may hold values from -0.21875 to 0.21875
- key_weight: bfloat16 [2, 768, 768], P(None, 'fsdp', 'tensor'), may hold values from -0.21875 to 0.21875
- value_weight: bfloat16 [2, 768, 768], P(None, 'fsdp', 'tensor'), may hold values from -0.21875 to 0.21875
- output_weight: bfloat16 [2, 768, 768], P(None, 'tensor', 'fsdp'), may hold values from -1.75 to 1.75
- up_weight: bfloat16 [2, 768, 3072], P(None, 'fsdp', 'tensor'), may hold values from -0.21875 to 0.21875
- down_weight: bfloat16 [2, 3072, 768], P(None, 'tensor', 'fsdp'), may hold values from -0.109375 to 0.109375
- query_bias: float32 [2, 768], P(None, 'tensor'), may hold values from -3 to 3
- value_bias: float32 [2, 768], P(None, 'tensor'), may hold values from -3 to 3
- output_bias: float32 [2, 768], replicated, may hold values from -3 to 3
- up_bias: float32 [2, 3072], P(None, 'tensor'), may hold values from -3 to 3
- down_bias: float32 [2, 768], replicated, may hold values from -3 to 3
- first_gain: float32 [2, 768], replicated, may hold values from 0.25 to 1.75
- first_shift: float32 [2, 768], replicated, may hold values from -3 to 3
- second_gain: float32 [2, 768], replicated, may hold values from 0.25 to 1.75
- second_shift: float32 [2, 768], replicated, may hold values from -3 to 3
Outputs:
- denoised: bfloat16 [8192, 768], P(('fsdp', 'tensor'))
- input_grad: float32 [8192, 768], P(('fsdp', 'tensor'))
- query_weight_grad: float32 [2, 768, 768], P(None, 'fsdp', 'tensor')
- key_weight_grad: float32 [2, 768, 768], P(None, 'fsdp', 'tensor')
- value_weight_grad: float32 [2, 768, 768], P(None, 'fsdp', 'tensor')
- output_weight_grad: float32 [2, 768, 768], P(None, 'tensor', 'fsdp')
- up_weight_grad: float32 [2, 768, 3072], P(None, 'fsdp', 'tensor')
- down_weight_grad: float32 [2, 3072, 768], P(None, 'tensor', 'fsdp')
- query_bias_grad: float32 [2, 768], P(None, 'tensor')
- value_bias_grad: float32 [2, 768], P(None, 'tensor')
- output_bias_grad: float32 [2, 768], replicated
- up_bias_grad: float32 [2, 3072], P(None, 'tensor')
- down_bias_grad: float32 [2, 768], replicated
- first_gain_grad: float32 [2, 768], replicated
- first_shift_grad: float32 [2, 768], replicated
- second_gain_grad: float32 [2, 768], replicated
- second_shift_grad: float32 [2, 768], replicated
The draws below stay inside these ranges and needn't reach their ends.
Inputs may be any that keep to these rules, and one draw needn't show every extreme that they name: `segment_ids`: each sequence holds 8 documents of at least one token in order 0 to 7, followed by padding of at least one token.
All inputs are finite; a program needn't handle non-finite values.
Results may differ from the reference program's by a relative error of at most 0.015.
Values may be sent and summed in bfloat16 or wider, within the bound.
No kernel may reach another device: no remote copies, remote signals or barrier semaphores. Data moves between devices by JAX's collectives and lax.ppermute only.
A program may use at most 192 MiB of HBM per device.

```python
import jax
import jax.numpy as jnp
from jax import lax

D = 768
HEADS = 12
HEAD_DIM = 64
FF = 3072
LAYERS = 2
LEN = 1024
DOCS = 8
SEQS = 8
TOKENS = 8192


def draw_segment_ids(key, part):

    def one_sequence(seq_key):
        order = jax.random.permutation(seq_key, LEN - 1) + 1
        cuts = jnp.sort(order[:DOCS])
        position = jnp.arange(LEN)
        labels = jnp.sum((position[:, None] >= cuts[None, :]).astype(jnp.int32), axis=1)
        return jnp.where(labels == DOCS, -1, labels).astype(jnp.int32)
    return jax.vmap(one_sequence)(jax.random.split(jax.random.fold_in(key, 11), SEQS))


def shard_levels(own_key, shape, pieces, least, high):
    def one(dim, shards_of):
        steps = jax.random.uniform(jax.random.fold_in(jax.random.fold_in(own_key, 6), dim), (shards_of,), jnp.float32, least / len(pieces), high / len(pieces))
        return jnp.repeat(jnp.exp(steps), shape[dim] // shards_of).reshape((-1,) + (1,) * (len(shape) - dim - 1))

    level = one(*pieces[0])
    for cut in pieces[1:]:
        level = level * one(*cut)
    return level


def gaussian(stream_key, dims, scale, bound, cuts=(), held_as=jnp.bfloat16):
    level = shard_levels(stream_key, dims, cuts, -0.22, 0.18) if cuts else 1.0
    entries = jax.random.normal(stream_key, dims, jnp.float32) * scale * level
    return jnp.minimum(jnp.maximum(entries, -bound), bound).astype(held_as)


def setup_inputs(seed: int = 0) -> dict:
    key_of = jax.random.split(jax.random.key(seed), 20)
    hidden_in = gaussian(key_of[0], (TOKENS, D), 1.0, 6.0, ((0, 32),))
    time_embed = gaussian(key_of[1], (SEQS, D), 1.0, 6.0, ((0, 8),))
    segment_ids = draw_segment_ids(jax.random.fold_in(key_of[19], 71), 0)
    cotangent = gaussian(key_of[3], (TOKENS, D), 1.0, 6.0, ((0, 32),))
    query_weight = gaussian(key_of[4], (LAYERS, D, D), D ** -0.5, 0.21875, ((1, 8), (2, 4)))
    key_weight = gaussian(key_of[5], (LAYERS, D, D), D ** -0.5, 0.21875, ((1, 8), (2, 4)))
    value_weight = gaussian(key_of[6], (LAYERS, D, D), D ** -0.5, 0.21875, ((1, 8), (2, 4)))
    output_weight = gaussian(key_of[7], (LAYERS, D, D), (D // 64) ** -0.5, 1.75, ((1, 4), (2, 8)))
    up_weight = gaussian(key_of[8], (LAYERS, D, FF), D ** -0.5, 0.21875, ((1, 8), (2, 4)))
    down_weight = gaussian(key_of[9], (LAYERS, FF, D), FF ** -0.5, 0.109375, ((1, 4), (2, 8)))
    query_bias = gaussian(key_of[10], (LAYERS, D), 0.5, 3.0, ((1, 4),), jnp.float32)
    value_bias = gaussian(key_of[11], (LAYERS, D), 0.5, 3.0, ((1, 4),), jnp.float32)
    output_bias = gaussian(key_of[12], (LAYERS, D), 0.5, 3.0, (), jnp.float32)
    up_bias = gaussian(key_of[13], (LAYERS, FF), 0.5, 3.0, ((1, 4),), jnp.float32)
    down_bias = gaussian(key_of[14], (LAYERS, D), 0.5, 3.0, (), jnp.float32)
    first_gain = jnp.clip(1.0 + 0.15 * jax.random.normal(key_of[15], (LAYERS, D), jnp.float32), 0.25, 1.75)
    first_shift = gaussian(key_of[16], (LAYERS, D), 0.5, 3.0, (), jnp.float32)
    second_gain = jnp.clip(1.0 + 0.15 * jax.random.normal(key_of[17], (LAYERS, D), jnp.float32), 0.25, 1.75)
    second_shift = gaussian(key_of[18], (LAYERS, D), 0.5, 3.0, (), jnp.float32)
    return dict(hidden_in=hidden_in, time_embed=time_embed, segment_ids=segment_ids, cotangent=cotangent, query_weight=query_weight, key_weight=key_weight, value_weight=value_weight, output_weight=output_weight, up_weight=up_weight, down_weight=down_weight, query_bias=query_bias, value_bias=value_bias, output_bias=output_bias, up_bias=up_bias, down_bias=down_bias, first_gain=first_gain, first_shift=first_shift, second_gain=second_gain, second_shift=second_shift)


@jax.custom_vjp
def low(v):
    return lax.optimization_barrier(v.astype(jnp.bfloat16)).astype(jnp.float32)

@jax.custom_vjp
def low_back(v):
    return v

def low_keep(v):
    return (low(v), None)

def low_pass(kept, grad):
    return (grad,)

def back_keep(v):
    return (v, None)

def back_low(kept, grad):
    return (low(grad),)
low.defvjp(low_keep, low_pass)
low_back.defvjp(back_keep, back_low)

def matmul(left, right):
    return jnp.dot(left, right, precision=lax.Precision.HIGHEST, preferred_element_type=jnp.float32)

def apply_layer_norm(token_rows, gain, shift):
    center = token_rows - lax.optimization_barrier(jnp.mean(token_rows, axis=-1, keepdims=True))
    return center * lax.rsqrt(lax.optimization_barrier(jnp.mean(center * center, axis=-1, keepdims=True)) + 1e-05) * gain + shift

def block(token_rows, same_doc, params):
    query_w, key_w, value_w, out_w, up_w, down_w, query_b, value_b, out_b, up_b, down_b, norm_gain_first, norm_offset_first, norm_gain_second, norm_offset_second = params
    length = token_rows.shape[0]
    first = low(apply_layer_norm(token_rows, norm_gain_first, norm_offset_first))
    query = low(low_back(matmul(first, query_w) + query_b)).reshape(length, HEADS, HEAD_DIM)
    key = low(low_back(matmul(first, key_w))).reshape(length, HEADS, HEAD_DIM)
    value = low(low_back(matmul(first, value_w) + value_b)).reshape(length, HEADS, HEAD_DIM)
    scores = jnp.einsum('qhd,khd->hqk', query, key, precision=lax.Precision.HIGHEST) * HEAD_DIM ** (-0.5)
    scores = low_back(scores)
    scores = jnp.where(same_doc[None], scores, -jnp.inf)
    probs = low(jax.nn.softmax(scores, axis=-1))
    mixed = jnp.einsum('hqk,khd->qhd', probs, value, precision=lax.Precision.HIGHEST).reshape(length, D)
    mixed = low(low_back(mixed))
    between_layers = token_rows + low_back(matmul(mixed, out_w)) + out_b
    second = low(apply_layer_norm(between_layers, norm_gain_second, norm_offset_second))
    act = low(jax.nn.gelu(low_back(matmul(second, up_w) + up_b), approximate=True))
    return between_layers + low_back(matmul(act, down_w)) + down_b

def forward(token_rows, embed, segments, params):

    def one_sequence(item):
        seq_rows, seq_embed, seq_ids = item
        same_doc = seq_ids[:, None] == seq_ids[None, :]
        state = seq_rows + seq_embed[None, :]
        for layer in range(LAYERS):
            state = block(state, same_doc, tuple((p[layer] for p in params)))
        return state
    return lax.map(jax.checkpoint(one_sequence), (token_rows, embed, segments))

def reference(hidden_in, time_embed, segment_ids, cotangent, query_weight, key_weight, value_weight, output_weight, up_weight, down_weight, query_bias, value_bias, output_bias, up_bias, down_bias, first_gain, first_shift, second_gain, second_shift):
    token_rows = hidden_in.astype(jnp.float32).reshape(SEQS, LEN, D)
    embed = time_embed.astype(jnp.float32)
    params = tuple((p.astype(jnp.float32) for p in (query_weight, key_weight, value_weight, output_weight, up_weight, down_weight, query_bias, value_bias, output_bias, up_bias, down_bias, first_gain, first_shift, second_gain, second_shift)))
    result, pull = jax.vjp(lambda r, p: forward(r, embed, segment_ids, p), token_rows, params)
    valid = (segment_ids >= 0).astype(jnp.float32)[:, :, None]
    start_grad = cotangent.astype(jnp.float32).reshape(SEQS, LEN, D) * valid
    grad_rows, grad_params = pull(start_grad)
    return (result.reshape(TOKENS, D).astype(jnp.bfloat16), grad_rows.reshape(TOKENS, D)) + tuple(grad_params)
```

```python
import functools

import jax
import jax.numpy as jnp
from jax import lax
from jax.experimental import pallas as pl
from jax.experimental.pallas import tpu as pltpu
from jax.sharding import PartitionSpec as P

HEAD_DIM = 64
EPSILON = 1e-05
LOW = jnp.bfloat16
WIDE = jnp.float32
ROOT = 0.7978845608028654
CUBE = 0.044715

SWAP_CORE = [(0, 1), (1, 0), (2, 3), (3, 2)]
SWAP_Y = [(0, 2), (2, 0), (1, 3), (3, 1)]


def swap_core(value):
    return lax.ppermute(value, "tensor", SWAP_CORE)


def swap_y(value):
    return lax.ppermute(value, "tensor", SWAP_Y)


def dot(a, b):
    return jnp.dot(a, b, preferred_element_type=WIDE)


def dot_nt(a, b):
    return lax.dot_general(a, b, (((1,), (1,)), ((), ())), preferred_element_type=WIDE)


def dot_tn(a, b):
    return lax.dot_general(a, b, (((0,), (0,)), ((), ())), preferred_element_type=WIDE)


def ring_order(count):
    return list(range(0, count, 2)) + list(range(count - 1, 0, -2))


def ring_pairs(count):
    order = ring_order(count)
    pairs = []
    for place, here in enumerate(order):
        for t in range(4):
            step = 1 if t % 2 == 0 else -1
            there = order[(place + step) % count]
            pairs.append((here * 4 + t, there * 4 + t))
    return pairs


def ring_step(value, count):
    return lax.ppermute(value, ("fsdp", "tensor"), ring_pairs(count))


class Ring:
    def __init__(self):
        self.count = lax.axis_size("fsdp")
        self.use = self.count == 8
        if self.use:
            order = ring_order(self.count)
            place = [0] * self.count
            for index, here in enumerate(order):
                place[here] = index
            self.order = jnp.array(order, jnp.int32)
            self.place = jnp.array(place, jnp.int32)[lax.axis_index("fsdp")]
            self.core = lax.axis_index("tensor") % 2
            self.way = 1 - 2 * self.core

    def block_at(self, steps):
        return self.order[(self.place + steps + 2 * self.count) % self.count]

    def gather(self, piece):
        count = self.count
        if not self.use:
            return lax.all_gather(piece, "fsdp", axis=0, tiled=True)
        rows, columns = piece.shape
        half = rows // 2
        whole = jnp.zeros((count * rows, columns), piece.dtype)

        def put(whole, value, block, offset=0):
            return lax.dynamic_update_slice(whole, value, (block * rows + offset, 0))

        whole = put(whole, piece, lax.axis_index("fsdp"))
        current = piece
        for step in range(1, count // 2):
            current = ring_step(current, count)
            whole = put(whole, current, self.block_at(-self.way * step))
            whole = put(whole, swap_core(current), self.block_at(self.way * step))
        last = lax.dynamic_slice(current, (self.core * half, 0), (half, columns))
        last = ring_step(last, count)
        block = self.block_at(count // 2)
        whole = put(whole, last, block, self.core * half)
        whole = put(whole, swap_core(last), block, (1 - self.core) * half)
        return whole

    def scatter(self, partial, own_columns, peer_columns):
        count = self.count
        if not self.use:
            mine = own_columns(partial).astype(WIDE) + swap_core(peer_columns(partial)).astype(WIDE)
            return lax.psum_scatter(mine, "fsdp", scatter_dimension=0, tiled=True)
        rows = partial.shape[0] // count
        columns = partial.shape[1]
        half = rows // 2

        def block(steps, offset=0, size=rows):
            return lax.dynamic_slice(
                partial, (self.block_at(steps) * rows + offset, 0), (size, columns)
            )

        far = count // 2
        give = [block(-self.way * step) for step in range(1, far)]
        give.append(block(far, (1 - self.core) * half, half))
        got = swap_core(jnp.concatenate(give))
        keep = [
            block(self.way * step).astype(WIDE) + got[(step - 1) * rows : step * rows].astype(WIDE)
            for step in range(1, far)
        ]
        last = block(far, self.core * half, half).astype(WIDE) + got[(far - 1) * rows :].astype(WIDE)
        moving = ring_step(last.astype(LOW), count).astype(WIDE)
        blank = jnp.zeros_like(moving)
        moving = jnp.where(
            self.core == 0, jnp.concatenate([moving, blank]), jnp.concatenate([blank, moving])
        )
        for step in range(far - 1, 0, -1):
            moving = ring_step((keep[step - 1] + moving).astype(LOW), count).astype(WIDE)
        total = moving + block(0).astype(WIDE)
        return own_columns(total) + swap_core(peer_columns(total).astype(LOW)).astype(WIDE)


def sum_everywhere(value):
    count = lax.axis_size("fsdp")
    if count & (count - 1):
        return lax.psum(value, ("fsdp", "tensor"))
    value = value + swap_core(value)
    value = value + swap_y(value)
    bit = 1
    while bit < count:
        value = value + lax.ppermute(value, "fsdp", [(i, i ^ bit) for i in range(count)])
        bit *= 2
    return value


SUB = 128


def pair_parts(heads):
    return [(pair, part) for pair in range(heads // 2) for part in range(2)]


def attention_forward_kernel(*refs, heads):
    segq, segk, q_ref = refs[:3]
    k_refs = refs[3:7]
    v_refs = refs[7:11]
    mixed_ref, norm_ref = refs[11:]
    scale = HEAD_DIM ** (-0.5)
    same = segq[...] == segk[...]
    lane = lax.broadcasted_iota(jnp.int32, (1, 128), 1)
    side = [lane < 64, lane >= 64]
    norms = jnp.zeros((SUB, 128), WIDE)
    for pair in range(heads // 2):
        columns = slice(pair * 128, pair * 128 + 128)
        q = q_ref[:, columns]
        total = jnp.zeros((SUB, 128), WIDE)
        for part in range(2):
            q_one = jnp.where(side[part], q, jnp.zeros_like(q))
            scores = jnp.concatenate([dot_nt(q_one, k[:, columns]) for k in k_refs], axis=1)
            scores = jnp.where(same, scores * scale, -jnp.inf)
            top = jnp.max(scores, axis=1, keepdims=True)
            grown = jnp.exp(scores - top)
            bulk = jnp.sum(grown, axis=1, keepdims=True)
            probs = (grown * (1.0 / bulk)).astype(LOW)
            for index, v in enumerate(v_refs):
                block = v[:, columns]
                v_one = jnp.where(side[part], block, jnp.zeros_like(block))
                width = block.shape[0]
                total += dot(probs[:, index * width : (index + 1) * width], v_one)
            norms = jnp.where(lane == pair * 2 + part, top + jnp.log(bulk), norms)
        mixed_ref[:, columns] = total.astype(LOW)
    norm_ref[...] = norms


def attention_forward(segq, segk, q, keys, values):
    rows, width = q.shape
    heads = width // HEAD_DIM
    full = [pl.BlockSpec(k.shape, lambda i: (0, 0)) for k in keys]
    flops = 4 * rows * 4 * rows * width
    return pl.pallas_call(
        functools.partial(attention_forward_kernel, heads=heads),
        grid=(rows // SUB,),
        in_specs=[
            pl.BlockSpec((SUB, 1), lambda i: (i, 0)),
            pl.BlockSpec(segk.shape, lambda i: (0, 0)),
            pl.BlockSpec((SUB, width), lambda i: (i, 0)),
            *full,
            *full,
        ],
        out_specs=[
            pl.BlockSpec((SUB, width), lambda i: (i, 0)),
            pl.BlockSpec((SUB, 128), lambda i: (i, 0)),
        ],
        out_shape=[
            jax.ShapeDtypeStruct((rows, width), LOW),
            jax.ShapeDtypeStruct((rows, 128), WIDE),
        ],
        compiler_params=pltpu.CompilerParams(vmem_limit_bytes=48 << 20),
        cost_estimate=pl.CostEstimate(
            flops=flops, bytes_accessed=10 * rows * width * 2, transcendentals=4 * rows * rows * heads
        ),
    )(segq, segk, q, *keys, *values)


def attention_backward_kernel(*refs, heads, first):
    segq, segk, q_ref, norm_ref, g_ref = refs[:5]
    k_refs = refs[5:9]
    v_refs = refs[9:13]
    if first:
        dq_ref, dk_ref, dv_ref = refs[13:]
    else:
        dk_in, dv_in, dq_ref, dk_ref, dv_ref = refs[13:]
    scale = HEAD_DIM ** (-0.5)

    @pl.when(pl.program_id(0) == 0)
    def _():
        if first:
            dk_ref[...] = jnp.zeros_like(dk_ref)
            dv_ref[...] = jnp.zeros_like(dv_ref)
        else:
            dk_ref[...] = dk_in[...]
            dv_ref[...] = dv_in[...]

    same = segq[...] == segk[...]
    lane = lax.broadcasted_iota(jnp.int32, (1, 128), 1)
    side = [lane < 64, lane >= 64]
    norms = norm_ref[...]
    width = k_refs[0].shape[0]
    for pair in range(heads // 2):
        columns = slice(pair * 128, pair * 128 + 128)
        q = q_ref[:, columns]
        g = g_ref[:, columns]
        dq = jnp.zeros((SUB, 128), WIDE)
        for part in range(2):
            q_one = jnp.where(side[part], q, jnp.zeros_like(q))
            g_one = jnp.where(side[part], g, jnp.zeros_like(g))
            norm = jnp.sum(jnp.where(lane == pair * 2 + part, norms, 0.0), axis=1, keepdims=True)
            scores = jnp.concatenate([dot_nt(q_one, k[:, columns]) for k in k_refs], axis=1)
            probs = jnp.where(same, jnp.exp(scores * scale - norm), 0.0)
            g_probs = jnp.concatenate([dot_nt(g_one, v[:, columns]) for v in v_refs], axis=1)
            row_total = jnp.sum(probs * g_probs, axis=1, keepdims=True)
            g_scores = (probs * (g_probs - row_total)).astype(LOW)
            probs_low = probs.astype(LOW)
            dk_ref[:, columns] += dot_tn(g_scores, q_one)
            dv_ref[:, columns] += dot_tn(probs_low, g_one)
            for index, k in enumerate(k_refs):
                block = k[:, columns]
                k_one = jnp.where(side[part], block, jnp.zeros_like(block))
                dq += dot(g_scores[:, index * width : (index + 1) * width], k_one)
        dq_ref[:, columns] = (dq * scale).astype(LOW)


def attention_backward(segq, segk, q, norms, g, keys, values, sums):
    rows, width = q.shape
    heads = width // HEAD_DIM
    full = [pl.BlockSpec(k.shape, lambda i: (0, 0)) for k in keys]
    length = 4 * keys[0].shape[0]
    whole = pl.BlockSpec((length, width), lambda i: (0, 0))
    first = sums is None
    extra = () if first else tuple(sums)
    return pl.pallas_call(
        functools.partial(attention_backward_kernel, heads=heads, first=first),
        grid=(rows // SUB,),
        in_specs=[
            pl.BlockSpec((SUB, 1), lambda i: (i, 0)),
            pl.BlockSpec(segk.shape, lambda i: (0, 0)),
            pl.BlockSpec((SUB, width), lambda i: (i, 0)),
            pl.BlockSpec((SUB, 128), lambda i: (i, 0)),
            pl.BlockSpec((SUB, width), lambda i: (i, 0)),
            *full,
            *full,
            *([whole] * len(extra)),
        ],
        out_specs=[pl.BlockSpec((SUB, width), lambda i: (i, 0)), whole, whole],
        out_shape=[
            jax.ShapeDtypeStruct((rows, width), LOW),
            jax.ShapeDtypeStruct((length, width), WIDE),
            jax.ShapeDtypeStruct((length, width), WIDE),
        ],
        compiler_params=pltpu.CompilerParams(vmem_limit_bytes=48 << 20),
        cost_estimate=pl.CostEstimate(
            flops=10 * rows * length * width,
            bytes_accessed=10 * rows * width * 2,
            transcendentals=rows * length * heads,
        ),
    )(segq, segk, q, norms, g, *keys, *values, *extra)


def norm_forward(rows, gain, shift):
    center = rows - jnp.mean(rows, axis=1, keepdims=True)
    factor = lax.rsqrt(jnp.mean(center * center, axis=1, keepdims=True) + EPSILON)
    return (center * factor * gain + shift).astype(LOW), factor


def norm_backward(grad, rows, factor, gain):
    normed = (rows - jnp.mean(rows, axis=1, keepdims=True)) * factor
    scaled = grad * gain
    through = factor * (
        scaled
        - jnp.mean(scaled, axis=1, keepdims=True)
        - normed * jnp.mean(scaled * normed, axis=1, keepdims=True)
    )
    return jnp.sum(grad * normed, axis=0), jnp.sum(grad, axis=0), through


def gelu_both(pre):
    inner = jnp.tanh(ROOT * (pre + CUBE * pre * pre * pre))
    slope = 0.5 * (1.0 + inner) + 0.5 * pre * (1.0 - inner * inner) * (
        ROOT * (1.0 + 3.0 * CUBE * pre * pre)
    )
    return (0.5 * pre * (1.0 + inner)).astype(LOW), slope.astype(LOW)


def local(
    hidden_in,
    time_embed,
    segment_ids,
    cotangent,
    query_weight,
    key_weight,
    value_weight,
    output_weight,
    up_weight,
    down_weight,
    query_bias,
    value_bias,
    output_bias,
    up_bias,
    down_bias,
    first_gain,
    first_shift,
    second_gain,
    second_shift,
):
    rows = hidden_in.shape[0]
    layers, _, head_width = query_weight.shape
    hidden_width = up_weight.shape[2]
    place = lax.axis_index("tensor")
    core = place % 2
    side = place // 2
    ring = Ring()

    def low_high(own):
        peer = swap_core(own)
        return jnp.where(core == 0, own, peer), jnp.where(core == 0, peer, own)

    def join(low, high, widths):
        parts, start = [], 0
        for width in widths:
            parts += [low[:, start : start + width], high[:, start : start + width]]
            start += width
        return jnp.concatenate(parts, axis=1)

    widths_a = (head_width,) * 3
    widths_b = (head_width, hidden_width, hidden_width)
    pieces_a, pieces_b = [], []
    packed = [
        jnp.concatenate(
            [
                query_weight[layer],
                key_weight[layer],
                value_weight[layer],
                output_weight[layer].T,
                up_weight[layer],
                down_weight[layer].T,
            ],
            axis=1,
        )
        for layer in range(layers)
    ]
    cut = 3 * head_width
    for layer in range(layers):
        low, high = low_high(packed[layer])
        pieces_a.append(join(low[:, :cut], high[:, :cut], widths_a))
        pieces_b.append(join(low[:, cut:], high[:, cut:], widths_b))

    bias_low, bias_high = low_high(jnp.concatenate([query_bias, value_bias, up_bias], axis=1))
    q_bias = jnp.concatenate([bias_low[:, :head_width], bias_high[:, :head_width]], axis=1)
    v_bias = jnp.concatenate(
        [bias_low[:, head_width : 2 * head_width], bias_high[:, head_width : 2 * head_width]], axis=1
    )
    u_bias = jnp.concatenate([bias_low[:, 2 * head_width :], bias_high[:, 2 * head_width :]], axis=1)

    def both_sides(own):
        other = swap_y(own)
        return [jnp.where(side == 0, own, other), jnp.where(side == 0, other, own)]

    def own_of(pair):
        return jnp.where(side == 0, pair[0], pair[1])

    def other_of(pair):
        return jnp.where(side == 0, pair[1], pair[0])

    segments = segment_ids[0]

    def ids_at(block):
        return lax.dynamic_slice_in_dim(segments, block * rows, rows)

    ids = [ids_at(core), ids_at(2 + core), ids_at(1 - core), ids_at(3 - core)]
    segk = jnp.concatenate(ids)[None, :]
    segq = [ids[0][:, None], ids[1][:, None]]
    own_ids = ids_at(place)
    embed = time_embed.astype(WIDE)

    state = [part.astype(WIDE) + embed for part in both_sides(hidden_in)]
    weights_a = [None] * layers
    weights_b = [None] * layers
    weights_a[0] = ring.gather(pieces_a[0])

    valid = (own_ids >= 0)[:, None]
    seed = jnp.where(valid, cotangent, jnp.zeros_like(cotangent))

    width = 2 * head_width
    hidden = 2 * hidden_width
    kept = []
    denoised = None
    for layer in range(layers):
        w_qkv = weights_a[layer]
        firsts, f_factors, queries, keys, values = [], [], [], [], []
        for j in range(2):
            first, factor = norm_forward(state[j], first_gain[layer], first_shift[layer])
            qkv = dot(first, w_qkv)
            firsts.append(first)
            f_factors.append(factor)
            queries.append((qkv[:, :width] + q_bias[layer]).astype(LOW))
            keys.append(qkv[:, width : 2 * width].astype(LOW))
            values.append((qkv[:, 2 * width :] + v_bias[layer]).astype(LOW))
        if layer == 0:
            weights_b[0] = ring.gather(pieces_b[0])
            weights_a[1] = ring.gather(pieces_a[1])
            weights_b[1] = ring.gather(pieces_b[1])
            seeds = both_sides(seed)
        w_out = weights_b[layer][:, :width]
        w_up = weights_b[layer][:, width : width + hidden]
        w_down = weights_b[layer][:, width + hidden :]
        far = swap_core((keys, values))
        keys = keys + list(far[0])
        values = values + list(far[1])
        mixeds, norms, parts = [], [], []
        for j in range(2):
            mixed, norm = attention_forward(segq[j], segk, queries[j], keys, values)
            mixeds.append(mixed)
            norms.append(norm)
            parts.append(dot_nt(mixed, w_out))
        arrived = [swap_y(part.astype(LOW)) for part in parts]
        middles, seconds, s_factors, acts, slopes, branches = [], [], [], [], [], []
        for j in range(2):
            middle = state[j] + (parts[j] + arrived[j].astype(WIDE)) + output_bias[layer]
            second, factor = norm_forward(middle, second_gain[layer], second_shift[layer])
            act, slope = gelu_both(dot(second, w_up) + u_bias[layer])
            middles.append(middle)
            seconds.append(second)
            s_factors.append(factor)
            acts.append(act)
            slopes.append(slope)
            branches.append(dot_nt(act, w_down))
        if layer < layers - 1:
            arrived = [swap_y(part.astype(LOW)) for part in branches]
            following = [
                middles[j] + (branches[j] + arrived[j].astype(WIDE)) + down_bias[layer]
                for j in range(2)
            ]
        else:
            arrived = swap_y(other_of(branches).astype(LOW))
            denoised = (
                own_of(middles) + own_of(branches) + arrived.astype(WIDE) + down_bias[layer]
            ).astype(LOW)
            following = None
        kept.append(
            (state, firsts, f_factors, queries, keys, values, norms, mixeds, middles, seconds, s_factors, acts, slopes)
        )
        state = following

    grads = [part.astype(WIDE) for part in seeds]
    lows = seeds
    matrix_out = [None] * layers
    vector_rows = []
    input_grad = None

    def wide_at(vector, count):
        spread = jnp.zeros((2 * vector.shape[0],), WIDE)
        return lax.dynamic_update_slice_in_dim(spread, vector, side * vector.shape[0], 0)

    for layer in reversed(range(layers)):
        (state, firsts, f_factors, queries, keys, values, norms, mixeds, middles, seconds, s_factors, acts, slopes) = kept[layer]
        w_qkv = weights_a[layer]
        w_out = weights_b[layer][:, :width]
        w_up = weights_b[layer][:, width : width + hidden]
        w_down = weights_b[layer][:, width + hidden :]
        down_b_grad = jnp.sum(own_of(grads), axis=0)
        g_pres, parts = [], []
        for j in range(2):
            g_pre = (dot(lows[j], w_down) * slopes[j].astype(WIDE)).astype(LOW)
            g_pres.append(g_pre)
            parts.append(dot_nt(g_pre, w_up))
        arrived = [swap_y(part.astype(LOW)) for part in parts]
        rows_of = jnp.concatenate
        d_down = dot_tn(rows_of(lows), rows_of(acts)).astype(LOW)
        d_up = dot_tn(rows_of(seconds), rows_of(g_pres)).astype(LOW)
        up_b_grad = jnp.sum(rows_of(g_pres).astype(WIDE), axis=0)
        g_middles, m_lows, gains, shifts = [], [], [], []
        for j in range(2):
            g_second = parts[j] + arrived[j].astype(WIDE)
            gain, shift, through = norm_backward(
                g_second, middles[j], s_factors[j], second_gain[layer]
            )
            g_middle = grads[j] + through
            g_middles.append(g_middle)
            m_lows.append(g_middle.astype(LOW))
            gains.append(gain)
            shifts.append(shift)
        gain_two, shift_two = own_of(gains), own_of(shifts)
        out_b_grad = jnp.sum(own_of(g_middles), axis=0)
        sums = None
        g_queries = []
        for j in range(2):
            g_mixed = dot(m_lows[j], w_out).astype(LOW)
            g_query, *sums = attention_backward(
                segq[j], segk, queries[j], norms[j], g_mixed, keys, values, sums
            )
            g_queries.append(g_query)
        d_out = dot_tn(rows_of(m_lows), rows_of(mixeds)).astype(LOW)
        near = 2 * rows
        scale = HEAD_DIM ** (-0.5)
        away = swap_core([total[near:].astype(LOW) for total in sums])
        g_key = ((sums[0][:near] + away[0].astype(WIDE)) * scale).astype(LOW)
        g_value = (sums[1][:near] + away[1].astype(WIDE)).astype(LOW)
        g_query = rows_of(g_queries)
        g_qkv = jnp.concatenate([g_query, g_key, g_value], axis=1)
        parts = [dot_nt(g_qkv[:rows], w_qkv), dot_nt(g_qkv[rows:], w_qkv)]
        d_qkv = dot_tn(rows_of(firsts), g_qkv).astype(LOW)
        q_b_grad = jnp.sum(g_query.astype(WIDE), axis=0)
        v_b_grad = jnp.sum(g_value.astype(WIDE), axis=0)
        if layer > 0:
            arrived = [swap_y(part.astype(LOW)) for part in parts]
            gains, shifts, grads, lows = [], [], [], []
            for j in range(2):
                g_first = parts[j] + arrived[j].astype(WIDE)
                gain, shift, through = norm_backward(
                    g_first, state[j], f_factors[j], first_gain[layer]
                )
                grad = g_middles[j] + through
                grads.append(grad)
                lows.append(grad.astype(LOW))
                gains.append(gain)
                shifts.append(shift)
            gain_one, shift_one = own_of(gains), own_of(shifts)
        else:
            arrived = swap_y(other_of(parts).astype(LOW))
            g_first = own_of(parts) + arrived.astype(WIDE)
            gain_one, shift_one, through = norm_backward(
                g_first, own_of(state), own_of(f_factors), first_gain[layer]
            )
            input_grad = own_of(g_middles) + through

        def columns_of(widths, which):
            def pick(array):
                low, high, start = [], [], 0
                for w in widths:
                    low.append(array[:, start : start + w])
                    high.append(array[:, start + w : start + 2 * w])
                    start += 2 * w
                low, high = jnp.concatenate(low, axis=1), jnp.concatenate(high, axis=1)
                return jnp.where(core == which, low, high)

            return pick

        groups = [
            ((hidden_width, hidden_width), jnp.concatenate([d_up, d_down], axis=1)),
            ((head_width,) * 4, jnp.concatenate([d_qkv, d_out], axis=1)),
        ]
        done = [
            ring.scatter(array, columns_of(widths, 0), columns_of(widths, 1))
            for widths, array in groups
        ]
        heads_of = lambda i: done[1][:, i * head_width : (i + 1) * head_width]
        matrix_out[layer] = (
            heads_of(0),
            heads_of(1),
            heads_of(2),
            heads_of(3).T,
            done[0][:, :hidden_width],
            done[0][:, hidden_width:].T,
        )
        vector_rows = [
            jnp.concatenate(
                [
                    jnp.stack(
                        [
                            gain_one,
                            shift_one,
                            gain_two,
                            shift_two,
                            out_b_grad,
                            down_b_grad,
                            wide_at(q_b_grad, 0),
                            wide_at(v_b_grad, 0),
                        ]
                    ).reshape(-1),
                    wide_at(up_b_grad, 0),
                ]
            )
        ] + vector_rows
    depth = hidden_in.shape[1]
    total = sum_everywhere(jnp.stack(vector_rows).reshape(-1, 128)).reshape(layers, -1)
    vectors = total[:, : 8 * depth].reshape(layers, 8, depth)
    ups = total[:, 8 * depth :]
    stacked = [jnp.stack([matrix_out[layer][index] for layer in range(layers)]) for index in range(6)]

    def mine(array, size):
        return lax.dynamic_slice_in_dim(array, place * size, size, 1)

    return (
        denoised,
        input_grad,
        *stacked,
        mine(vectors[:, 6], head_width),
        mine(vectors[:, 7], head_width),
        vectors[:, 4],
        mine(ups, hidden_width),
        vectors[:, 5],
        vectors[:, 0],
        vectors[:, 1],
        vectors[:, 2],
        vectors[:, 3],
    )


def solution(mesh):
    rows = P(("fsdp", "tensor"), None)
    inner = P(None, "fsdp", "tensor")
    outer = P(None, "tensor", "fsdp")
    cut = P(None, "tensor")
    in_specs = (
        rows,
        P("fsdp", None),
        P("fsdp", None),
        rows,
        inner,
        inner,
        inner,
        outer,
        inner,
        outer,
        cut,
        cut,
        P(),
        cut,
        P(),
        P(),
        P(),
        P(),
        P(),
    )
    out_specs = (
        rows,
        rows,
        inner,
        inner,
        inner,
        outer,
        inner,
        outer,
        cut,
        cut,
        P(),
        cut,
        P(),
        P(),
        P(),
        P(),
        P(),
    )
    return jax.shard_map(local, mesh=mesh, in_specs=in_specs, out_specs=out_specs, check_vma=False)
```

```python
import functools

import jax
import jax.numpy as jnp
from jax import lax
from jax.experimental import pallas as pl
from jax.experimental.pallas import tpu as pltpu
from jax.sharding import PartitionSpec as P

HEAD_DIM = 64
EPSILON = 1e-05
LOW = jnp.bfloat16
WIDE = jnp.float32
ROOT = 0.7978845608028654
CUBE = 0.044715

SWAP_CORE = [(0, 1), (1, 0), (2, 3), (3, 2)]
SWAP_Y = [(0, 2), (2, 0), (1, 3), (3, 1)]


def swap_core(value):
    return lax.ppermute(value, "tensor", SWAP_CORE)


def swap_y(value):
    return lax.ppermute(value, "tensor", SWAP_Y)


def dot(a, b):
    return jnp.dot(a, b, preferred_element_type=WIDE)


def dot_nt(a, b):
    return lax.dot_general(a, b, (((1,), (1,)), ((), ())), preferred_element_type=WIDE)


def dot_tn(a, b):
    return lax.dot_general(a, b, (((0,), (0,)), ((), ())), preferred_element_type=WIDE)


def tie(*values):
    return lax.optimization_barrier(values)


def ring_order(count):
    return list(range(0, count, 2)) + list(range(count - 1, 0, -2))


def ring_pairs(count):
    order = ring_order(count)
    pairs = []
    for place, here in enumerate(order):
        for t in range(4):
            step = 1 if t % 2 == 0 else -1
            there = order[(place + step) % count]
            pairs.append((here * 4 + t, there * 4 + t))
    return pairs


class Ring:
    def __init__(self):
        self.count = lax.axis_size("fsdp")
        self.use = self.count == 8
        self.core = lax.axis_index("tensor") % 2
        if self.use:
            order = ring_order(self.count)
            place = [0] * self.count
            for index, here in enumerate(order):
                place[here] = index
            self.order = jnp.array(order, jnp.int32)
            self.place = jnp.array(place, jnp.int32)[lax.axis_index("fsdp")]
            self.way = 1 - 2 * self.core
            self.far = self.count // 2
            self.blocks = {}

    def send(self, value):
        return lax.ppermute(value, ("fsdp", "tensor"), ring_pairs(self.count))

    def block_at(self, steps):
        return self.order[(self.place + steps + 2 * self.count) % self.count]


class Gather:
    def __init__(self, ring, piece):
        self.ring = ring
        self.piece = piece
        self.rows, self.columns = piece.shape
        self.todo = []
        self.done = 0
        if ring.use:
            self.whole = jnp.zeros((ring.count * self.rows, self.columns), piece.dtype)
            self.put(piece, lax.axis_index("fsdp"))
            self.current = piece
        else:
            self.whole = lax.all_gather(piece, "fsdp", axis=0, tiled=True)

    def put(self, value, block, offset=0):
        start = block * self.rows + offset
        self.whole = lax.dynamic_update_slice(self.whole, value, (start, 0))

    def flush(self):
        ring = self.ring
        half = self.rows // 2
        for step, value in self.todo:
            if step < ring.far:
                self.put(value, ring.block_at(-ring.way * step))
                self.put(swap_core(value), ring.block_at(ring.way * step))
            else:
                block = ring.block_at(step)
                self.put(value, block, ring.core * half)
                self.put(swap_core(value), block, (1 - ring.core) * half)
        self.todo = []

    def slot(self, main):
        ring = self.ring
        if not ring.use or self.done == ring.far:
            return main
        self.flush()
        self.done += 1
        current = self.current
        if self.done == ring.far:
            half = self.rows // 2
            current = lax.dynamic_slice(current, (ring.core * half, 0), (half, self.columns))
        moved = ring.send(current)
        if main is None:
            self.current = moved
        else:
            main, self.current, self.whole = tie(main, moved, self.whole)
        self.todo.append((self.done, self.current))
        return main

    def finish(self, main=None):
        if self.ring.use:
            while self.done < self.ring.far:
                main = self.slot(main)
            self.flush()
        return main


class Scatter:
    def __init__(self, ring, partial, own, peer):
        self.ring = ring
        self.partial = partial
        self.own = own
        self.peer = peer
        self.steps = 0
        if not ring.use:
            mine = own(partial).astype(WIDE) + swap_core(peer(partial)).astype(WIDE)
            self.result = lax.psum_scatter(mine, "fsdp", scatter_dimension=0, tiled=True)
            return
        self.rows = partial.shape[0] // ring.count
        self.half = self.rows // 2

    def block(self, steps, offset=0, size=None):
        size = self.rows if size is None else size
        return lax.dynamic_slice(
            self.partial,
            (self.ring.block_at(steps) * self.rows + offset, 0),
            (size, self.partial.shape[1]),
        )

    def slot(self, main):
        ring = self.ring
        if not ring.use or self.steps > ring.far + 1:
            return main
        far, half, rows = ring.far, self.half, self.rows
        if self.steps == 0:
            give = [self.block(-ring.way * step) for step in range(1, far)]
            give.append(self.block(far, (1 - ring.core) * half, half))
            moved = swap_core(jnp.concatenate(give))
        elif self.steps == 1:
            got = self.got
            last = self.block(far, ring.core * half, half).astype(WIDE)
            moved = ring.send((last + got[(far - 1) * rows :].astype(WIDE)).astype(LOW))
        elif self.steps <= far:
            step = far + 1 - self.steps
            here = self.block(ring.way * step).astype(WIDE)
            here += self.got[(step - 1) * rows : step * rows].astype(WIDE)
            moved = ring.send((here + self.padded()).astype(LOW))
        else:
            self.total = self.padded() + self.block(0).astype(WIDE)
            moved = swap_core(self.peer(self.total).astype(LOW))
        if main is None:
            (moved,) = tie(moved)
        else:
            main, moved = tie(main, moved)
        if self.steps == 0:
            self.got = moved
        else:
            self.moving = moved
        self.steps += 1
        if self.steps == far + 2:
            self.result = self.own(self.total) + self.moving.astype(WIDE)
        return main

    def padded(self):
        moving = self.moving.astype(WIDE)
        if moving.shape[0] == self.rows:
            return moving
        blank = jnp.zeros_like(moving)
        return jnp.where(
            self.ring.core == 0,
            jnp.concatenate([moving, blank]),
            jnp.concatenate([blank, moving]),
        )

    def finish(self, main=None):
        if self.ring.use:
            while self.steps < self.ring.far + 2:
                main = self.slot(main)
        return self.result


def sum_everywhere(value):
    count = lax.axis_size("fsdp")
    if count & (count - 1):
        return lax.psum(value, ("fsdp", "tensor"))
    value = value + swap_core(value)
    value = value + swap_y(value)
    bit = 1
    while bit < count:
        value = value + lax.ppermute(value, "fsdp", [(i, i ^ bit) for i in range(count)])
        bit *= 2
    return value


ROOM = 16 << 20
NEVER = -1e30


def out(shape, dtype=LOW):
    return jax.ShapeDtypeStruct(shape, dtype)


def head_lanes(half):
    lane = lax.broadcasted_iota(jnp.int32, (1, 128), 1)
    return (lane >= half * HEAD_DIM) & (lane < (half + 1) * HEAD_DIM)


def only(mask, value):
    return jnp.where(mask, value, jnp.zeros_like(value))


def kernel_call(kernel, operands, outs, scratch, flops, exps):
    inside = pl.BlockSpec(memory_space=pltpu.VMEM)
    moved = sum(x.size * x.dtype.itemsize for x in (*operands, *outs))
    return pl.pallas_call(
        kernel,
        in_specs=[inside] * len(operands),
        out_specs=[inside] * len(outs),
        out_shape=outs,
        scratch_shapes=scratch,
        compiler_params=pltpu.CompilerParams(vmem_limit_bytes=ROOM),
        cost_estimate=pl.CostEstimate(flops=flops, bytes_accessed=moved, transcendentals=exps),
    )(*operands)


def fold(value, reduce):
    return reduce(value.reshape(value.shape[0] // 8, 8, value.shape[1]), axis=0)


def attend(query, q_marks, pairs, k_marks):
    rows, width = query.shape
    heads = width // HEAD_DIM
    blocks = len(pairs)
    size = pairs[0].shape[0]

    def kernel(q_ref, qm_ref, *refs):
        kv_refs, km_refs = refs[:blocks], refs[blocks : 2 * blocks]
        mixed_ref, norm_ref, held = refs[2 * blocks :]
        parts = []
        for pair in range(heads // 2):
            at = slice(pair * 128, pair * 128 + 128)
            to = slice(width + pair * 128, width + pair * 128 + 128)
            q = q_ref[:, at]
            turned = [kv[:, to].astype(WIDE).T.astype(LOW) for kv in kv_refs]
            for half in range(2):
                q_one = jnp.concatenate([only(head_lanes(half), q), qm_ref[...]], axis=1)
                top = None
                for b in range(blocks):
                    key = jnp.concatenate([kv_refs[b][:, at], km_refs[b][...]], axis=1)
                    scores = dot_nt(key, q_one)
                    held[b] = scores
                    here = fold(scores, jnp.max)
                    top = here if top is None else jnp.maximum(top, here)
                top = jnp.max(top, axis=0, keepdims=True)
                total, bulk = None, None
                for b in range(blocks):
                    grown = jnp.exp(held[b] - top)
                    here = fold(grown, jnp.sum)
                    bulk = here if bulk is None else bulk + here
                    value = turned[b][half * HEAD_DIM : (half + 1) * HEAD_DIM]
                    part = dot(value, grown.astype(LOW))
                    total = part if total is None else total + part
                bulk = jnp.sum(bulk, axis=0, keepdims=True)
                parts.append(total * (1.0 / bulk))
                row = pair * 2 + half
                norm_ref[row : row + 1, :] = top + jnp.log(bulk)
        mixed_ref[...] = jnp.concatenate(parts).T.astype(LOW)

    return kernel_call(
        kernel,
        (query, q_marks, *pairs, *k_marks),
        [out((rows, width)), out((8, rows), WIDE)],
        [pltpu.VMEM((blocks, size, rows), WIDE)],
        4 * rows * blocks * size * width,
        rows * blocks * size * heads,
    )


def attend_back(query, q_marks, norms, g_mixed, pairs, k_marks):
    rows, width = query.shape
    heads = width // HEAD_DIM
    blocks = len(pairs)
    size = pairs[0].shape[0]
    scale = HEAD_DIM ** (-0.5)
    near = blocks // 2

    def kernel(q_ref, qm_ref, norm_ref, g_ref, *refs):
        kv_refs, km_refs = refs[:blocks], refs[blocks : 2 * blocks]
        dq_ref, own_ref, away_ref, p_wide, w_wide, p_all, s_all = refs[2 * blocks :]
        dqs = []
        for pair in range(heads // 2):
            at = slice(pair * 128, pair * 128 + 128)
            to = slice(width + pair * 128, width + pair * 128 + 128)
            q, g = q_ref[:, at], g_ref[:, at]
            turned = [kv[:, at].astype(WIDE).T.astype(LOW) for kv in kv_refs]
            q_stack, g_stack = [], []
            for half in range(2):
                lanes = head_lanes(half)
                q_stack.append(only(lanes, q))
                g_stack.append(only(lanes, g))
                q_one = jnp.concatenate([q_stack[half], qm_ref[...]], axis=1)
                row = pair * 2 + half
                norm = norm_ref[row : row + 1, :]
                total = None
                for b in range(blocks):
                    key = jnp.concatenate([kv_refs[b][:, at], km_refs[b][...]], axis=1)
                    probs = jnp.exp(dot_nt(key, q_one) - norm)
                    weighed = probs * dot_nt(kv_refs[b][:, to], g_stack[half])
                    here = fold(weighed, jnp.sum)
                    total = here if total is None else total + here
                    p_wide[b] = probs
                    w_wide[b] = weighed
                    p_all[b * size : (b + 1) * size, half * rows : (half + 1) * rows] = probs.astype(LOW)
                total = jnp.sum(total, axis=0, keepdims=True)
                dq = None
                for b in range(blocks):
                    g_scores = (w_wide[b] - p_wide[b] * total).astype(LOW)
                    s_all[b * size : (b + 1) * size, half * rows : (half + 1) * rows] = g_scores
                    part = dot(turned[b][half * HEAD_DIM : (half + 1) * HEAD_DIM], g_scores)
                    dq = part if dq is None else dq + part
                dqs.append(dq)
            dk = dot(s_all[...], jnp.concatenate(q_stack)).astype(LOW)
            dv = dot(p_all[...], jnp.concatenate(g_stack)).astype(LOW)
            own_ref[:, at] = dk[: near * size]
            away_ref[:, at] = dk[near * size :]
            own_ref[:, to] = dv[: near * size]
            away_ref[:, to] = dv[near * size :]
        dq_ref[...] = (jnp.concatenate(dqs).T * scale).astype(LOW)

    half_rows = near * size
    length = blocks * size
    return kernel_call(
        kernel,
        (query, q_marks, norms, g_mixed, *pairs, *k_marks),
        [out((rows, width)), out((half_rows, 2 * width)), out((half_rows, 2 * width))],
        [
            pltpu.VMEM((blocks, size, rows), WIDE),
            pltpu.VMEM((blocks, size, rows), WIDE),
            pltpu.VMEM((length, 2 * rows), LOW),
            pltpu.VMEM((length, 2 * rows), LOW),
        ],
        10 * rows * length * width,
        rows * length * heads,
    )


def weave(core, owns, peers, layer, turned):
    count = len(owns)
    straight = count - turned
    widths = [x.shape[2] for x in owns[:straight]] + [x.shape[1] for x in owns[straight:]]
    rows = owns[0].shape[1] if straight else owns[0].shape[2]

    def kernel(core_ref, *refs):
        first = core_ref[0] == 0
        own_refs, peer_refs, out_ref = refs[:count], refs[count : 2 * count], refs[2 * count]
        parts = []
        for index in range(count):
            own, peer = own_refs[index][0], peer_refs[index][0]
            low, high = jnp.where(first, own, peer), jnp.where(first, peer, own)
            if index >= straight:
                low, high = low.astype(WIDE).T.astype(LOW), high.astype(WIDE).T.astype(LOW)
            parts += [low, high]
        out_ref[...] = jnp.concatenate(parts, axis=1)

    operands = (*owns, *peers)
    return pl.pallas_call(
        kernel,
        grid=(1,),
        in_specs=[pl.BlockSpec(memory_space=pltpu.SMEM)]
        + [pl.BlockSpec((1, *x.shape[1:]), lambda i: (layer, 0, 0)) for x in operands],
        out_specs=pl.BlockSpec((rows, 2 * sum(widths)), lambda i: (0, 0)),
        out_shape=out((rows, 2 * sum(widths))),
        compiler_params=pltpu.CompilerParams(vmem_limit_bytes=ROOM),
        cost_estimate=pl.CostEstimate(
            flops=0, bytes_accessed=8 * rows * sum(widths), transcendentals=0
        ),
    )(core, *operands)


def norm_parts(rows):
    center = rows - jnp.mean(rows, axis=1, keepdims=True)
    factor = lax.rsqrt(jnp.mean(center * center, axis=1, keepdims=True) + EPSILON)
    return center * factor, factor


def norm_forward(rows, gain, shift):
    return (norm_parts(rows)[0] * gain + shift).astype(LOW)


def norm_backward(grad, rows, gain):
    normed, factor = norm_parts(rows)
    scaled = grad * gain
    through = factor * (
        scaled
        - jnp.mean(scaled, axis=1, keepdims=True)
        - normed * jnp.mean(scaled * normed, axis=1, keepdims=True)
    )
    return jnp.sum(grad * normed, axis=0), jnp.sum(grad, axis=0), through


def gelu_both(pre):
    inner = jnp.tanh(ROOT * (pre + CUBE * pre * pre * pre))
    slope = 0.5 * (1.0 + inner) + 0.5 * pre * (1.0 - inner * inner) * (
        ROOT * (1.0 + 3.0 * CUBE * pre * pre)
    )
    return (0.5 * pre * (1.0 + inner)).astype(LOW), slope.astype(LOW)


def local(
    hidden_in,
    time_embed,
    segment_ids,
    cotangent,
    query_weight,
    key_weight,
    value_weight,
    output_weight,
    up_weight,
    down_weight,
    query_bias,
    value_bias,
    output_bias,
    up_bias,
    down_bias,
    first_gain,
    first_shift,
    second_gain,
    second_shift,
):
    rows, depth = hidden_in.shape
    layers, _, head_width = query_weight.shape
    hidden_width = up_weight.shape[2]
    width = 2 * head_width
    hidden = 2 * hidden_width
    place = lax.axis_index("tensor")
    core = place % 2
    side = place // 2
    core_word = core.reshape(1)
    ring = Ring()
    scale = HEAD_DIM ** (-0.5)

    def both_sides(own):
        other = swap_y(own)
        return [jnp.where(side == 0, own, other), jnp.where(side == 0, other, own)]

    def own_of(pair):
        return jnp.where(side == 0, pair[0], pair[1])

    def other_of(pair):
        return jnp.where(side == 0, pair[1], pair[0])

    def rows_of(pair):
        return jnp.concatenate(pair)

    near_own = [query_weight, key_weight, value_weight, output_weight]
    near_peer = [swap_core(w) for w in near_own]
    hidden_pair = both_sides(hidden_in)
    near = [Gather(ring, weave(core_word, near_own, near_peer, 0, 1))]
    near[0].slot(None)

    def after(token, *values):
        return tie(token, *values)[1:] if ring.use else values

    def moving(gather):
        return gather.current if ring.use else None

    (query_bias, value_bias, up_bias, up_weight, down_weight, segment_ids, cotangent, time_embed) = after(
        moving(near[0]),
        query_bias,
        value_bias,
        up_bias,
        up_weight,
        down_weight,
        segment_ids,
        cotangent,
        time_embed,
    )
    near[0].finish()
    far_own = [up_weight, down_weight]
    far_peer = [swap_core(w) for w in far_own]

    def far_gather(layer, token):
        (piece,) = after(token, weave(core_word, far_own, far_peer, layer, 1))
        return Gather(ring, piece)

    def near_gather(layer, token):
        (piece,) = after(token, weave(core_word, near_own, near_peer, layer, 1))
        return Gather(ring, piece)

    far = [far_gather(0, moving(near[0]))]

    biases = jnp.concatenate([query_bias, value_bias, up_bias], axis=1)
    peer_biases = swap_core(biases)
    bias_low = jnp.where(core == 0, biases, peer_biases)
    bias_high = jnp.where(core == 0, peer_biases, biases)

    def bias_of(start, size):
        return jnp.concatenate(
            [bias_low[:, start : start + size], bias_high[:, start : start + size]], axis=1
        )

    q_bias = bias_of(0, head_width)
    v_bias = bias_of(head_width, head_width)
    u_bias = bias_of(2 * head_width, hidden_width)

    segments = segment_ids[0]

    def ids_at(block):
        return lax.dynamic_slice_in_dim(segments, block * rows, rows)

    ids = [ids_at(core), ids_at(2 + core), ids_at(1 - core), ids_at(3 - core)]
    lane = jnp.arange(128)[None, :]
    marks = [lane == part[:, None] + 1 for part in ids]
    q_marks = [jnp.where((lane < 9) & ~mark, NEVER, 0.0).astype(LOW) for mark in marks[:2]]
    k_marks = [mark.astype(LOW) for mark in marks]
    valid = (ids_at(place) >= 0)[:, None]
    seed = jnp.where(valid, cotangent, jnp.zeros_like(cotangent))

    kept = []
    state = [part.astype(WIDE) + time_embed.astype(WIDE) for part in hidden_pair]
    for layer in range(layers):
        w_qkv = near[layer].whole[:, : 3 * width]
        w_out = near[layer].whole[:, 3 * width :]
        firsts, queries, pairs = [], [], []
        for j in range(2):
            first = norm_forward(state[j], first_gain[layer], first_shift[layer])
            made = dot(first, w_qkv)
            firsts.append(first)
            query = (made[:, :width] + q_bias[layer]).astype(LOW)
            queries.append(query * jnp.asarray(scale, LOW))
            pairs.append(
                jnp.concatenate(
                    [
                        made[:, width : 2 * width].astype(LOW),
                        (made[:, 2 * width :] + v_bias[layer]).astype(LOW),
                    ],
                    axis=1,
                )
            )
        pairs = pairs + [swap_core(pair) for pair in pairs]
        mixeds, norms, parts = [], [], []
        for j in range(2):
            if j == 1:
                queries[1] = far[layer].slot(queries[1])
            mixed, norm = attend(queries[j], q_marks[j], pairs, k_marks)
            mixeds.append(mixed)
            norms.append(norm)
            parts.append(dot_nt(mixed, w_out))
        arrived = [swap_y(part.astype(LOW)) for part in parts]
        arrived[0] = far[layer].finish(arrived[0])
        if layer == 0:
            seeds = both_sides(seed)
            near.append(near_gather(1, moving(far[0])))
        w_up = far[layer].whole[:, :hidden]
        w_down = far[layer].whole[:, hidden:]
        middles, seconds, acts, slopes, branches = [], [], [], [], []
        for j in range(2):
            if j == 1:
                if layer == 0:
                    arrived[1] = near[1].slot(arrived[1])
                arrived[1], acts[0] = tie(arrived[1], acts[0])
            middle = state[j] + (parts[j] + arrived[j].astype(WIDE)) + output_bias[layer]
            second = norm_forward(middle, second_gain[layer], second_shift[layer])
            act, slope = gelu_both(dot(second, w_up) + u_bias[layer])
            middles.append(middle)
            seconds.append(second)
            acts.append(act)
            slopes.append(slope)
            if layer < layers - 1:
                branches.append(dot_nt(act, w_down))
        kept.append((state, firsts, queries, pairs, norms, mixeds, middles, seconds, acts, slopes))
        if layer < layers - 1:
            arrived = [swap_y(part.astype(LOW)) for part in branches]
            arrived[0] = near[1].finish(arrived[0])
            far.append(far_gather(1, moving(near[1])))
            arrived[1] = far[1].slot(arrived[1])
            state = [
                middles[j] + (branches[j] + arrived[j].astype(WIDE)) + down_bias[layer]
                for j in range(2)
            ]

    def wide_at(vector):
        spread = jnp.zeros((2 * vector.shape[0],), WIDE)
        return lax.dynamic_update_slice_in_dim(spread, vector, side * vector.shape[0], 0)

    def columns_of(size, pieces):
        def pick(which):
            def run(array):
                low, high, start = [], [], 0
                for _ in range(pieces):
                    low.append(array[:, start : start + size])
                    high.append(array[:, start + size : start + 2 * size])
                    start += 2 * size
                low, high = jnp.concatenate(low, axis=1), jnp.concatenate(high, axis=1)
                return jnp.where(core == which, low, high)

            return run

        return pick(0), pick(1)

    heads_columns = columns_of(head_width, 4)
    feed_columns = columns_of(hidden_width, 2)
    vectors = [dict() for _ in range(layers)]
    grads = [part.astype(WIDE) for part in seeds]
    lows = seeds
    scatters = {}

    def advance(main):
        for scatter in scatters.values():
            main = scatter.slot(main)
        return main

    for layer in reversed(range(layers)):
        (state, firsts, queries, pairs, norms, mixeds, middles, seconds, acts, slopes) = kept[layer]
        w_qkv = near[layer].whole[:, : 3 * width]
        w_out = near[layer].whole[:, 3 * width :]
        w_up = far[layer].whole[:, :hidden]
        w_down = far[layer].whole[:, hidden:]
        if layer < layers - 1:
            grads, lows, gains, shifts = [], [], [], []
            for j in range(2):
                arrived[j] = advance(arrived[j])
                if j == 1:
                    arrived[1], lows[0] = tie(arrived[1], lows[0])
                g_first = first_parts[j] + arrived[j].astype(WIDE)
                gain, shift, through = norm_backward(g_first, above[j], first_gain[layer + 1])
                grad = g_middles[j] + through
                grads.append(grad)
                lows.append(grad.astype(LOW))
                gains.append(gain)
                shifts.append(shift)
            vectors[layer + 1]["first"] = [own_of(gains), own_of(shifts)]
        vectors[layer]["down"] = jnp.sum(own_of(grads), axis=0)
        g_pres, parts = [], []
        for j in range(2):
            g_pre = (dot(lows[j], w_down) * slopes[j].astype(WIDE)).astype(LOW)
            g_pres.append(g_pre)
            parts.append(dot_nt(g_pre, w_up))
        arrived = [swap_y(part.astype(LOW)) for part in parts]
        g_pre = rows_of(g_pres)
        vectors[layer]["up"] = wide_at(jnp.sum(g_pre.astype(WIDE), axis=0))
        d_feed = jnp.concatenate(
            [
                dot_tn(rows_of(seconds), g_pre).astype(LOW),
                dot_tn(rows_of(lows), rows_of(acts)).astype(LOW),
            ],
            axis=1,
        )
        scatters[layer, "feed"] = Scatter(ring, d_feed, *feed_columns)
        g_middles, m_lows, gains, shifts, dqs, owns, aways = [], [], [], [], [], [], []
        for j in range(2):
            arrived[j] = advance(arrived[j])
            if j == 1:
                arrived[1], m_lows[0] = tie(arrived[1], m_lows[0])
            g_second = parts[j] + arrived[j].astype(WIDE)
            gain, shift, through = norm_backward(g_second, middles[j], second_gain[layer])
            g_middle = grads[j] + through
            m_low = g_middle.astype(LOW)
            g_mixed = dot(m_low, w_out).astype(LOW)
            dq, own, away = attend_back(queries[j], q_marks[j], norms[j], g_mixed, pairs, k_marks)
            gains.append(gain)
            shifts.append(shift)
            g_middles.append(g_middle)
            m_lows.append(m_low)
            dqs.append(dq)
            owns.append(own)
            aways.append(swap_core(away))
        vectors[layer]["second"] = [own_of(gains), own_of(shifts)]
        vectors[layer]["out"] = jnp.sum(own_of(g_middles), axis=0)
        aways[1] = advance(aways[1])
        g_pair = (
            owns[0].astype(WIDE)
            + owns[1].astype(WIDE)
            + (aways[0].astype(WIDE) + aways[1].astype(WIDE))
        ).astype(LOW)
        g_qkv = jnp.concatenate([rows_of(dqs), g_pair], axis=1)
        first_parts = [dot_nt(g_qkv[:rows], w_qkv), dot_nt(g_qkv[rows:], w_qkv)]
        sums = jnp.sum(g_qkv.astype(WIDE), axis=0)
        vectors[layer]["query"] = wide_at(sums[:width])
        vectors[layer]["value"] = wide_at(sums[2 * width :])
        if layer > 0:
            arrived = [swap_y(part.astype(LOW)) for part in first_parts]
            above = state
        else:
            arrived = swap_y(other_of(first_parts).astype(LOW))
            g_first = own_of(first_parts) + arrived.astype(WIDE)
            gain, shift, through = norm_backward(g_first, own_of(state), first_gain[0])
            input_grad = own_of(g_middles) + through
            vectors[0]["first"] = [gain, shift]
        d_near = jnp.concatenate(
            [
                dot_tn(rows_of(firsts), g_qkv).astype(LOW),
                dot_tn(rows_of(m_lows), rows_of(mixeds)).astype(LOW),
            ],
            axis=1,
        )
        scatters[layer, "near"] = Scatter(ring, d_near, *heads_columns)
        if layer == layers - 1:
            crossed = swap_y(dot_nt(other_of(acts), w_down).astype(LOW))
            denoised = (
                own_of(middles)
                + (dot_nt(own_of(acts), w_down) + crossed.astype(WIDE))
                + down_bias[layer]
            ).astype(LOW)

    matrix_out = [None] * layers
    for layer in reversed(range(layers)):
        big = scatters[layer, "feed"].finish()
        small = scatters[layer, "near"].finish()
        heads_of = lambda i: small[:, i * head_width : (i + 1) * head_width]
        matrix_out[layer] = (
            heads_of(0),
            heads_of(1),
            heads_of(2),
            heads_of(3).T,
            big[:, :hidden_width],
            big[:, hidden_width:].T,
        )
    rows_out = []
    for layer in range(layers):
        v = vectors[layer]
        rows_out += [
            *v["first"],
            *v["second"],
            v["out"],
            v["down"],
            v["query"],
            v["value"],
            *jnp.split(v["up"], 4),
        ]
    total = sum_everywhere(jnp.stack(rows_out)).reshape(layers, -1, depth)
    ups = total[:, 8:].reshape(layers, -1)
    stacked = [jnp.stack([matrix_out[layer][index] for layer in range(layers)]) for index in range(6)]

    def mine(array, size):
        return lax.dynamic_slice_in_dim(array, place * size, size, 1)

    return (
        denoised,
        input_grad,
        *stacked,
        mine(total[:, 6], head_width),
        mine(total[:, 7], head_width),
        total[:, 4],
        mine(ups, hidden_width),
        total[:, 5],
        total[:, 0],
        total[:, 1],
        total[:, 2],
        total[:, 3],
    )


def solution(mesh):
    rows = P(("fsdp", "tensor"), None)
    inner = P(None, "fsdp", "tensor")
    outer = P(None, "tensor", "fsdp")
    cut = P(None, "tensor")
    in_specs = (
        rows,
        P("fsdp", None),
        P("fsdp", None),
        rows,
        inner,
        inner,
        inner,
        outer,
        inner,
        outer,
        cut,
        cut,
        P(),
        cut,
        P(),
        P(),
        P(),
        P(),
        P(),
    )
    out_specs = (
        rows,
        rows,
        inner,
        inner,
        inner,
        outer,
        inner,
        outer,
        cut,
        cut,
        P(),
        cut,
        P(),
        P(),
        P(),
        P(),
        P(),
    )
    return jax.shard_map(local, mesh=mesh, in_specs=in_specs, out_specs=out_specs, check_vma=False)
```

```python
import functools

import jax
import jax.numpy as jnp
from jax import lax
from jax.experimental import pallas as pl
from jax.experimental.pallas import tpu as pltpu
from jax.sharding import PartitionSpec as P

HEAD_DIM = 64
EPSILON = 1e-05
LOW = jnp.bfloat16
WIDE = jnp.float32
ROOT = 0.7978845608028654
CUBE = 0.044715

SWAP_CORE = [(0, 1), (1, 0), (2, 3), (3, 2)]
SWAP_Y = [(0, 2), (2, 0), (1, 3), (3, 1)]


def swap_core(value):
    return lax.ppermute(value, "tensor", SWAP_CORE)


def swap_y(value):
    return lax.ppermute(value, "tensor", SWAP_Y)


def dot(a, b):
    return jnp.dot(a, b, preferred_element_type=WIDE)


def dot_nt(a, b):
    return lax.dot_general(a, b, (((1,), (1,)), ((), ())), preferred_element_type=WIDE)


def dot_tn(a, b):
    return lax.dot_general(a, b, (((0,), (0,)), ((), ())), preferred_element_type=WIDE)


def tie(*values):
    return lax.optimization_barrier(values)


def ring_order(count):
    return list(range(0, count, 2)) + list(range(count - 1, 0, -2))


class Ring:
    def __init__(self):
        self.count = lax.axis_size("fsdp")
        self.use = self.count == 8
        self.core = lax.axis_index("tensor") % 2
        if self.use:
            here = lax.axis_index("fsdp")
            self.place = jnp.where(here % 2 == 0, here // 2, self.count - 1 - here // 2)
            self.way = 1 - 2 * self.core
            self.far = self.count // 2
            order = ring_order(self.count)
            self.pairs = [
                [(order[i], order[(i + way) % self.count]) for i in range(self.count)]
                for way in (1, -1)
            ]
            self.split = [
                (here * 4 + t, there * 4 + t)
                for t in range(4)
                for here, there in self.pairs[t % 2]
            ]
            self.blocks = jnp.stack([self.block_at(step) for step in range(self.count)])

    def split_send(self, value):
        return lax.ppermute(value, ("fsdp", "tensor"), self.split)

    def send_both(self, ahead, behind):
        return lax.ppermute(ahead, "fsdp", self.pairs[0]), lax.ppermute(behind, "fsdp", self.pairs[1])

    def block_at(self, steps):
        place = (self.place + steps + 2 * self.count) % self.count
        return jnp.where(place < self.count // 2, 2 * place, 2 * (self.count - 1 - place) + 1)


class Gather:
    def __init__(self, ring, piece):
        self.ring = ring
        self.rows, self.columns = piece.shape
        self.todo = []
        self.done = 0
        if ring.use:
            self.whole = jnp.zeros((ring.count * self.rows, self.columns), piece.dtype)
            self.put(piece, lax.axis_index("fsdp"))
            self.current = piece
        else:
            self.whole = lax.all_gather(piece, "fsdp", axis=0, tiled=True)

    def put(self, value, block, offset=0):
        start = block * self.rows + offset
        self.whole = lax.dynamic_update_slice(self.whole, value, (start, 0))

    def flush(self):
        ring = self.ring
        half = self.rows // 2
        for step, value in self.todo:
            if step < ring.far:
                self.put(value, ring.block_at(-ring.way * step))
                self.put(swap_core(value), ring.block_at(ring.way * step))
            else:
                block = ring.block_at(step)
                self.put(value, block, ring.core * half)
                self.put(swap_core(value), block, (1 - ring.core) * half)
        self.todo = []

    def step(self, token=None):
        ring = self.ring
        if not ring.use or self.done == ring.far:
            return
        self.flush()
        self.done += 1
        current = self.current
        if token is not None:
            current, _ = tie(current, token)
        if self.done == ring.far:
            half = self.rows // 2
            current = lax.dynamic_slice(current, (ring.core * half, 0), (half, self.columns))
        self.current = ring.split_send(current)
        self.todo.append((self.done, self.current))

    def finish(self):
        if self.ring.use:
            while self.done < self.ring.far:
                self.step()
            self.flush()


class Scatter:
    def __init__(self, ring, owns, gots):
        self.ring = ring
        self.owns, self.gots = owns, gots
        self.done = 0
        if ring.use:
            self.rows = owns[0].shape[0] // ring.count
        else:
            total = jnp.concatenate(
                [own.astype(WIDE) + got.astype(WIDE) for own, got in zip(owns, gots)], axis=1
            )
            self.result = lax.psum_scatter(total, "fsdp", scatter_dimension=0, tiled=True)

    def step(self, main=None):
        ring = self.ring
        if not ring.use or self.done == ring.far:
            return main
        moving = self.moving if self.done else None
        ahead, behind = ring.send_both(
            *passing(ring.blocks, self.owns, self.gots, ring.far - self.done, ring.count, moving)
        )
        if main is not None:
            main, ahead, behind = tie(main, ahead, behind)
        self.moving = (ahead, behind)
        self.done += 1
        if self.done == ring.far:
            self.result = passing(ring.blocks, self.owns, self.gots, 0, ring.count, self.moving)[0]
        return main

    def finish(self):
        if self.ring.use:
            while self.done < self.ring.far:
                self.step()
        return self.result


def exchanges(count):
    moves = [swap_core, swap_y]
    bit = 1
    while bit < count:
        pairs = [(i, i ^ bit) for i in range(count)]
        moves.append(lambda value, pairs=pairs: lax.ppermute(value, "fsdp", pairs))
        bit *= 2
    return moves


ROOM = 16 << 20
NEVER = -1e30


def out(shape, dtype=LOW):
    return jax.ShapeDtypeStruct(shape, dtype)


def kernel_call(kernel, operands, outs, scratch=(), scalars=0, cost=1.0):
    inside = pl.BlockSpec(memory_space=pltpu.VMEM)
    word = pl.BlockSpec(memory_space=pltpu.SMEM)
    return pl.pallas_call(
        kernel,
        in_specs=[word] * scalars + [inside] * (len(operands) - scalars),
        out_specs=[inside] * len(outs),
        out_shape=outs,
        scratch_shapes=scratch,
        compiler_params=pltpu.CompilerParams(vmem_limit_bytes=ROOM),
        cost_estimate=pl.CostEstimate(
            flops=int(cost * 1e9), bytes_accessed=1024, transcendentals=0
        ),
    )(*operands)


def norm_parts(rows):
    center = rows - jnp.mean(rows, axis=1, keepdims=True)
    factor = lax.rsqrt(jnp.mean(center * center, axis=1, keepdims=True) + EPSILON)
    return center * factor, factor


def norm_backward(grad, rows, gain):
    normed, factor = norm_parts(rows)
    scaled = grad * gain
    through = factor * (
        scaled
        - jnp.mean(scaled, axis=1, keepdims=True)
        - normed * jnp.mean(scaled * normed, axis=1, keepdims=True)
    )
    gain_grad = jnp.sum(grad * normed, axis=0, keepdims=True)
    return gain_grad, jnp.sum(grad, axis=0, keepdims=True), through


def gelu_both(pre):
    inner = jnp.tanh(ROOT * (pre + CUBE * pre * pre * pre))
    slope = 0.5 * (1.0 + inner) + 0.5 * pre * (1.0 - inner * inner) * (
        ROOT * (1.0 + 3.0 * CUBE * pre * pre)
    )
    return 0.5 * pre * (1.0 + inner), slope


def project(layer, base, part, arrived, bias, gain, shift, weights, q_bias, v_bias):
    rows, depth = base.shape
    width = q_bias.shape[1]
    scale = HEAD_DIM ** (-0.5)
    at = slice(layer, layer + 1)

    def kernel(base_ref, part_ref, arrived_ref, bias_ref, gain_ref, shift_ref, w_ref, qb_ref, vb_ref,
               state_ref, first_ref, q_ref, kv_ref):
        state = base_ref[...] + (part_ref[...].astype(WIDE) + arrived_ref[...].astype(WIDE))
        state += bias_ref[layer - 1 : layer, :]
        first = (norm_parts(state)[0] * gain_ref[at, :] + shift_ref[at, :]).astype(LOW)
        state_ref[...] = state
        first_ref[...] = first
        query = (dot(first, w_ref[:, :width]) + qb_ref[at, :]).astype(LOW)
        q_ref[...] = query * jnp.asarray(scale, LOW)
        kv_ref[:, :width] = dot(first, w_ref[:, width : 2 * width]).astype(LOW)
        kv_ref[:, width:] = (dot(first, w_ref[:, 2 * width : 3 * width]) + vb_ref[at, :]).astype(LOW)

    return kernel_call(
        kernel,
        (base, part, arrived, bias, gain, shift, weights, q_bias, v_bias),
        [
            out((rows, depth), WIDE),
            out((rows, depth)),
            out((rows, width)),
            out((rows, 2 * width)),
        ], cost=1.2)


def feed(layer, state, part, arrived, out_bias, gain, shift, weights, up_bias, lows=None):
    rows, depth = state.shape
    hidden = up_bias.shape[1]
    back = lows is not None
    half = hidden // 2
    tile = 384
    row = slice(layer, layer + 1)

    def kernel(*refs):
        state_ref, part_ref, arrived_ref, ob_ref, gain_ref, shift_ref, w_ref, ub_ref = refs[:8]
        refs = refs[8:]
        middle = (
            state_ref[...] + (part_ref[...].astype(WIDE) + arrived_ref[...].astype(WIDE)) + ob_ref[row, :]
        )
        second = (norm_parts(middle)[0] * gain_ref[row, :] + shift_ref[row, :]).astype(LOW)
        if back:
            lows_ref, middle_ref, second_ref, act_ref, other_ref, branch_ref, ubg_ref = refs
            low = lows_ref[...]
        else:
            middle_ref, second_ref, act_ref, other_ref, branch_ref = refs
        middle_ref[...] = middle
        second_ref[...] = second
        total = None
        for start in range(0, hidden, tile):
            at = slice(start, start + tile)
            inside = start + start // half * half
            up = w_ref[:, inside : inside + tile]
            down = w_ref[:, half + inside : half + inside + tile]
            act, slope = gelu_both(dot(second, up) + ub_ref[row, at])
            act = act.astype(LOW)
            act_ref[:, at] = act
            if back:
                other = (dot(low, down) * slope).astype(LOW)
                ubg_ref[0:1, at] = jnp.sum(other.astype(WIDE), axis=0, keepdims=True)
                here = dot_nt(other, up)
            else:
                other = slope.astype(LOW)
                here = dot_nt(act, down)
            other_ref[:, at] = other
            total = here if total is None else total + here
        branch_ref[...] = total.astype(LOW)

    operands = [state, part, arrived, out_bias, gain, shift, weights, up_bias]
    outs = [
        out((rows, depth), WIDE),
        out((rows, depth)),
        out((rows, hidden)),
        out((rows, hidden)),
        out((rows, depth)),
    ]
    if back:
        operands.append(lows)
        outs.append(out((8, hidden), WIDE))
    return kernel_call(kernel, operands, outs, cost=4.0)


def feed_back(layer, g_middle, part, arrived, state, gain, slopes, weights):
    rows, depth = state.shape
    hidden = slopes.shape[1]
    half = hidden // 2
    tile = 384

    def kernel(gm_ref, part_ref, arrived_ref, state_ref, gain_ref, slope_ref, w_ref,
               grad_ref, low_ref, gpre_ref, branch_ref, sums_ref, ubg_ref):
        incoming = part_ref[...].astype(WIDE) + arrived_ref[...].astype(WIDE)
        gain_grad, shift_grad, through = norm_backward(incoming, state_ref[...], gain_ref[layer : layer + 1, :])
        grad = gm_ref[...] + through
        low = grad.astype(LOW)
        grad_ref[...] = grad
        low_ref[...] = low
        sums_ref[0:1, :] = gain_grad
        sums_ref[1:2, :] = shift_grad
        sums_ref[2:3, :] = jnp.sum(grad, axis=0, keepdims=True)
        total = None
        for start in range(0, hidden, tile):
            at = slice(start, start + tile)
            inside = start + start // half * half
            up = w_ref[:, inside : inside + tile]
            down = w_ref[:, half + inside : half + inside + tile]
            gpre = (dot(low, down) * slope_ref[:, at].astype(WIDE)).astype(LOW)
            gpre_ref[:, at] = gpre
            ubg_ref[0:1, at] = jnp.sum(gpre.astype(WIDE), axis=0, keepdims=True)
            here = dot_nt(gpre, up)
            total = here if total is None else total + here
        branch_ref[...] = total.astype(LOW)

    return kernel_call(
        kernel,
        (g_middle, part, arrived, state, gain, slopes, weights),
        [
            out((rows, depth), WIDE),
            out((rows, depth)),
            out((rows, hidden)),
            out((rows, depth)),
            out((8, depth), WIDE),
            out((8, hidden), WIDE),
        ], cost=3.8)

def turned(value):
    return value.astype(WIDE).T.astype(LOW)


def outer_feed(core, seconds, g_pres, lows, acts, which):
    depth = seconds[0].shape[1]
    size = acts[0].shape[1] // 2

    def kernel(core_ref, s0, s1, g0, g1, l0, l1, a0, a1, out_ref):
        start = jnp.where(core_ref[0] == which, 0, size)
        for index, (left_refs, right_refs) in enumerate((((s0, s1), (g0, g1)), ((l0, l1), (a0, a1)))):
            left = jnp.concatenate([turned(ref[...]) for ref in left_refs], axis=1)
            for at in range(0, size, 384):
                columns = pl.ds(pl.multiple_of(start + at, 128), 384)
                right = jnp.concatenate([ref[:, columns] for ref in right_refs])
                base = index * size + at
                out_ref[:, base : base + 384] = dot(left, right).astype(LOW)

    return kernel_call(
        kernel,
        (core, *seconds, *g_pres, *lows, *acts),
        [out((depth, 2 * size))],
        scalars=1,
        cost=2.0,
    )[0]


def outer_heads(core, firsts, g_qkv, m_lows, mixeds, which):
    depth = firsts[0].shape[1]
    width = mixeds[0].shape[1]
    size = width // 2

    def kernel(core_ref, f0, f1, g_ref, l0, l1, m0, m1, out_ref):
        low = core_ref[0] == which

        def pick(value):
            return jnp.where(low, value[:, :size], value[:, size:])

        first = jnp.concatenate([turned(f0[...]), turned(f1[...])], axis=1)
        g = g_ref[...]
        right = jnp.concatenate(
            [pick(g[:, i * width : (i + 1) * width]) for i in range(3)], axis=1
        )
        m_low = jnp.concatenate([turned(l0[...]), turned(l1[...])], axis=1)
        mixed = jnp.concatenate([pick(m0[...]), pick(m1[...])])
        out_ref[...] = jnp.concatenate([dot(first, right), dot(m_low, mixed)], axis=1).astype(LOW)

    return kernel_call(
        kernel, (core, *firsts, g_qkv, *m_lows, *mixeds), [out((depth, 4 * size))], scalars=1, cost=1.8)[0]


def passing(blocks, owns, gots, step, count, moving):
    parts = len(owns)
    rows = owns[0].shape[0] // count
    half = rows // 2
    columns = sum(own.shape[1] for own in owns)
    first = moving is None
    last = step == 0
    partial_in = not first and moving[0].shape[0] == half

    def kernel(blocks_ref, *refs):
        own_refs, got_refs = refs[:parts], refs[parts : 2 * parts]
        rest = refs[2 * parts :]
        moving_refs, out_refs = (rest[:2], rest[2:]) if not first else ((), rest)

        def here(index, offset=0, size=rows):
            start = pl.multiple_of(blocks_ref[index] * rows + offset, 16)
            at = pl.ds(start, size)
            return jnp.concatenate(
                [
                    own[at, :].astype(WIDE) + got[at, :].astype(WIDE)
                    for own, got in zip(own_refs, got_refs)
                ],
                axis=1,
            )

        if first:
            out_refs[0][...] = here(step, 0, half).astype(LOW)
            out_refs[1][...] = here(step, half, half).astype(LOW)
        elif last:
            total = here(0) + moving_refs[0][...].astype(WIDE) + moving_refs[1][...].astype(WIDE)
            out_refs[0][...] = total
        else:
            ahead, behind = here(step), here((count - step) % count)
            a, b = moving_refs[0][...].astype(WIDE), moving_refs[1][...].astype(WIDE)
            if partial_in:
                out_refs[0][:half, :] = (ahead[:half] + a).astype(LOW)
                out_refs[0][half:, :] = ahead[half:].astype(LOW)
                out_refs[1][:half, :] = behind[:half].astype(LOW)
                out_refs[1][half:, :] = (behind[half:] + b).astype(LOW)
            else:
                out_refs[0][...] = (ahead + a).astype(LOW)
                out_refs[1][...] = (behind + b).astype(LOW)

    if last:
        outs = [out((rows, columns), WIDE)]
    else:
        outs = [out((half if first else rows, columns))] * 2
    operands = (blocks, *owns, *gots) + (() if first else tuple(moving))
    return kernel_call(kernel, operands, outs, scalars=1, cost=0.8)


def pack_near(weights):
    layers, rows, size = weights[0].shape

    def kernel(q_ref, k_ref, v_ref, o_ref, out_ref):
        for layer in range(layers):
            out_ref[layer] = jnp.concatenate(
                [q_ref[layer], k_ref[layer], v_ref[layer], turned(o_ref[layer])], axis=1
            )

    return kernel_call(kernel, weights, [out((layers, rows, 4 * size))])[0]


def weave_near(core, own, peer):
    layers, rows, columns = own.shape
    size = columns // 4

    def kernel(core_ref, own_ref, peer_ref, *out_refs):
        first = core_ref[0] == 0
        for layer, out_ref in enumerate(out_refs):
            a, b = own_ref[layer], peer_ref[layer]
            low, high = jnp.where(first, a, b), jnp.where(first, b, a)
            parts = []
            for i in range(4):
                parts += [low[:, i * size : (i + 1) * size], high[:, i * size : (i + 1) * size]]
            out_ref[...] = jnp.concatenate(parts, axis=1)

    return kernel_call(
        kernel, (core, own, peer), [out((rows, 2 * columns))] * layers, scalars=1
    )


def pack_far(up, down):
    layers, rows, size = up.shape

    def kernel(up_ref, down_ref, *out_refs):
        for layer, out_ref in enumerate(out_refs):
            out_ref[:, :size] = up_ref[layer]
            out_ref[:, size:] = turned(down_ref[layer])

    return kernel_call(kernel, (up, down), [out((rows, 2 * size))] * layers)


def weave_far(core, own, peer):
    rows, columns = own[0].shape

    def kernel(core_ref, *refs):
        first = core_ref[0] == 0
        count = len(own)
        for index in range(count):
            a, b = refs[index][...], refs[count + index][...]
            refs[2 * count + index][:, :columns] = jnp.where(first, a, b)
            refs[2 * count + index][:, columns:] = jnp.where(first, b, a)

    return kernel_call(
        kernel, (core, *own, *peer), [out((rows, 2 * columns))] * len(own), scalars=1
    )


def weave_bias(core, own, peer, size):
    layers = own.shape[0]
    rest = own.shape[1] - 2 * size

    def kernel(core_ref, own_ref, peer_ref, q_ref, v_ref, u_ref):
        first = core_ref[0] == 0
        a, b = own_ref[...], peer_ref[...]
        low, high = jnp.where(first, a, b), jnp.where(first, b, a)
        q_ref[...] = jnp.concatenate([low[:, :size], high[:, :size]], axis=1)
        v_ref[...] = jnp.concatenate([low[:, size : 2 * size], high[:, size : 2 * size]], axis=1)
        u_ref[...] = jnp.concatenate([low[:, 2 * size :], high[:, 2 * size :]], axis=1)

    return kernel_call(
        kernel,
        (core, own, peer),
        [
            out((layers, 2 * size), WIDE),
            out((layers, 2 * size), WIDE),
            out((layers, 2 * rest), WIDE),
        ],
        scalars=1,
    )


def mark_documents(core, segments, rows):
    def kernel(core_ref, segment_ref, *refs):
        core = core_ref[0]
        blocks = [core, 2 + core, 1 - core, 3 - core]
        lane = lax.broadcasted_iota(jnp.int32, (128, rows), 0)
        for index, block in enumerate(blocks):
            at = pl.ds(pl.multiple_of(block * rows, 128), rows)
            mark = jnp.where(lane == segment_ref[:, at] + 1, 1.0, 0.0).T
            refs[2 + index][...] = mark.astype(LOW)
            if index < 2:
                real = lax.broadcasted_iota(jnp.int32, (rows, 128), 1) < 9
                refs[index][...] = jnp.where(real & (mark == 0.0), NEVER, 0.0).astype(LOW)

    made = kernel_call(kernel, (core, segments), [out((rows, 128))] * 6, scalars=1)
    return made[:2], made[2:]


def seed_rows(side, own, other, marks):
    rows, depth = own.shape

    def kernel(side_ref, own_ref, other_ref, m0, m1, low0, low1, sums_ref):
        total = None
        for j, (mark, low) in enumerate(((m0, low0), (m1, low1))):
            mine = side_ref[0] == j
            value = jnp.where(mine, own_ref[...], other_ref[...])
            value = jnp.where(mark[:, 0:1] > 0, jnp.zeros_like(value), value)
            low[...] = value
            here = jnp.sum(value.astype(WIDE), axis=0, keepdims=True)
            here = jnp.where(mine, here, 0.0)
            total = here if total is None else total + here
        sums_ref[0:1, :] = total

    return kernel_call(
        kernel,
        (side, own, other, *marks),
        [out((rows, depth)), out((rows, depth)), out((8, depth), WIDE)],
        scalars=1,
    )


def project_first(side, own, other, embed, gain, shift, weights, q_bias, v_bias):
    rows, depth = own.shape
    width = q_bias.shape[1]
    scale = HEAD_DIM ** (-0.5)

    def kernel(side_ref, own_ref, other_ref, embed_ref, gain_ref, shift_ref, w_ref, qb_ref, vb_ref, *refs):
        firsts = []
        for j in range(2):
            rows_in = jnp.where(side_ref[0] == j, own_ref[...], other_ref[...])
            state = rows_in.astype(WIDE) + embed_ref[...].astype(WIDE)
            refs[j][...] = state
            first = (norm_parts(state)[0] * gain_ref[0:1, :] + shift_ref[0:1, :]).astype(LOW)
            refs[2 + j][...] = first
            firsts.append(first)
        first = jnp.concatenate(firsts)
        query = (dot(first, w_ref[:, :width]) + qb_ref[0:1, :]).astype(LOW)
        query = query * jnp.asarray(scale, LOW)
        key = dot(first, w_ref[:, width : 2 * width]).astype(LOW)
        value = (dot(first, w_ref[:, 2 * width : 3 * width]) + vb_ref[0:1, :]).astype(LOW)
        for j in range(2):
            at = slice(j * rows, (j + 1) * rows)
            refs[4 + j][...] = query[at]
            refs[6 + j][:, :width] = key[at]
            refs[6 + j][:, width:] = value[at]

    made = kernel_call(
        kernel,
        (side, own, other, embed, gain, shift, weights, q_bias, v_bias),
        [out((rows, depth), WIDE)] * 2
        + [out((rows, depth))] * 2
        + [out((rows, width))] * 2
        + [out((rows, 2 * width))] * 2,
        scalars=1, cost=1.8)
    return [made[2 * i : 2 * i + 2] for i in range(4)]


def last_branch(side, acts, weights):
    rows, hidden = acts[0].shape
    depth = weights.shape[0]
    size = hidden // 2

    def kernel(side_ref, a0, a1, w_ref, away_ref, here_ref):
        for flip, ref in ((1, away_ref), (0, here_ref)):
            act = jnp.where(side_ref[0] == flip, a0[...], a1[...])
            total = dot_nt(act[:, :size], w_ref[:, size : 2 * size])
            total += dot_nt(act[:, size:], w_ref[:, 3 * size :])
            ref[...] = total.astype(ref.dtype)

    return kernel_call(
        kernel,
        (side, *acts, weights),
        [out((rows, depth)), out((rows, depth), WIDE)],
        scalars=1, cost=1.4)


def last_rows(side, middles, here, crossed, bias, layer):
    rows, depth = here.shape

    def kernel(side_ref, m0, m1, here_ref, crossed_ref, bias_ref, out_ref):
        middle = jnp.where(side_ref[0] == 0, m0[...], m1[...])
        total = here_ref[...] + crossed_ref[...].astype(WIDE)
        out_ref[...] = (middle + total + bias_ref[layer : layer + 1, :]).astype(LOW)

    return kernel_call(
        kernel, (side, *middles, here, crossed, bias), [out((rows, depth))], scalars=1
    )[0]


def project_back(side, dqs, owns, aways, weights, last):
    rows, width = dqs[0].shape
    depth = weights.shape[0]

    def kernel(side_ref, dq0, dq1, own0, own1, away0, away1, w_ref, g_ref, part0, part1, sums_ref):
        pair = (
            own0[...].astype(WIDE)
            + own1[...].astype(WIDE)
            + (away0[...].astype(WIDE) + away1[...].astype(WIDE))
        ).astype(LOW)
        g_ref[:rows, :width] = dq0[...]
        g_ref[rows:, :width] = dq1[...]
        g_ref[:, width:] = pair
        g = g_ref[...]
        total = dot_nt(g, w_ref[:, : 3 * width])
        low, high = total[:rows], total[rows:]
        if last:
            part0[...] = jnp.where(side_ref[0] == 0, high, low).astype(LOW)
            part1[...] = jnp.where(side_ref[0] == 0, low, high)
        else:
            part0[...] = low.astype(LOW)
            part1[...] = high.astype(LOW)
        sums_ref[0:1, :] = jnp.sum(g[:, :width].astype(WIDE), axis=0, keepdims=True)
        sums_ref[1:2, :] = jnp.sum(pair[:, width:].astype(WIDE), axis=0, keepdims=True)

    return kernel_call(
        kernel,
        (side, *dqs, *owns, *aways, weights),
        [
            out((2 * rows, 3 * width)),
            out((rows, depth)),
            out((rows, depth), WIDE if last else LOW),
            out((8, width), WIDE),
        ],
        scalars=1, cost=1.6)


def first_rows(side, here, arrived, states, g_middles, gain):
    rows, depth = here.shape

    def kernel(side_ref, here_ref, arrived_ref, s0, s1, g0, g1, gain_ref, out_ref, sums_ref):
        low = side_ref[0] == 0
        incoming = here_ref[...] + arrived_ref[...].astype(WIDE)
        state = jnp.where(low, s0[...], s1[...])
        gain_grad, shift_grad, through = norm_backward(incoming, state, gain_ref[0:1, :])
        out_ref[...] = jnp.where(low, g0[...], g1[...]) + through
        sums_ref[0:1, :] = gain_grad
        sums_ref[1:2, :] = shift_grad

    return kernel_call(
        kernel,
        (side, here, arrived, *states, *g_middles, gain),
        [out((rows, depth), WIDE), out((8, depth), WIDE)],
        scalars=1,
    )


def vector_rows(place, entries, layers, depth):
    arrays = [array for _, _, group in entries for array in group]

    def kernel(place_ref, *refs):
        out_ref = refs[-1]
        place = place_ref[0]
        side = place // 2
        at = 0
        for row, (take, index), group in entries:
            here = refs[at : at + len(group)]
            at += len(group)
            if take == "own":
                value = jnp.where(side == 0, here[0][index : index + 1, :], here[1][index : index + 1, :])
                out_ref[row : row + 1, :] = value
            elif take == "one":
                out_ref[row : row + 1, :] = here[0][index : index + 1, :]
            elif take == "half":
                value = here[0][index : index + 1, :]
                zero = jnp.zeros_like(value)
                out_ref[row : row + 1, :] = jnp.concatenate(
                    [jnp.where(side == 0, value, zero), jnp.where(side == 0, zero, value)], axis=1
                )
            else:
                value = here[0][0:1, :] + here[1][0:1, :]
                for t in range(4):
                    here_row = value[:, t % 2 * depth : (t % 2 + 1) * depth]
                    out_ref[row + t : row + t + 1, :] = jnp.where(side == t // 2, here_row, 0.0)

    return kernel_call(
        kernel, (place, *arrays), [out((12 * layers, depth), WIDE)], scalars=1
    )[0]


def vector_outputs(place, total, layers, size):
    depth = total.shape[1]

    def kernel(place_ref, total_ref, qb, vb, ob, ub, db, fg, fs, sg, ss):
        place = place_ref[0]

        def pick(values):
            result = values[0]
            for t in range(1, 4):
                result = jnp.where(place == t, values[t], result)
            return result

        for layer in range(layers):
            at = slice(layer, layer + 1)
            row = lambda i: total_ref[12 * layer + i : 12 * layer + i + 1, :]
            for ref, i in ((fg, 0), (fs, 1), (sg, 2), (ss, 3), (ob, 4), (db, 5)):
                ref[at, :] = row(i)
            for ref, i in ((qb, 6), (vb, 7)):
                value = row(i)
                ref[at, :] = pick([value[:, t * size : (t + 1) * size] for t in range(4)])
            ub[at, :] = pick([row(8 + t) for t in range(4)])

    small, large = out((layers, size), WIDE), out((layers, depth), WIDE)
    return kernel_call(
        kernel, (place, total), [small, small] + [large] * 7, scalars=1
    )


def matrix_outputs(results, size):
    layers = len(results)
    rows, columns = results[0].shape
    count = columns // size

    def kernel(*refs):
        for layer in range(layers):
            value = refs[layer][...].astype(WIDE)
            for i in range(count):
                part = value[:, i * size : (i + 1) * size]
                refs[layers + i][layer] = part.T if i == count - 1 else part

    return kernel_call(
        kernel,
        results,
        [out((layers, rows, size), WIDE)] * (count - 1) + [out((layers, size, rows), WIDE)],
    )


def head_lanes(half):
    lane = lax.broadcasted_iota(jnp.int32, (1, 128), 1)
    return (lane >= half * HEAD_DIM) & (lane < (half + 1) * HEAD_DIM)


def only(mask, value):
    return jnp.where(mask, value, jnp.zeros_like(value))


def fold(value, reduce):
    return reduce(value.reshape(value.shape[0] // 8, 8, value.shape[1]), axis=0)


def attend(query, q_marks, pairs, k_marks, weights):
    rows, width = query.shape
    heads = width // HEAD_DIM
    blocks = len(pairs)
    size = pairs[0].shape[0]

    def kernel(q_ref, qm_ref, *refs):
        kv_refs, km_refs = refs[:blocks], refs[blocks : 2 * blocks]
        w_ref, mixed_ref, norm_ref, part_ref, held = refs[2 * blocks :]
        parts = []
        for pair in range(heads // 2):
            at = slice(pair * 128, pair * 128 + 128)
            to = slice(width + pair * 128, width + pair * 128 + 128)
            q = q_ref[:, at]
            values = [turned(kv[:, to]) for kv in kv_refs]
            for half in range(2):
                q_one = jnp.concatenate([only(head_lanes(half), q), qm_ref[...]], axis=1)
                top = None
                for b in range(blocks):
                    key = jnp.concatenate([kv_refs[b][:, at], km_refs[b][...]], axis=1)
                    scores = dot_nt(key, q_one)
                    held[b] = scores
                    here = fold(scores, jnp.max)
                    top = here if top is None else jnp.maximum(top, here)
                top = jnp.max(top, axis=0, keepdims=True)
                total, bulk = None, None
                for b in range(blocks):
                    grown = jnp.exp(held[b] - top)
                    here = fold(grown, jnp.sum)
                    bulk = here if bulk is None else bulk + here
                    value = values[b][half * HEAD_DIM : (half + 1) * HEAD_DIM]
                    part = dot(value, grown.astype(LOW))
                    total = part if total is None else total + part
                bulk = jnp.sum(bulk, axis=0, keepdims=True)
                parts.append(total * (1.0 / bulk))
                row = pair * 2 + half
                norm_ref[row : row + 1, :] = top + jnp.log(bulk)
        mixed = jnp.concatenate(parts).T.astype(LOW)
        mixed_ref[...] = mixed
        part_ref[...] = dot_nt(mixed, w_ref[:, 3 * width :]).astype(LOW)

    return kernel_call(
        kernel,
        (query, q_marks, *pairs, *k_marks, weights),
        [out((rows, width)), out((8, rows), WIDE), out((rows, weights.shape[0]))],
        [pltpu.VMEM((blocks, size, rows), WIDE)], cost=4.0)


def attend_back(layer, grads, part, arrived, middle, gain, weights, query, q_marks, norms, pairs, k_marks):
    rows, width = query.shape
    depth = middle.shape[1]
    heads = width // HEAD_DIM
    blocks = len(pairs)
    size = pairs[0].shape[0]
    scale = HEAD_DIM ** (-0.5)
    near = blocks // 2

    def kernel(grads_ref, part_ref, arrived_ref, middle_ref, gain_ref, weight_ref, q_ref, qm_ref, norm_ref, *refs):
        kv_refs, km_refs = refs[:blocks], refs[blocks : 2 * blocks]
        gm_ref, low_ref, sums_ref, dq_ref, own_ref, away_ref, p_wide, w_wide, p_all, s_all = refs[2 * blocks :]
        incoming = part_ref[...].astype(WIDE) + arrived_ref[...].astype(WIDE)
        gain_grad, shift_grad, through = norm_backward(
            incoming, middle_ref[...], gain_ref[layer : layer + 1, :]
        )
        g_middle = grads_ref[...].astype(WIDE) + through
        low = g_middle.astype(LOW)
        gm_ref[...] = g_middle
        low_ref[...] = low
        sums_ref[0:1, :] = gain_grad
        sums_ref[1:2, :] = shift_grad
        sums_ref[2:3, :] = jnp.sum(g_middle, axis=0, keepdims=True)
        g_mixed = dot(low, weight_ref[:, 3 * width :]).astype(LOW)
        dqs = []
        for pair in range(heads // 2):
            at = slice(pair * 128, pair * 128 + 128)
            to = slice(width + pair * 128, width + pair * 128 + 128)
            q, g = q_ref[:, at], g_mixed[:, at]
            keys = [turned(kv[:, at]) for kv in kv_refs]
            q_stack, g_stack = [], []
            for half in range(2):
                lanes = head_lanes(half)
                q_stack.append(only(lanes, q))
                g_stack.append(only(lanes, g))
                q_one = jnp.concatenate([q_stack[half], qm_ref[...]], axis=1)
                row = pair * 2 + half
                norm = norm_ref[row : row + 1, :]
                total = None
                for b in range(blocks):
                    key = jnp.concatenate([kv_refs[b][:, at], km_refs[b][...]], axis=1)
                    probs = jnp.exp(dot_nt(key, q_one) - norm)
                    weighed = probs * dot_nt(kv_refs[b][:, to], g_stack[half])
                    here = fold(weighed, jnp.sum)
                    total = here if total is None else total + here
                    p_wide[b] = probs
                    w_wide[b] = weighed
                    p_all[b * size : (b + 1) * size, half * rows : (half + 1) * rows] = probs.astype(LOW)
                total = jnp.sum(total, axis=0, keepdims=True)
                dq = None
                for b in range(blocks):
                    g_scores = (w_wide[b] - p_wide[b] * total).astype(LOW)
                    s_all[b * size : (b + 1) * size, half * rows : (half + 1) * rows] = g_scores
                    part = dot(keys[b][half * HEAD_DIM : (half + 1) * HEAD_DIM], g_scores)
                    dq = part if dq is None else dq + part
                dqs.append(dq)
            dk = dot(s_all[...], jnp.concatenate(q_stack)).astype(LOW)
            dv = dot(p_all[...], jnp.concatenate(g_stack)).astype(LOW)
            own_ref[:, at] = dk[: near * size]
            away_ref[:, at] = dk[near * size :]
            own_ref[:, to] = dv[: near * size]
            away_ref[:, to] = dv[near * size :]
        dq_ref[...] = (jnp.concatenate(dqs).T * scale).astype(LOW)

    half_rows = near * size
    length = blocks * size
    return kernel_call(
        kernel,
        (grads, part, arrived, middle, gain, weights, query, q_marks, norms, *pairs, *k_marks),
        [
            out((rows, depth), WIDE),
            out((rows, depth)),
            out((8, depth), WIDE),
            out((rows, width)),
            out((half_rows, 2 * width)),
            out((half_rows, 2 * width)),
        ],
        [
            pltpu.VMEM((blocks, size, rows), WIDE),
            pltpu.VMEM((blocks, size, rows), WIDE),
            pltpu.VMEM((length, 2 * rows), LOW),
            pltpu.VMEM((length, 2 * rows), LOW),
        ], cost=6.4)


def local(
    hidden_in,
    time_embed,
    segment_ids,
    cotangent,
    query_weight,
    key_weight,
    value_weight,
    output_weight,
    up_weight,
    down_weight,
    query_bias,
    value_bias,
    output_bias,
    up_bias,
    down_bias,
    first_gain,
    first_shift,
    second_gain,
    second_shift,
):
    rows, depth = hidden_in.shape
    layers, _, head_width = query_weight.shape
    hidden_width = up_weight.shape[2]
    place = lax.axis_index("tensor")
    core = (place % 2).reshape(1)
    side = (place // 2).reshape(1)
    place = place.reshape(1)
    ring = Ring()
    last = layers - 1

    near_own = pack_near((query_weight, key_weight, value_weight, output_weight))
    near_peer = swap_core(near_own)
    hidden_other = swap_y(hidden_in)
    pieces = weave_near(core, near_own, near_peer)
    near = [Gather(ring, pieces[0])]
    near[0].step()
    if ring.use:
        (_, query_bias, value_bias, up_bias, segment_ids, cotangent, up_weight, down_weight) = tie(
            near[0].current,
            query_bias,
            value_bias,
            up_bias,
            segment_ids,
            cotangent,
            up_weight,
            down_weight,
        )
    far_own = pack_far(up_weight, down_weight)
    far_pieces = weave_far(core, far_own, [swap_core(piece) for piece in far_own])
    near[0].step()
    near[0].step()
    token = near[0].current if ring.use else None
    near[0].finish()
    far = [Gather(ring, far_pieces[0])]
    far[0].step(token)
    biases = jnp.concatenate([query_bias, value_bias, up_bias], axis=1)
    q_bias, v_bias, u_bias = weave_bias(core, biases, swap_core(biases), head_width)
    q_marks, k_marks = mark_documents(core, segment_ids, rows)
    near.append(Gather(ring, pieces[1]))
    far.append(Gather(ring, far_pieces[1]))

    def exchange(parts):
        first = swap_y(parts[0])
        second = swap_y(tie(parts[1], first)[0])
        first, _ = tie(first, parts[1])
        return [first, second]

    kept = []
    for layer in range(layers):
        w_near = near[layer].whole
        if layer == 0:
            states, firsts, queries, pairs = project_first(
                side, hidden_in, hidden_other, time_embed, first_gain, first_shift, w_near, q_bias, v_bias
            )
            seeds = None
        else:
            made = [
                project(
                    layer,
                    middles[j],
                    branches[j],
                    arrived[j],
                    down_bias,
                    first_gain,
                    first_shift,
                    w_near,
                    q_bias,
                    v_bias,
                )
                for j in range(2)
            ]
            states, firsts, queries, pairs = ([m[i] for m in made] for i in range(4))
        pairs = list(pairs) + [swap_core(pair) for pair in pairs]
        mixeds, norms, parts = [], [], []
        for j in range(2):
            mixed, norm, part = attend(queries[j], q_marks[j], pairs, k_marks, w_near)
            mixeds.append(mixed)
            norms.append(norm)
            parts.append(part)
            far[layer].step(part)
        arrived = exchange(parts)
        if layer == 0:
            token = far[0].current if ring.use else None
            near[1].step(token)
        far[layer].finish()
        w_far = far[layer].whole
        if layer == 0:
            cotangent, _ = tie(cotangent, parts[1])
            seed0, seed1, seed_sums = seed_rows(side, cotangent, swap_y(cotangent), k_marks[:2])
            seeds = [seed0, seed1]
        made = []
        for j in range(2):
            made.append(
                feed(
                    layer,
                    states[j],
                    parts[j],
                    arrived[j],
                    output_bias,
                    second_gain,
                    second_shift,
                    w_far,
                    u_bias,
                    seeds[j] if layer == last else None,
                )
            )
            if layer == 0:
                near[1].step(made[j][4])
        middles, seconds, acts, others, branches = ([m[i] for m in made] for i in range(5))
        kept.append((states, firsts, queries, pairs, norms, mixeds, middles, seconds, acts, others))
        if layer < last:
            arrived = [swap_y(branch) for branch in branches]
            arrived[0], branches[1] = tie(arrived[0], branches[1])
            token = near[1].current if ring.use else None
            near[1].finish()
            far[1].step(token)

    entries = [(12 * last + 5, ("one", 0), (seed_sums,))]
    up_sums = [m[5] for m in made]
    grads, lows, g_pres, parts = seeds, seeds, others, branches
    under_way, results = [], {}

    def advance(main):
        for scatter in under_way:
            main = scatter.step(main)
        return main

    for layer in reversed(range(layers)):
        (states, firsts, queries, pairs, norms, mixeds, middles, seconds, acts, slopes) = kept[layer]
        w_near = near[layer].whole
        w_far = far[layer].whole
        base = 12 * layer
        if layer < last:
            made = []
            for j in range(2):
                if j == 1:
                    arrived[1] = advance(arrived[1])
                made.append(feed_back(
                    layer + 1,
                    g_middles[j],
                    parts[j],
                    arrived[j],
                    above[j],
                    first_gain,
                    slopes[j],
                    w_far,
                ))
            grads, lows, g_pres, parts, sums, up_sums = ([m[i] for m in made] for i in range(6))
            entries += [
                (base + 12, ("own", 0), sums),
                (base + 13, ("own", 1), sums),
                (base + 5, ("own", 2), sums),
            ]
        entries.append((base + 8, ("up", 0), up_sums))
        arrived = exchange(parts)
        if layer < last:
            arrived[0] = advance(arrived[0])
        made = []
        for j in range(2):
            if j == 1:
                feed_away = outer_feed(core, seconds, g_pres, lows, acts, 1)
                got = swap_core(feed_away)
                feed_own = outer_feed(core, seconds, g_pres, lows, acts, 0)
                arrived[1], feed_own, got = tie(arrived[1], feed_own, got)
                arrived[1] = advance(arrived[1])
                under_way.append(Scatter(ring, [feed_own], [got]))
                results[layer, "feed"] = under_way[-1]
            made.append(
                attend_back(
                    layer,
                    grads[j],
                    parts[j],
                    arrived[j],
                    middles[j],
                    second_gain,
                    w_near,
                    queries[j],
                    q_marks[j],
                    norms[j],
                    pairs,
                    k_marks,
                )
            )
            if j == 0:
                g_pres, _ = tie(g_pres, made[0][1])
        g_middles, m_lows, sums, dqs, owns, aways = ([m[i] for m in made] for i in range(6))
        entries += [
            (base + 2, ("own", 0), sums),
            (base + 3, ("own", 1), sums),
            (base + 4, ("own", 2), sums),
        ]
        aways = [swap_core(away) for away in aways]
        aways[1] = advance(aways[1])
        g_qkv, part0, part1, sums = project_back(side, dqs, owns, aways, w_near, layer == 0)
        entries += [(base + 6, ("half", 0), (sums,)), (base + 7, ("half", 1), (sums,))]
        if layer > 0:
            parts = [part0, part1]
            arrived = exchange(parts)
            above = states
        else:
            arrived = swap_y(part0)
        near_away = outer_heads(core, firsts, g_qkv, m_lows, mixeds, 1)
        near_got = swap_core(near_away)
        near_own = outer_heads(core, firsts, g_qkv, m_lows, mixeds, 0)
        if layer == last:
            arrived[0], near_own, near_got = tie(arrived[0], near_own, near_got)
            arrived[0] = advance(arrived[0])
        under_way.append(Scatter(ring, [near_own], [near_got]))
        results[layer, "near"] = under_way[-1]
        if layer == last:
            acts_after, _ = tie(acts, near_own)
            away_rows, here_rows = last_branch(side, acts_after, w_far)
            crossed = swap_y(away_rows)
            denoised = last_rows(side, middles, here_rows, crossed, down_bias, layer)
    input_grad, sums = first_rows(side, part1, arrived, states, g_middles, first_gain)
    entries += [(0, ("one", 0), (sums,)), (1, ("one", 1), (sums,))]
    total = vector_rows(place, entries, layers, depth)
    results[0, "near"].step()
    if ring.use:
        for move_by in exchanges(ring.count):
            total = total + move_by(total)
            total = advance(total)
    else:
        total = lax.psum(total, ("fsdp", "tensor"))
    vectors = vector_outputs(place, total, layers, head_width)
    up_out, down_out = matrix_outputs(
        [results[layer, "feed"].finish() for layer in range(layers)], hidden_width
    )
    heads = matrix_outputs([results[layer, "near"].finish() for layer in range(layers)], head_width)
    return (denoised, input_grad, *heads, up_out, down_out, *vectors)


def solution(mesh):
    rows = P(("fsdp", "tensor"), None)
    inner = P(None, "fsdp", "tensor")
    outer = P(None, "tensor", "fsdp")
    cut = P(None, "tensor")
    in_specs = (
        rows,
        P("fsdp", None),
        P("fsdp", None),
        rows,
        inner,
        inner,
        inner,
        outer,
        inner,
        outer,
        cut,
        cut,
        P(),
        cut,
        P(),
        P(),
        P(),
        P(),
        P(),
    )
    out_specs = (
        rows,
        rows,
        inner,
        inner,
        inner,
        outer,
        inner,
        outer,
        cut,
        cut,
        P(),
        cut,
        P(),
        P(),
        P(),
        P(),
        P(),
    )
    return jax.shard_map(local, mesh=mesh, in_specs=in_specs, out_specs=out_specs, check_vma=False)
```

```python
import functools

import jax
import jax.numpy as jnp
from jax import lax
from jax.experimental import pallas as pl
from jax.experimental.pallas import tpu as pltpu
from jax.sharding import PartitionSpec as P

HEAD_DIM = 64
EPSILON = 1e-05
LOW = jnp.bfloat16
WIDE = jnp.float32
ROOT = 0.7978845608028654
CUBE = 0.044715

SWAP_CORE = [(0, 1), (1, 0), (2, 3), (3, 2)]
SWAP_Y = [(0, 2), (2, 0), (1, 3), (3, 1)]


def swap_core(value):
    return lax.ppermute(value, "tensor", SWAP_CORE)


def swap_y(value):
    return lax.ppermute(value, "tensor", SWAP_Y)


def dot(a, b):
    return jnp.dot(a, b, preferred_element_type=WIDE)


def dot_nt(a, b):
    return lax.dot_general(a, b, (((1,), (1,)), ((), ())), preferred_element_type=WIDE)


def dot_tn(a, b):
    return lax.dot_general(a, b, (((0,), (0,)), ((), ())), preferred_element_type=WIDE)


def tie(*values):
    return lax.optimization_barrier(values)


def ring_order(count):
    return list(range(0, count, 2)) + list(range(count - 1, 0, -2))


class Ring:
    def __init__(self):
        self.count = lax.axis_size("fsdp")
        self.use = self.count == 8
        self.core = lax.axis_index("tensor") % 2
        if self.use:
            here = lax.axis_index("fsdp")
            self.place = jnp.where(here % 2 == 0, here // 2, self.count - 1 - here // 2)
            self.way = 1 - 2 * self.core
            self.far = self.count // 2
            order = ring_order(self.count)
            self.pairs = [
                [(order[i], order[(i + way) % self.count]) for i in range(self.count)]
                for way in (1, -1)
            ]
            self.split = [
                (here * 4 + t, there * 4 + t)
                for t in range(4)
                for here, there in self.pairs[t % 2]
            ]
            self.blocks = jnp.stack([self.block_at(step) for step in range(self.count)])

    def split_send(self, value):
        return lax.ppermute(value, ("fsdp", "tensor"), self.split)

    def send_both(self, ahead, behind):
        return lax.ppermute(ahead, "fsdp", self.pairs[0]), lax.ppermute(behind, "fsdp", self.pairs[1])

    def block_at(self, steps):
        place = (self.place + steps + 2 * self.count) % self.count
        return jnp.where(place < self.count // 2, 2 * place, 2 * (self.count - 1 - place) + 1)


class Gather:
    def __init__(self, ring, piece):
        self.ring = ring
        self.rows, self.columns = piece.shape
        self.todo = []
        self.done = 0
        self.current = piece
        if ring.use:
            self.whole = jnp.zeros((ring.count * self.rows, self.columns), piece.dtype)
            self.put(piece, lax.axis_index("fsdp"))
        else:
            self.whole = lax.all_gather(piece, "fsdp", axis=0, tiled=True)

    def put(self, value, block, offset=0):
        start = block * self.rows + offset
        self.whole = lax.dynamic_update_slice(self.whole, value, (start, 0))

    def flush(self):
        ring = self.ring
        half = self.rows // 2
        for step, value in self.todo:
            if step < ring.far:
                self.put(value, ring.block_at(-ring.way * step))
                self.put(swap_core(value), ring.block_at(ring.way * step))
            else:
                block = ring.block_at(step)
                self.put(value, block, ring.core * half)
                self.put(swap_core(value), block, (1 - ring.core) * half)
        self.todo = []

    def step(self, token=None):
        ring = self.ring
        if not ring.use or self.done == ring.far:
            return
        self.flush()
        self.done += 1
        current = self.current
        if token is not None:
            current, _ = tie(current, token)
        if self.done == ring.far:
            half = self.rows // 2
            current = lax.dynamic_slice(current, (ring.core * half, 0), (half, self.columns))
        self.current = ring.split_send(current)
        self.todo.append((self.done, self.current))

    def finish(self):
        if self.ring.use:
            while self.done < self.ring.far:
                self.step()
            self.flush()


class Scatter:
    def __init__(self, ring, owns, gots):
        self.ring = ring
        self.owns, self.gots = owns, gots
        self.done = 0
        self.made = owns
        if ring.use:
            self.rows = owns[0].shape[0] // ring.count
        else:
            total = jnp.concatenate(
                [own.astype(WIDE) + got.astype(WIDE) for own, got in zip(owns, gots)], axis=1
            )
            self.result = lax.psum_scatter(total, "fsdp", scatter_dimension=0, tiled=True)

    def step(self, main=None, token=None):
        ring = self.ring
        if not ring.use or self.done > ring.far:
            return main
        moving = None
        if self.done:
            moving = self.flying
            if main is not None:
                main, *moving = tie(main, *moving)
        if self.done == ring.far:
            self.done += 1
            self.result = passing(ring.blocks, self.owns, self.gots, 0, ring.count, moving)[0]
            return main
        owns = self.owns
        if main is None and token is not None:
            owns, _ = tie(owns, token)
        made = passing(ring.blocks, owns, self.gots, ring.far - self.done, ring.count, moving)
        if main is not None:
            main, *made = tie(main, *made)
        self.made = made
        self.flying = ring.send_both(*made)
        self.done += 1
        return main

    def finish(self):
        if self.ring.use:
            while self.done <= self.ring.far:
                self.step()
        return self.result


def exchanges(count):
    moves = [swap_core, swap_y]
    bit = 1
    while bit < count:
        pairs = [(i, i ^ bit) for i in range(count)]
        moves.append(lambda value, pairs=pairs: lax.ppermute(value, "fsdp", pairs))
        bit *= 2
    return moves


NEVER = -1e30


def out(shape, dtype=LOW):
    return jax.ShapeDtypeStruct(shape, dtype)


def kernel_call(kernel, operands, outs, scratch=(), scalars=0, cost=1.0, room=8, apart=0):
    inside = pl.BlockSpec(memory_space=pltpu.VMEM)
    word = pl.BlockSpec(memory_space=pltpu.SMEM)
    return pl.pallas_call(
        kernel,
        in_specs=[word] * scalars
        + [inside] * (len(operands) - scalars - apart)
        + [pl.BlockSpec(memory_space=pl.ANY)] * apart,
        out_specs=[inside] * len(outs),
        out_shape=outs,
        scratch_shapes=scratch,
        compiler_params=pltpu.CompilerParams(vmem_limit_bytes=room << 20),
        cost_estimate=pl.CostEstimate(
            flops=int(cost * 1e9), bytes_accessed=1024, transcendentals=0
        ),
    )(*operands)


def start_copies(pairs, sems):
    copies = [
        pltpu.make_async_copy(source, target, sems.at[index])
        for index, (source, target) in enumerate(pairs)
    ]
    for copy in copies:
        copy.start()
    return copies


def norm_parts(rows):
    center = rows - jnp.mean(rows, axis=1, keepdims=True)
    factor = lax.rsqrt(jnp.mean(center * center, axis=1, keepdims=True) + EPSILON)
    return center * factor, factor


def norm_backward(grad, rows, gain):
    normed, factor = norm_parts(rows)
    scaled = grad * gain
    through = factor * (
        scaled
        - jnp.mean(scaled, axis=1, keepdims=True)
        - normed * jnp.mean(scaled * normed, axis=1, keepdims=True)
    )
    gain_grad = jnp.sum(grad * normed, axis=0, keepdims=True)
    return gain_grad, jnp.sum(grad, axis=0, keepdims=True), through


def gelu_both(pre):
    inner = jnp.tanh(ROOT * (pre + CUBE * pre * pre * pre))
    slope = 0.5 * (1.0 + inner) + 0.5 * pre * (1.0 - inner * inner) * (
        ROOT * (1.0 + 3.0 * CUBE * pre * pre)
    )
    return 0.5 * pre * (1.0 + inner), slope


def project(layer, base, part, arrived, bias, gain, shift, weights, q_bias, v_bias):
    rows, depth = base.shape
    width = q_bias.shape[1]
    scale = HEAD_DIM ** (-0.5)
    at = slice(layer, layer + 1)

    def kernel(base_ref, part_ref, arrived_ref, bias_ref, gain_ref, shift_ref, qb_ref, vb_ref, w_far,
               state_ref, first_ref, q_ref, kv_ref, w_ref, sems):
        (copy,) = start_copies([(w_far.at[:, : 3 * width], w_ref)], sems)
        state = base_ref[...] + (part_ref[...].astype(WIDE) + arrived_ref[...].astype(WIDE))
        state += bias_ref[layer - 1 : layer, :]
        first = (norm_parts(state)[0] * gain_ref[at, :] + shift_ref[at, :]).astype(LOW)
        state_ref[...] = state
        first_ref[...] = first
        copy.wait()
        query = (dot(first, w_ref[:, :width]) + qb_ref[at, :]).astype(LOW)
        q_ref[...] = query * jnp.asarray(scale, LOW)
        kv_ref[:, :width] = dot(first, w_ref[:, width : 2 * width]).astype(LOW)
        kv_ref[:, width:] = (dot(first, w_ref[:, 2 * width : 3 * width]) + vb_ref[at, :]).astype(LOW)

    return kernel_call(
        kernel,
        (base, part, arrived, bias, gain, shift, q_bias, v_bias, weights),
        [
            out((rows, depth), WIDE),
            out((rows, depth)),
            out((rows, width)),
            out((rows, 2 * width)),
        ], scratch=[pltpu.VMEM((depth, 3 * width), LOW), pltpu.SemaphoreType.DMA((1,))],
        cost=1.2,
        apart=1,
    )


def feed(layer, state, part, arrived, out_bias, gain, shift, weights, up_bias, lows=None):
    rows, depth = state.shape
    hidden = up_bias.shape[1]
    back = lows is not None
    half = hidden // 2
    tile = 384
    row = slice(layer, layer + 1)

    def kernel(*refs):
        state_ref, part_ref, arrived_ref, ob_ref, gain_ref, shift_ref, w_ref, ub_ref = refs[:8]
        refs = refs[8:]
        middle = (
            state_ref[...] + (part_ref[...].astype(WIDE) + arrived_ref[...].astype(WIDE)) + ob_ref[row, :]
        )
        second = (norm_parts(middle)[0] * gain_ref[row, :] + shift_ref[row, :]).astype(LOW)
        if back:
            lows_ref, middle_ref, second_ref, act_ref, other_ref, branch_ref, ubg_ref = refs
            low = lows_ref[...]
        else:
            middle_ref, second_ref, act_ref, other_ref, branch_ref = refs
        middle_ref[...] = middle
        second_ref[...] = second
        total = None
        for start in range(0, hidden, tile):
            at = slice(start, start + tile)
            inside = start + start // half * half
            up = w_ref[:, inside : inside + tile]
            down = w_ref[:, half + inside : half + inside + tile]
            act, slope = gelu_both(dot(second, up) + ub_ref[row, at])
            act = act.astype(LOW)
            act_ref[:, at] = act
            if back:
                other = (dot(low, down) * slope).astype(LOW)
                ubg_ref[0:1, at] = jnp.sum(other.astype(WIDE), axis=0, keepdims=True)
                here = dot_nt(other, up)
            else:
                other = slope.astype(LOW)
                here = dot_nt(act, down)
            other_ref[:, at] = other
            total = here if total is None else total + here
        branch_ref[...] = total.astype(LOW)

    operands = [state, part, arrived, out_bias, gain, shift, weights, up_bias]
    outs = [
        out((rows, depth), WIDE),
        out((rows, depth)),
        out((rows, hidden)),
        out((rows, hidden)),
        out((rows, depth)),
    ]
    if back:
        operands.append(lows)
        outs.append(out((8, hidden), WIDE))
    return kernel_call(kernel, operands, outs, cost=4.0)


def feed_back(layer, g_middle, part, arrived, state, gain, slopes, weights):
    rows, depth = state.shape
    hidden = slopes.shape[1]
    half = hidden // 2
    tile = 384

    def kernel(gm_ref, part_ref, arrived_ref, state_ref, gain_ref, slope_ref, w_ref,
               grad_ref, low_ref, gpre_ref, branch_ref, sums_ref, ubg_ref):
        incoming = part_ref[...].astype(WIDE) + arrived_ref[...].astype(WIDE)
        gain_grad, shift_grad, through = norm_backward(incoming, state_ref[...], gain_ref[layer : layer + 1, :])
        grad = gm_ref[...] + through
        low = grad.astype(LOW)
        grad_ref[...] = grad
        low_ref[...] = low
        sums_ref[0:1, :] = gain_grad
        sums_ref[1:2, :] = shift_grad
        sums_ref[2:3, :] = jnp.sum(grad, axis=0, keepdims=True)
        total = None
        for start in range(0, hidden, tile):
            at = slice(start, start + tile)
            inside = start + start // half * half
            up = w_ref[:, inside : inside + tile]
            down = w_ref[:, half + inside : half + inside + tile]
            gpre = (dot(low, down) * slope_ref[:, at].astype(WIDE)).astype(LOW)
            gpre_ref[:, at] = gpre
            ubg_ref[0:1, at] = jnp.sum(gpre.astype(WIDE), axis=0, keepdims=True)
            here = dot_nt(gpre, up)
            total = here if total is None else total + here
        branch_ref[...] = total.astype(LOW)

    return kernel_call(
        kernel,
        (g_middle, part, arrived, state, gain, slopes, weights),
        [
            out((rows, depth), WIDE),
            out((rows, depth)),
            out((rows, hidden)),
            out((rows, depth)),
            out((8, depth), WIDE),
            out((8, hidden), WIDE),
        ], cost=3.8)

def turned(value):
    return value.astype(WIDE).T.astype(LOW)


def outer_feed(core, seconds, g_pres, lows, acts):
    depth = seconds[0].shape[1]
    size = acts[0].shape[1] // 2

    def kernel(core_ref, s0, s1, g0, g1, l0, l1, a0, a1, *out_refs):
        for index, (left_refs, right_refs) in enumerate((((s0, s1), (g0, g1)), ((l0, l1), (a0, a1)))):
            left = jnp.concatenate([turned(ref[...]) for ref in left_refs], axis=1)
            for which, out_ref in ((1, out_refs[0]), (0, out_refs[1])):
                start = jnp.where(core_ref[0] == which, 0, size)
                for at in range(0, size, 384):
                    columns = pl.ds(pl.multiple_of(start + at, 128), 384)
                    right = jnp.concatenate([ref[:, columns] for ref in right_refs])
                    base = index * size + at
                    out_ref[:, base : base + 384] = dot(left, right).astype(LOW)

    return kernel_call(
        kernel,
        (core, *seconds, *g_pres, *lows, *acts),
        [out((depth, 2 * size))] * 2,
        scalars=1,
        cost=3.4,
    )


def outer_heads(core, firsts, g_qkv, m_lows, mixeds, which):
    depth = firsts[0].shape[1]
    width = mixeds[0].shape[1]
    size = width // 2

    def kernel(core_ref, f0, f1, g_ref, l0, l1, m0, m1, out_ref):
        low = core_ref[0] == which

        def pick(value):
            return jnp.where(low, value[:, :size], value[:, size:])

        first = jnp.concatenate([turned(f0[...]), turned(f1[...])], axis=1)
        g = g_ref[...]
        right = jnp.concatenate(
            [pick(g[:, i * width : (i + 1) * width]) for i in range(3)], axis=1
        )
        m_low = jnp.concatenate([turned(l0[...]), turned(l1[...])], axis=1)
        mixed = jnp.concatenate([pick(m0[...]), pick(m1[...])])
        out_ref[...] = jnp.concatenate([dot(first, right), dot(m_low, mixed)], axis=1).astype(LOW)

    return kernel_call(
        kernel, (core, *firsts, g_qkv, *m_lows, *mixeds), [out((depth, 4 * size))], scalars=1, cost=1.8)[0]


def passing(blocks, owns, gots, step, count, moving):
    parts = len(owns)
    rows = owns[0].shape[0] // count
    half = rows // 2
    columns = sum(own.shape[1] for own in owns)
    first = moving is None
    last = step == 0
    partial_in = not first and moving[0].shape[0] == half

    def kernel(blocks_ref, *refs):
        if first:
            moving_refs, refs = (), refs
        else:
            moving_refs, refs = refs[:2], refs[2:]
        own_refs, got_refs = refs[:parts], refs[parts : 2 * parts]
        out_refs, held, sems = refs[2 * parts : -1 - 2 * parts], refs[-1 - 2 * parts : -1], refs[-1]
        if first:
            wanted = [(step, 0, half), (step, half, half)]
        elif last:
            wanted = [(0, 0, rows)]
        else:
            wanted = [(step, 0, rows), ((count - step) % count, 0, rows)]
        pairs = []
        for index, (block, offset, size) in enumerate(wanted):
            start = pl.multiple_of(blocks_ref[block] * rows + offset, 16)
            for ref, target in zip((*own_refs, *got_refs), held):
                pairs.append((ref.at[pl.ds(start, size), :], target.at[index, pl.ds(0, size), :]))
        copies = start_copies(pairs, sems)
        for copy in copies:
            copy.wait()

        def here(index, size=rows):
            return jnp.concatenate(
                [
                    held[k][index, :size].astype(WIDE) + held[parts + k][index, :size].astype(WIDE)
                    for k in range(parts)
                ],
                axis=1,
            )

        if first:
            out_refs[0][...] = here(0, half).astype(LOW)
            out_refs[1][...] = here(1, half).astype(LOW)
        elif last:
            total = here(0) + moving_refs[0][...].astype(WIDE) + moving_refs[1][...].astype(WIDE)
            out_refs[0][...] = total
        else:
            ahead, behind = here(0), here(1)
            a, b = moving_refs[0][...].astype(WIDE), moving_refs[1][...].astype(WIDE)
            if partial_in:
                out_refs[0][:half, :] = (ahead[:half] + a).astype(LOW)
                out_refs[0][half:, :] = ahead[half:].astype(LOW)
                out_refs[1][:half, :] = behind[:half].astype(LOW)
                out_refs[1][half:, :] = (behind[half:] + b).astype(LOW)
            else:
                out_refs[0][...] = (ahead + a).astype(LOW)
                out_refs[1][...] = (behind + b).astype(LOW)

    if last:
        outs = [out((rows, columns), WIDE)]
    else:
        outs = [out((half if first else rows, columns))] * 2
    operands = (blocks, *(() if first else moving), *owns, *gots)
    return kernel_call(
        kernel,
        operands,
        outs,
        [pltpu.VMEM((2, rows, own.shape[1]), LOW) for own in (*owns, *gots)]
        + [pltpu.SemaphoreType.DMA((4 * parts,))],
        scalars=1,
        cost=0.8,
        apart=2 * parts,
    )


def pack_near(weights):
    layers, rows, size = weights[0].shape

    def kernel(*refs):
        out_ref, held, sems = refs[4], refs[5:9], refs[9]
        copies = [
            pltpu.make_async_copy(refs[i], held[i], sems.at[i]) for i in range(4)
        ]
        for copy in copies:
            copy.start()
        for copy in copies:
            copy.wait()
        q_ref, k_ref, v_ref, o_ref = held
        for layer in range(layers):
            out_ref[layer] = jnp.concatenate(
                [q_ref[layer], k_ref[layer], v_ref[layer], turned(o_ref[layer])], axis=1
            )

    return pl.pallas_call(
        kernel,
        in_specs=[pl.BlockSpec(memory_space=pl.ANY)] * 4,
        out_specs=pl.BlockSpec(memory_space=pltpu.VMEM),
        out_shape=out((layers, rows, 4 * size)),
        scratch_shapes=[pltpu.VMEM(w.shape, LOW) for w in weights]
        + [pltpu.SemaphoreType.DMA((4,))],
        compiler_params=pltpu.CompilerParams(vmem_limit_bytes=8 << 20),
        cost_estimate=pl.CostEstimate(flops=1000, bytes_accessed=1024, transcendentals=0),
    )(*weights)


def weave_near(core, own, peer):
    layers, rows, columns = own.shape
    size = columns // 4

    def kernel(core_ref, own_ref, peer_ref, *out_refs):
        first = core_ref[0] == 0
        for layer, out_ref in enumerate(out_refs):
            a, b = own_ref[layer], peer_ref[layer]
            low, high = jnp.where(first, a, b), jnp.where(first, b, a)
            parts = []
            for i in range(4):
                parts += [low[:, i * size : (i + 1) * size], high[:, i * size : (i + 1) * size]]
            out_ref[...] = jnp.concatenate(parts, axis=1)

    return kernel_call(
        kernel, (core, own, peer), [out((rows, 2 * columns))] * layers, scalars=1
    )


def weave_far(core, own, peer):
    layers, rows, columns = own[0].shape

    def kernel(core_ref, u_own, d_own, u_peer, d_peer, *out_refs):
        first = core_ref[0] == 0
        for layer, out_ref in enumerate(out_refs):
            for index, (own_ref, peer_ref) in enumerate(((u_own, u_peer), (d_own, d_peer))):
                a, b = own_ref[layer], peer_ref[layer]
                low, high = index * columns, (2 + index) * columns
                out_ref[:, low : low + columns] = jnp.where(first, a, b)
                out_ref[:, high : high + columns] = jnp.where(first, b, a)

    return kernel_call(
        kernel, (core, *own, *peer), [out((rows, 4 * columns))] * layers, scalars=1
    )


def weave_bias(core, own, peer, size):
    layers = own.shape[0]
    rest = own.shape[1] - 2 * size

    def kernel(core_ref, own_ref, peer_ref, q_ref, v_ref, u_ref):
        first = core_ref[0] == 0
        a, b = own_ref[...], peer_ref[...]
        low, high = jnp.where(first, a, b), jnp.where(first, b, a)
        q_ref[...] = jnp.concatenate([low[:, :size], high[:, :size]], axis=1)
        v_ref[...] = jnp.concatenate([low[:, size : 2 * size], high[:, size : 2 * size]], axis=1)
        u_ref[...] = jnp.concatenate([low[:, 2 * size :], high[:, 2 * size :]], axis=1)

    return kernel_call(
        kernel,
        (core, own, peer),
        [
            out((layers, 2 * size), WIDE),
            out((layers, 2 * size), WIDE),
            out((layers, 2 * rest), WIDE),
        ],
        scalars=1,
    )


def mark_documents(core, segments, rows):
    def kernel(core_ref, segment_ref, *refs):
        core = core_ref[0]
        blocks = [core, 2 + core, 1 - core, 3 - core]
        lane = lax.broadcasted_iota(jnp.int32, (128, rows), 0)
        for index, block in enumerate(blocks):
            at = pl.ds(pl.multiple_of(block * rows, 128), rows)
            mark = jnp.where(lane == segment_ref[:, at] + 1, 1.0, 0.0).T
            refs[2 + index][...] = mark.astype(LOW)
            if index < 2:
                real = lax.broadcasted_iota(jnp.int32, (rows, 128), 1) < 9
                refs[index][...] = jnp.where(real & (mark == 0.0), NEVER, 0.0).astype(LOW)

    made = kernel_call(kernel, (core, segments), [out((rows, 128))] * 6, scalars=1)
    return made[:2], made[2:]


def seed_rows(side, own, other, marks):
    rows, depth = own.shape

    def kernel(side_ref, own_ref, other_ref, m0, m1, low0, low1, sums_ref):
        total = None
        for j, (mark, low) in enumerate(((m0, low0), (m1, low1))):
            mine = side_ref[0] == j
            value = jnp.where(mine, own_ref[...], other_ref[...])
            value = jnp.where(mark[:, 0:1] > 0, jnp.zeros_like(value), value)
            low[...] = value
            here = jnp.sum(value.astype(WIDE), axis=0, keepdims=True)
            here = jnp.where(mine, here, 0.0)
            total = here if total is None else total + here
        sums_ref[0:1, :] = total

    return kernel_call(
        kernel,
        (side, own, other, *marks),
        [out((rows, depth)), out((rows, depth)), out((8, depth), WIDE)],
        scalars=1,
    )


def project_first(side, own, other, embed, gain, shift, weights, q_bias, v_bias):
    rows, depth = own.shape
    width = q_bias.shape[1]
    scale = HEAD_DIM ** (-0.5)

    def kernel(side_ref, own_ref, other_ref, embed_ref, gain_ref, shift_ref, qb_ref, vb_ref, w_far, *refs):
        w_ref, sems = refs[8:]
        (copy,) = start_copies([(w_far.at[:, : 3 * width], w_ref)], sems)
        firsts = []
        for j in range(2):
            rows_in = jnp.where(side_ref[0] == j, own_ref[...], other_ref[...])
            state = rows_in.astype(WIDE) + embed_ref[...].astype(WIDE)
            refs[j][...] = state
            first = (norm_parts(state)[0] * gain_ref[0:1, :] + shift_ref[0:1, :]).astype(LOW)
            refs[2 + j][...] = first
            firsts.append(first)
        first = jnp.concatenate(firsts)
        copy.wait()
        query = (dot(first, w_ref[:, :width]) + qb_ref[0:1, :]).astype(LOW)
        query = query * jnp.asarray(scale, LOW)
        key = dot(first, w_ref[:, width : 2 * width]).astype(LOW)
        value = (dot(first, w_ref[:, 2 * width : 3 * width]) + vb_ref[0:1, :]).astype(LOW)
        for j in range(2):
            at = slice(j * rows, (j + 1) * rows)
            refs[4 + j][...] = query[at]
            refs[6 + j][:, :width] = key[at]
            refs[6 + j][:, width:] = value[at]

    made = kernel_call(
        kernel,
        (side, own, other, embed, gain, shift, q_bias, v_bias, weights),
        [out((rows, depth), WIDE)] * 2
        + [out((rows, depth))] * 2
        + [out((rows, width))] * 2
        + [out((rows, 2 * width))] * 2,
        scalars=1, scratch=[pltpu.VMEM((depth, 3 * width), LOW), pltpu.SemaphoreType.DMA((1,))],
        cost=1.8,
        apart=1,
    )
    return [made[2 * i : 2 * i + 2] for i in range(4)]


def last_branch(side, acts, weights):
    rows, hidden = acts[0].shape
    depth = weights.shape[0]
    size = hidden // 2

    def kernel(side_ref, a0, a1, w_far, away_ref, here_ref, w_ref, sems):
        copies = start_copies(
            [(w_far.at[:, (2 * i + 1) * size : (2 * i + 2) * size], w_ref.at[i]) for i in range(2)], sems
        )
        for copy in copies:
            copy.wait()
        for flip, ref in ((1, away_ref), (0, here_ref)):
            act = jnp.where(side_ref[0] == flip, a0[...], a1[...])
            total = dot_nt(act[:, :size], w_ref[0])
            total += dot_nt(act[:, size:], w_ref[1])
            ref[...] = total.astype(ref.dtype)

    return kernel_call(
        kernel,
        (side, *acts, weights),
        [out((rows, depth)), out((rows, depth), WIDE)],
        scalars=1, scratch=[pltpu.VMEM((2, depth, size), LOW), pltpu.SemaphoreType.DMA((2,))],
        cost=1.4,
        apart=1,
    )


def last_rows(side, middles, here, crossed, bias, layer):
    rows, depth = here.shape

    def kernel(side_ref, m0, m1, here_ref, crossed_ref, bias_ref, out_ref):
        middle = jnp.where(side_ref[0] == 0, m0[...], m1[...])
        total = here_ref[...] + crossed_ref[...].astype(WIDE)
        out_ref[...] = (middle + total + bias_ref[layer : layer + 1, :]).astype(LOW)

    return kernel_call(
        kernel, (side, *middles, here, crossed, bias), [out((rows, depth))], scalars=1
    )[0]


def project_back(side, dqs, owns, aways, weights, last):
    rows, width = dqs[0].shape
    depth = weights.shape[0]

    def kernel(side_ref, dq0, dq1, own0, own1, away0, away1, w_far, g_ref, part0, part1, sums_ref, w_ref, sems):
        (copy,) = start_copies([(w_far.at[:, : 3 * width], w_ref)], sems)
        pair = (
            own0[...].astype(WIDE)
            + own1[...].astype(WIDE)
            + (away0[...].astype(WIDE) + away1[...].astype(WIDE))
        ).astype(LOW)
        g_ref[:rows, :width] = dq0[...]
        g_ref[rows:, :width] = dq1[...]
        g_ref[:, width:] = pair
        g = g_ref[...]
        copy.wait()
        total = dot_nt(g, w_ref[...])
        low, high = total[:rows], total[rows:]
        if last:
            part0[...] = jnp.where(side_ref[0] == 0, high, low).astype(LOW)
            part1[...] = jnp.where(side_ref[0] == 0, low, high)
        else:
            part0[...] = low.astype(LOW)
            part1[...] = high.astype(LOW)
        sums_ref[0:1, :] = jnp.sum(g[:, :width].astype(WIDE), axis=0, keepdims=True)
        sums_ref[1:2, :] = jnp.sum(pair[:, width:].astype(WIDE), axis=0, keepdims=True)

    return kernel_call(
        kernel,
        (side, *dqs, *owns, *aways, weights),
        [
            out((2 * rows, 3 * width)),
            out((rows, depth)),
            out((rows, depth), WIDE if last else LOW),
            out((8, width), WIDE),
        ],
        scalars=1, scratch=[pltpu.VMEM((depth, 3 * width), LOW), pltpu.SemaphoreType.DMA((1,))],
        cost=1.6,
        apart=1,
    )


def first_rows(side, here, arrived, states, g_middles, gain):
    rows, depth = here.shape

    def kernel(side_ref, here_ref, arrived_ref, s0, s1, g0, g1, gain_ref, out_ref, sums_ref):
        low = side_ref[0] == 0
        incoming = here_ref[...] + arrived_ref[...].astype(WIDE)
        state = jnp.where(low, s0[...], s1[...])
        gain_grad, shift_grad, through = norm_backward(incoming, state, gain_ref[0:1, :])
        out_ref[...] = jnp.where(low, g0[...], g1[...]) + through
        sums_ref[0:1, :] = gain_grad
        sums_ref[1:2, :] = shift_grad

    return kernel_call(
        kernel,
        (side, here, arrived, *states, *g_middles, gain),
        [out((rows, depth), WIDE), out((8, depth), WIDE)],
        scalars=1,
    )


def vector_rows(place, entries, layers, depth):
    arrays = [array for _, _, group in entries for array in group]

    def kernel(place_ref, *refs):
        out_ref = refs[-1]
        place = place_ref[0]
        side = place // 2
        at = 0
        for row, (take, index), group in entries:
            here = refs[at : at + len(group)]
            at += len(group)
            if take == "own":
                value = jnp.where(side == 0, here[0][index : index + 1, :], here[1][index : index + 1, :])
                out_ref[row : row + 1, :] = value
            elif take == "one":
                out_ref[row : row + 1, :] = here[0][index : index + 1, :]
            elif take == "half":
                value = here[0][index : index + 1, :]
                zero = jnp.zeros_like(value)
                out_ref[row : row + 1, :] = jnp.concatenate(
                    [jnp.where(side == 0, value, zero), jnp.where(side == 0, zero, value)], axis=1
                )
            else:
                value = here[0][0:1, :] + here[1][0:1, :]
                for t in range(4):
                    here_row = value[:, t % 2 * depth : (t % 2 + 1) * depth]
                    out_ref[row + t : row + t + 1, :] = jnp.where(side == t // 2, here_row, 0.0)

    return kernel_call(
        kernel, (place, *arrays), [out((12 * layers, depth), WIDE)], scalars=1
    )[0]


def vector_outputs(place, total, layers, size):
    depth = total.shape[1]

    def kernel(place_ref, total_ref, qb, vb, ob, ub, db, fg, fs, sg, ss):
        place = place_ref[0]

        def pick(values):
            result = values[0]
            for t in range(1, 4):
                result = jnp.where(place == t, values[t], result)
            return result

        for layer in range(layers):
            at = slice(layer, layer + 1)
            row = lambda i: total_ref[12 * layer + i : 12 * layer + i + 1, :]
            for ref, i in ((fg, 0), (fs, 1), (sg, 2), (ss, 3), (ob, 4), (db, 5)):
                ref[at, :] = row(i)
            for ref, i in ((qb, 6), (vb, 7)):
                value = row(i)
                ref[at, :] = pick([value[:, t * size : (t + 1) * size] for t in range(4)])
            ub[at, :] = pick([row(8 + t) for t in range(4)])

    small, large = out((layers, size), WIDE), out((layers, depth), WIDE)
    return kernel_call(
        kernel, (place, total), [small, small] + [large] * 7, scalars=1
    )


def matrix_outputs(results, size, turn):
    layers = len(results)
    rows, columns = results[0].shape
    count = columns // size

    def kernel(*refs):
        for layer in range(layers):
            value = refs[layer][...].astype(WIDE)
            for i in range(count):
                part = value[:, i * size : (i + 1) * size]
                refs[layers + i][layer] = part.T if turn and i == count - 1 else part

    return kernel_call(
        kernel,
        results,
        [out((layers, rows, size), WIDE)] * (count - 1)
        + [out((layers, size, rows) if turn else (layers, rows, size), WIDE)],
    )


def head_lanes(half):
    lane = lax.broadcasted_iota(jnp.int32, (1, 128), 1)
    return (lane >= half * HEAD_DIM) & (lane < (half + 1) * HEAD_DIM)


def only(mask, value):
    return jnp.where(mask, value, jnp.zeros_like(value))


def fold(value, reduce):
    return reduce(value.reshape(value.shape[0] // 8, 8, value.shape[1]), axis=0)


def attend(query, q_marks, pairs, k_marks, weights):
    rows, width = query.shape
    heads = width // HEAD_DIM
    blocks = len(pairs)
    size = pairs[0].shape[0]

    def kernel(q_ref, qm_ref, *refs):
        kv_refs, km_refs = refs[:blocks], refs[blocks : 2 * blocks]
        w_far, mixed_ref, norm_ref, part_ref, held, w_ref, sems = refs[2 * blocks :]
        (copy,) = start_copies([(w_far.at[:, 3 * width :], w_ref)], sems)
        parts = []
        for pair in range(heads // 2):
            at = slice(pair * 128, pair * 128 + 128)
            to = slice(width + pair * 128, width + pair * 128 + 128)
            q = q_ref[:, at]
            values = [turned(kv[:, to]) for kv in kv_refs]
            for half in range(2):
                q_one = jnp.concatenate([only(head_lanes(half), q), qm_ref[...]], axis=1)
                top = None
                for b in range(blocks):
                    key = jnp.concatenate([kv_refs[b][:, at], km_refs[b][...]], axis=1)
                    scores = dot_nt(key, q_one)
                    held[b] = scores
                    here = fold(scores, jnp.max)
                    top = here if top is None else jnp.maximum(top, here)
                top = jnp.max(top, axis=0, keepdims=True)
                total, bulk = None, None
                for b in range(blocks):
                    grown = jnp.exp(held[b] - top)
                    here = fold(grown, jnp.sum)
                    bulk = here if bulk is None else bulk + here
                    value = values[b][half * HEAD_DIM : (half + 1) * HEAD_DIM]
                    part = dot(value, grown.astype(LOW))
                    total = part if total is None else total + part
                bulk = jnp.sum(bulk, axis=0, keepdims=True)
                parts.append(total * (1.0 / bulk))
                row = pair * 2 + half
                norm_ref[row : row + 1, :] = top + jnp.log(bulk)
        mixed = jnp.concatenate(parts).T.astype(LOW)
        mixed_ref[...] = mixed
        copy.wait()
        part_ref[...] = dot_nt(mixed, w_ref[...]).astype(LOW)

    return kernel_call(
        kernel,
        (query, q_marks, *pairs, *k_marks, weights),
        [out((rows, width)), out((8, rows), WIDE), out((rows, weights.shape[0]))],
        [
            pltpu.VMEM((blocks, size, rows), WIDE),
            pltpu.VMEM((weights.shape[0], width), LOW),
            pltpu.SemaphoreType.DMA((1,)),
        ], cost=4.0,
        apart=1,
    )


def attend_back(layer, grads, part, arrived, middle, gain, weights, query, q_marks, norms, pairs, k_marks):
    rows, width = query.shape
    depth = middle.shape[1]
    heads = width // HEAD_DIM
    blocks = len(pairs)
    size = pairs[0].shape[0]
    scale = HEAD_DIM ** (-0.5)
    near = blocks // 2

    def kernel(grads_ref, part_ref, arrived_ref, middle_ref, gain_ref, q_ref, qm_ref, norm_ref, *refs):
        kv_refs, km_refs = refs[:blocks], refs[blocks : 2 * blocks]
        w_far, *refs = refs[2 * blocks :]
        gm_ref, low_ref, sums_ref, dq_ref, own_ref, away_ref, *refs = refs
        p_wide, w_wide, p_all, s_all, weight_ref, sems = refs
        (copy,) = start_copies([(w_far.at[:, 3 * width :], weight_ref)], sems)
        incoming = part_ref[...].astype(WIDE) + arrived_ref[...].astype(WIDE)
        gain_grad, shift_grad, through = norm_backward(
            incoming, middle_ref[...], gain_ref[layer : layer + 1, :]
        )
        g_middle = grads_ref[...].astype(WIDE) + through
        low = g_middle.astype(LOW)
        gm_ref[...] = g_middle
        low_ref[...] = low
        sums_ref[0:1, :] = gain_grad
        sums_ref[1:2, :] = shift_grad
        sums_ref[2:3, :] = jnp.sum(g_middle, axis=0, keepdims=True)
        copy.wait()
        g_mixed = dot(low, weight_ref[...]).astype(LOW)
        dqs = []
        for pair in range(heads // 2):
            at = slice(pair * 128, pair * 128 + 128)
            to = slice(width + pair * 128, width + pair * 128 + 128)
            q, g = q_ref[:, at], g_mixed[:, at]
            keys = [turned(kv[:, at]) for kv in kv_refs]
            q_stack, g_stack = [], []
            for half in range(2):
                lanes = head_lanes(half)
                q_stack.append(only(lanes, q))
                g_stack.append(only(lanes, g))
                q_one = jnp.concatenate([q_stack[half], qm_ref[...]], axis=1)
                row = pair * 2 + half
                norm = norm_ref[row : row + 1, :]
                total = None
                for b in range(blocks):
                    key = jnp.concatenate([kv_refs[b][:, at], km_refs[b][...]], axis=1)
                    probs = jnp.exp(dot_nt(key, q_one) - norm)
                    weighed = probs * dot_nt(kv_refs[b][:, to], g_stack[half])
                    here = fold(weighed, jnp.sum)
                    total = here if total is None else total + here
                    p_wide[b] = probs
                    w_wide[b] = weighed
                    p_all[b * size : (b + 1) * size, half * rows : (half + 1) * rows] = probs.astype(LOW)
                total = jnp.sum(total, axis=0, keepdims=True)
                dq = None
                for b in range(blocks):
                    g_scores = (w_wide[b] - p_wide[b] * total).astype(LOW)
                    s_all[b * size : (b + 1) * size, half * rows : (half + 1) * rows] = g_scores
                    part = dot(keys[b][half * HEAD_DIM : (half + 1) * HEAD_DIM], g_scores)
                    dq = part if dq is None else dq + part
                dqs.append(dq)
            dk = dot(s_all[...], jnp.concatenate(q_stack)).astype(LOW)
            dv = dot(p_all[...], jnp.concatenate(g_stack)).astype(LOW)
            own_ref[:, at] = dk[: near * size]
            away_ref[:, at] = dk[near * size :]
            own_ref[:, to] = dv[: near * size]
            away_ref[:, to] = dv[near * size :]
        dq_ref[...] = (jnp.concatenate(dqs).T * scale).astype(LOW)

    half_rows = near * size
    length = blocks * size
    return kernel_call(
        kernel,
        (grads, part, arrived, middle, gain, query, q_marks, norms, *pairs, *k_marks, weights),
        [
            out((rows, depth), WIDE),
            out((rows, depth)),
            out((8, depth), WIDE),
            out((rows, width)),
            out((half_rows, 2 * width)),
            out((half_rows, 2 * width)),
        ],
        [
            pltpu.VMEM((blocks, size, rows), WIDE),
            pltpu.VMEM((blocks, size, rows), WIDE),
            pltpu.VMEM((length, 2 * rows), LOW),
            pltpu.VMEM((length, 2 * rows), LOW),
            pltpu.VMEM((depth, width), LOW),
            pltpu.SemaphoreType.DMA((1,)),
        ], cost=1.0,
        room=14,
        apart=1,
    )


def local(
    hidden_in,
    time_embed,
    segment_ids,
    cotangent,
    query_weight,
    key_weight,
    value_weight,
    output_weight,
    up_weight,
    down_weight,
    query_bias,
    value_bias,
    output_bias,
    up_bias,
    down_bias,
    first_gain,
    first_shift,
    second_gain,
    second_shift,
):
    rows, depth = hidden_in.shape
    layers, _, head_width = query_weight.shape
    hidden_width = up_weight.shape[2]
    place = lax.axis_index("tensor")
    core = (place % 2).reshape(1)
    side = (place // 2).reshape(1)
    place = place.reshape(1)
    ring = Ring()
    last = layers - 1

    near_own = pack_near((query_weight, key_weight, value_weight, output_weight))
    near_peer = swap_core(near_own)
    hidden_other = swap_y(hidden_in)
    pieces = weave_near(core, near_own, near_peer)
    near = [Gather(ring, pieces[0])]
    near[0].step()
    if ring.use:
        (_, query_bias, value_bias, up_bias, segment_ids, cotangent, up_weight, down_weight) = tie(
            near[0].current,
            query_bias,
            value_bias,
            up_bias,
            segment_ids,
            cotangent,
            up_weight,
            down_weight,
        )
    far_own = (up_weight, jnp.swapaxes(down_weight, 1, 2))
    far_pieces = weave_far(core, far_own, [swap_core(piece) for piece in far_own])
    near[0].step()
    near[0].step()
    token = near[0].current if ring.use else None
    cotangent_other = swap_y(tie(cotangent, token)[0] if ring.use else cotangent)
    near[0].finish()
    far = [Gather(ring, far_pieces[0])]
    far[0].step(token)
    biases = jnp.concatenate([query_bias, value_bias, up_bias], axis=1)
    q_bias, v_bias, u_bias = weave_bias(core, biases, swap_core(biases), head_width)
    q_marks, k_marks = mark_documents(core, segment_ids, rows)
    near.append(Gather(ring, pieces[1]))
    far.append(Gather(ring, far_pieces[1]))

    def exchange(parts):
        arrived = [swap_y(part) for part in parts]
        arrived[0], parts[1] = tie(arrived[0], parts[1])
        return arrived

    kept = []
    for layer in range(layers):
        w_near = near[layer].whole
        if layer == 0:
            states, firsts, queries, pairs = project_first(
                side, hidden_in, hidden_other, time_embed, first_gain, first_shift, w_near, q_bias, v_bias
            )
            seeds = None
        else:
            made = [
                project(
                    layer,
                    middles[j],
                    branches[j],
                    arrived[j],
                    down_bias,
                    first_gain,
                    first_shift,
                    w_near,
                    q_bias,
                    v_bias,
                )
                for j in range(2)
            ]
            states, firsts, queries, pairs = ([m[i] for m in made] for i in range(4))
        pairs = list(pairs) + [swap_core(pair) for pair in pairs]
        mixeds, norms, parts = [], [], []
        far[layer].step(queries[1])
        for j in range(2):
            mixed, norm, part = attend(queries[j], q_marks[j], pairs, k_marks, w_near)
            mixeds.append(mixed)
            norms.append(norm)
            parts.append(part)
        far[layer].step(parts[1])
        arrived = [swap_y(part) for part in parts]
        if layer == 0:
            token = far[0].current if ring.use else None
            near[1].step(token)
        far[layer].finish()
        if layer == 0:
            near[1].step(far[0].current)
        w_far = far[layer].whole
        arrived[0], w_far = tie(arrived[0], w_far)
        if layer == 0:
            seed0, seed1, seed_sums = seed_rows(side, cotangent, cotangent_other, k_marks[:2])
            seeds = [seed0, seed1]
        made = []
        for j in range(2):
            made.append(
                feed(
                    layer,
                    states[j],
                    parts[j],
                    arrived[j],
                    output_bias,
                    second_gain,
                    second_shift,
                    w_far,
                    u_bias,
                    seeds[j] if layer == last else None,
                )
            )
            if layer == 0 and j == 0:
                near[1].step(made[j][4])
        middles, seconds, acts, others, branches = ([m[i] for m in made] for i in range(5))
        kept.append((states, firsts, queries, pairs, norms, mixeds, middles, seconds, acts, others))
        if layer < last:
            arrived = [swap_y(branch) for branch in branches]
            arrived[0], branches[1] = tie(arrived[0], branches[1])
            token = near[1].current if ring.use else None
            near[1].finish()
            far[1].step(token)

    entries = [(12 * last + 5, ("one", 0), (seed_sums,))]
    up_sums = [m[5] for m in made]
    grads, lows, g_pres, parts = seeds, seeds, others, branches
    under_way, results = [], {}

    def advance(main):
        for scatter in under_way:
            main = scatter.step(main)
        return main

    for layer in reversed(range(layers)):
        (states, firsts, queries, pairs, norms, mixeds, middles, seconds, acts, slopes) = kept[layer]
        w_near = near[layer].whole
        w_far = far[layer].whole
        base = 12 * layer
        if layer < last:
            made = []
            for j in range(2):
                if j == 1:
                    arrived[1] = advance(arrived[1])
                made.append(feed_back(
                    layer + 1,
                    g_middles[j],
                    parts[j],
                    arrived[j],
                    above[j],
                    first_gain,
                    slopes[j],
                    w_far,
                ))
            grads, lows, g_pres, parts, sums, up_sums = ([m[i] for m in made] for i in range(6))
            entries += [
                (base + 12, ("own", 0), sums),
                (base + 13, ("own", 1), sums),
                (base + 5, ("own", 2), sums),
            ]
        entries.append((base + 8, ("up", 0), up_sums))
        arrived = exchange(parts)
        if layer < last:
            arrived[0] = advance(arrived[0])
            feed_away, feed_own = outer_feed(core, seconds, g_pres, lows, acts)
            arrived[0], feed_own = tie(arrived[0], feed_own)
            got = swap_core(feed_away)
        made = []
        for j in range(2):
            if j == 1:
                if layer == last:
                    feed_away, feed_own = outer_feed(core, seconds, g_pres, lows, acts)
                    got = swap_core(feed_away)
                arrived[1], feed_own, got = tie(arrived[1], feed_own, got)
                under_way.append(Scatter(ring, [feed_own], [got]))
                results[layer, "feed"] = under_way[-1]
                arrived[1] = advance(arrived[1])
                if layer == last:
                    acts_after, _ = tie(acts, arrived[1])
                    away_rows, here_rows = last_branch(side, acts_after, w_far)
            made.append(
                attend_back(
                    layer,
                    grads[j],
                    parts[j],
                    arrived[j],
                    middles[j],
                    second_gain,
                    w_near,
                    queries[j],
                    q_marks[j],
                    norms[j],
                    pairs,
                    k_marks,
                )
            )
            if j == 0:
                g_pres, _ = tie(g_pres, made[0][1])
        g_middles, m_lows, sums, dqs, owns, aways = ([m[i] for m in made] for i in range(6))
        entries += [
            (base + 2, ("own", 0), sums),
            (base + 3, ("own", 1), sums),
            (base + 4, ("own", 2), sums),
        ]
        aways = [swap_core(away) for away in aways]
        if layer == last:
            aways[1] = advance(aways[1])
            aways[1], away_rows = tie(aways[1], away_rows)
            crossed = swap_y(away_rows)
        g_qkv, part0, part1, sums = project_back(side, dqs, owns, aways, w_near, layer == 0)
        entries += [(base + 6, ("half", 0), (sums,)), (base + 7, ("half", 1), (sums,))]
        if layer > 0:
            parts = [part0, part1]
            arrived = exchange(parts)
            above = states
        else:
            arrived = swap_y(part0)
        near_away = outer_heads(core, firsts, g_qkv, m_lows, mixeds, 1)
        near_got = swap_core(near_away)
        near_own = outer_heads(core, firsts, g_qkv, m_lows, mixeds, 0)
        results[layer, "near"] = Scatter(ring, [near_own], [near_got])
        under_way.append(results[layer, "near"])
        if layer == last:
            arrived[0], near_own, near_got = tie(arrived[0], near_own, near_got)
            arrived[0] = advance(arrived[0])
        else:
            results[0, "near"].step()
            first_message = results[0, "near"].made[0]
            results[0, "feed"].step(token=first_message)
            arrived, _ = tie(arrived, first_message)
        if layer == last:
            denoised = last_rows(side, middles, here_rows, crossed, down_bias, layer)
    input_grad, sums = first_rows(side, part1, arrived, states, g_middles, first_gain)
    entries += [(0, ("one", 0), (sums,)), (1, ("one", 1), (sums,))]
    total = vector_rows(place, entries, layers, depth)
    if ring.use:
        for move_by in exchanges(ring.count):
            total = total + move_by(total)
            total = advance(total)
    else:
        total = lax.psum(total, ("fsdp", "tensor"))
    vectors = vector_outputs(place, total, layers, head_width)
    up_out, down_out = matrix_outputs(
        [results[layer, "feed"].finish() for layer in range(layers)], hidden_width, False
    )
    down_out = jnp.swapaxes(down_out, 1, 2)
    heads = matrix_outputs([results[layer, "near"].finish() for layer in range(layers)], head_width, True)
    return (denoised, input_grad, *heads, up_out, down_out, *vectors)


def solution(mesh):
    rows = P(("fsdp", "tensor"), None)
    inner = P(None, "fsdp", "tensor")
    outer = P(None, "tensor", "fsdp")
    cut = P(None, "tensor")
    in_specs = (
        rows,
        P("fsdp", None),
        P("fsdp", None),
        rows,
        inner,
        inner,
        inner,
        outer,
        inner,
        outer,
        cut,
        cut,
        P(),
        cut,
        P(),
        P(),
        P(),
        P(),
        P(),
    )
    out_specs = (
        rows,
        rows,
        inner,
        inner,
        inner,
        outer,
        inner,
        outer,
        cut,
        cut,
        P(),
        cut,
        P(),
        P(),
        P(),
        P(),
        P(),
    )
    return jax.shard_map(local, mesh=mesh, in_specs=in_specs, out_specs=out_specs, check_vma=False)
```

```python
import functools

import jax
import jax.numpy as jnp
from jax import lax
from jax.experimental import pallas as pl
from jax.experimental.pallas import tpu as pltpu
from jax.sharding import PartitionSpec as P

HEAD_DIM = 64
EPSILON = 1e-05
LOW = jnp.bfloat16
WIDE = jnp.float32
ROOT = 0.7978845608028654
CUBE = 0.044715

SWAP_CORE = [(0, 1), (1, 0), (2, 3), (3, 2)]
SWAP_Y = [(0, 2), (2, 0), (1, 3), (3, 1)]


def swap_core(value):
    return lax.ppermute(value, "tensor", SWAP_CORE)


def swap_y(value):
    return lax.ppermute(value, "tensor", SWAP_Y)


def dot(a, b):
    return jnp.dot(a, b, preferred_element_type=WIDE)


def dot_nt(a, b):
    return lax.dot_general(a, b, (((1,), (1,)), ((), ())), preferred_element_type=WIDE)


def dot_tn(a, b):
    return lax.dot_general(a, b, (((0,), (0,)), ((), ())), preferred_element_type=WIDE)


def tie(*values):
    return lax.optimization_barrier(values)


def ring_order(count):
    return list(range(0, count, 2)) + list(range(count - 1, 0, -2))


class Ring:
    def __init__(self):
        self.count = lax.axis_size("fsdp")
        self.use = self.count == 8
        self.core = lax.axis_index("tensor") % 2
        if self.use:
            here = lax.axis_index("fsdp")
            self.place = jnp.where(here % 2 == 0, here // 2, self.count - 1 - here // 2)
            self.way = 1 - 2 * self.core
            self.far = self.count // 2
            order = ring_order(self.count)
            self.pairs = [
                [(order[i], order[(i + way) % self.count]) for i in range(self.count)]
                for way in (1, -1)
            ]
            self.split = [
                (here * 4 + t, there * 4 + t)
                for t in range(4)
                for here, there in self.pairs[t % 2]
            ]
            self.blocks = jnp.stack([self.block_at(step) for step in range(self.count)])

    def split_send(self, value):
        return lax.ppermute(value, ("fsdp", "tensor"), self.split)

    def send_both(self, ahead, behind):
        return lax.ppermute(ahead, "fsdp", self.pairs[0]), lax.ppermute(behind, "fsdp", self.pairs[1])

    def block_at(self, steps):
        place = (self.place + steps + 2 * self.count) % self.count
        return jnp.where(place < self.count // 2, 2 * place, 2 * (self.count - 1 - place) + 1)


class Gather:
    def __init__(self, ring, piece):
        self.ring = ring
        self.rows, self.columns = piece.shape
        self.todo = []
        self.done = 0
        self.current = piece
        if ring.use:
            self.whole = jnp.zeros((ring.count * self.rows, self.columns), piece.dtype)
            self.put(piece, lax.axis_index("fsdp"))
        else:
            self.whole = lax.all_gather(piece, "fsdp", axis=0, tiled=True)

    def put(self, value, block, offset=0):
        start = block * self.rows + offset
        self.whole = lax.dynamic_update_slice(self.whole, value, (start, 0))

    def flush(self):
        ring = self.ring
        half = self.rows // 2
        for step, value in self.todo:
            if step < ring.far:
                self.put(value, ring.block_at(-ring.way * step))
                self.put(swap_core(value), ring.block_at(ring.way * step))
            else:
                block = ring.block_at(step)
                self.put(value, block, ring.core * half)
                self.put(swap_core(value), block, (1 - ring.core) * half)
        self.todo = []

    def step(self, token=None):
        ring = self.ring
        if not ring.use or self.done == ring.far:
            return
        self.flush()
        self.done += 1
        current = self.current
        if token is not None:
            current, _ = tie(current, token)
        if self.done == ring.far:
            half = self.rows // 2
            current = lax.dynamic_slice(current, (ring.core * half, 0), (half, self.columns))
        self.current = ring.split_send(current)
        self.todo.append((self.done, self.current))

    def finish(self):
        if self.ring.use:
            while self.done < self.ring.far:
                self.step()
            self.flush()


class Scatter:
    def __init__(self, ring, owns, gots):
        self.ring = ring
        self.owns, self.gots = owns, gots
        self.done = 0
        self.made = owns
        if ring.use:
            self.rows = owns[0].shape[0] // ring.count
        else:
            total = jnp.concatenate(
                [own.astype(WIDE) + got.astype(WIDE) for own, got in zip(owns, gots)], axis=1
            )
            self.result = lax.psum_scatter(total, "fsdp", scatter_dimension=0, tiled=True)

    def step(self, main=None, token=None):
        ring = self.ring
        if not ring.use or self.done > ring.far:
            return main
        moving = None
        if self.done:
            moving = self.flying
            if main is not None:
                main, *moving = tie(main, *moving)
        if self.done == ring.far:
            self.done += 1
            self.result = passing(ring.blocks, self.owns, self.gots, 0, ring.count, moving)[0]
            return main
        owns = self.owns
        if main is None and token is not None:
            owns, _ = tie(owns, token)
        made = passing(ring.blocks, owns, self.gots, ring.far - self.done, ring.count, moving)
        if main is not None:
            main, *made = tie(main, *made)
        self.made = made
        self.flying = ring.send_both(*made)
        self.done += 1
        return main

    def finish(self):
        if self.ring.use:
            while self.done <= self.ring.far:
                self.step()
        return self.result


def exchanges(count):
    moves = [swap_core, swap_y]
    bit = 1
    while bit < count:
        pairs = [(i, i ^ bit) for i in range(count)]
        moves.append(lambda value, pairs=pairs: lax.ppermute(value, "fsdp", pairs))
        bit *= 2
    return moves


NEVER = -1e30


def out(shape, dtype=LOW):
    return jax.ShapeDtypeStruct(shape, dtype)


def kernel_call(kernel, operands, outs, scratch=(), scalars=0, cost=1.0, room=8, apart=0):
    inside = pl.BlockSpec(memory_space=pltpu.VMEM)
    word = pl.BlockSpec(memory_space=pltpu.SMEM)
    return pl.pallas_call(
        kernel,
        in_specs=[word] * scalars
        + [inside] * (len(operands) - scalars - apart)
        + [pl.BlockSpec(memory_space=pl.ANY)] * apart,
        out_specs=[inside] * len(outs),
        out_shape=outs,
        scratch_shapes=scratch,
        compiler_params=pltpu.CompilerParams(vmem_limit_bytes=room << 20),
        cost_estimate=pl.CostEstimate(
            flops=int(cost * 1e9), bytes_accessed=1024, transcendentals=0
        ),
    )(*operands)


def start_copies(pairs, sems):
    copies = [
        pltpu.make_async_copy(source, target, sems.at[index])
        for index, (source, target) in enumerate(pairs)
    ]
    for copy in copies:
        copy.start()
    return copies


def norm_parts(rows):
    center = rows - jnp.mean(rows, axis=1, keepdims=True)
    factor = lax.rsqrt(jnp.mean(center * center, axis=1, keepdims=True) + EPSILON)
    return center * factor, factor


def norm_backward(grad, rows, gain):
    normed, factor = norm_parts(rows)
    scaled = grad * gain
    through = factor * (
        scaled
        - jnp.mean(scaled, axis=1, keepdims=True)
        - normed * jnp.mean(scaled * normed, axis=1, keepdims=True)
    )
    gain_grad = jnp.sum(grad * normed, axis=0, keepdims=True)
    return gain_grad, jnp.sum(grad, axis=0, keepdims=True), through


def gelu_both(pre):
    inner = jnp.tanh(ROOT * (pre + CUBE * pre * pre * pre))
    slope = 0.5 * (1.0 + inner) + 0.5 * pre * (1.0 - inner * inner) * (
        ROOT * (1.0 + 3.0 * CUBE * pre * pre)
    )
    return 0.5 * pre * (1.0 + inner), slope


def project(layer, base, part, arrived, bias, gain, shift, weights, q_bias, v_bias):
    rows, depth = base.shape
    width = q_bias.shape[1]
    scale = HEAD_DIM ** (-0.5)
    at = slice(layer, layer + 1)

    def kernel(base_ref, part_ref, arrived_ref, bias_ref, gain_ref, shift_ref, qb_ref, vb_ref, w_far,
               state_ref, first_ref, q_ref, kv_ref, w_ref, sems):
        (copy,) = start_copies([(w_far.at[:, : 3 * width], w_ref)], sems)
        state = base_ref[...] + (part_ref[...].astype(WIDE) + arrived_ref[...].astype(WIDE))
        state += bias_ref[layer - 1 : layer, :]
        first = (norm_parts(state)[0] * gain_ref[at, :] + shift_ref[at, :]).astype(LOW)
        state_ref[...] = state
        first_ref[...] = first
        copy.wait()
        query = (dot(first, w_ref[:, :width]) + qb_ref[at, :]).astype(LOW)
        q_ref[...] = query * jnp.asarray(scale, LOW)
        kv_ref[:, :width] = dot(first, w_ref[:, width : 2 * width]).astype(LOW)
        kv_ref[:, width:] = (dot(first, w_ref[:, 2 * width : 3 * width]) + vb_ref[at, :]).astype(LOW)

    return kernel_call(
        kernel,
        (base, part, arrived, bias, gain, shift, q_bias, v_bias, weights),
        [
            out((rows, depth), WIDE),
            out((rows, depth)),
            out((rows, width)),
            out((rows, 2 * width)),
        ], scratch=[pltpu.VMEM((depth, 3 * width), LOW), pltpu.SemaphoreType.DMA((1,))],
        cost=1.2,
        apart=1,
    )


def feed(layer, state, part, arrived, out_bias, gain, shift, weights, up_bias, lows=None):
    rows, depth = state.shape
    hidden = up_bias.shape[1]
    back = lows is not None
    half = hidden // 2
    tile = 384
    row = slice(layer, layer + 1)

    def kernel(*refs):
        state_ref, part_ref, arrived_ref, ob_ref, gain_ref, shift_ref, w_ref, ub_ref = refs[:8]
        refs = refs[8:]
        middle = (
            state_ref[...] + (part_ref[...].astype(WIDE) + arrived_ref[...].astype(WIDE)) + ob_ref[row, :]
        )
        second = (norm_parts(middle)[0] * gain_ref[row, :] + shift_ref[row, :]).astype(LOW)
        if back:
            lows_ref, middle_ref, second_ref, act_ref, other_ref, branch_ref, ubg_ref = refs
            low = lows_ref[...]
        else:
            middle_ref, second_ref, act_ref, other_ref, branch_ref = refs
        middle_ref[...] = middle
        second_ref[...] = second
        total = None
        for start in range(0, hidden, tile):
            at = slice(start, start + tile)
            inside = start + start // half * half
            up = w_ref[:, inside : inside + tile]
            down = w_ref[:, half + inside : half + inside + tile]
            act, slope = gelu_both(dot(second, up) + ub_ref[row, at])
            act = act.astype(LOW)
            act_ref[:, at] = act
            if back:
                other = (dot(low, down) * slope).astype(LOW)
                ubg_ref[0:1, at] = jnp.sum(other.astype(WIDE), axis=0, keepdims=True)
                here = dot_nt(other, up)
            else:
                other = slope.astype(LOW)
                here = dot_nt(act, down)
            other_ref[:, at] = other
            total = here if total is None else total + here
        branch_ref[...] = total.astype(LOW)

    operands = [state, part, arrived, out_bias, gain, shift, weights, up_bias]
    outs = [
        out((rows, depth), WIDE),
        out((rows, depth)),
        out((rows, hidden)),
        out((rows, hidden)),
        out((rows, depth)),
    ]
    if back:
        operands.append(lows)
        outs.append(out((8, hidden), WIDE))
    return kernel_call(kernel, operands, outs, cost=4.0)


def feed_back(layer, g_middle, part, arrived, state, gain, slopes, weights):
    rows, depth = state.shape
    hidden = slopes.shape[1]
    half = hidden // 2
    tile = 384

    def kernel(gm_ref, part_ref, arrived_ref, state_ref, gain_ref, slope_ref, w_ref,
               grad_ref, low_ref, gpre_ref, branch_ref, sums_ref, ubg_ref):
        incoming = part_ref[...].astype(WIDE) + arrived_ref[...].astype(WIDE)
        gain_grad, shift_grad, through = norm_backward(incoming, state_ref[...], gain_ref[layer : layer + 1, :])
        grad = gm_ref[...] + through
        low = grad.astype(LOW)
        grad_ref[...] = grad
        low_ref[...] = low
        sums_ref[0:1, :] = gain_grad
        sums_ref[1:2, :] = shift_grad
        sums_ref[2:3, :] = jnp.sum(grad, axis=0, keepdims=True)
        total = None
        for start in range(0, hidden, tile):
            at = slice(start, start + tile)
            inside = start + start // half * half
            up = w_ref[:, inside : inside + tile]
            down = w_ref[:, half + inside : half + inside + tile]
            gpre = (dot(low, down) * slope_ref[:, at].astype(WIDE)).astype(LOW)
            gpre_ref[:, at] = gpre
            ubg_ref[0:1, at] = jnp.sum(gpre.astype(WIDE), axis=0, keepdims=True)
            here = dot_nt(gpre, up)
            total = here if total is None else total + here
        branch_ref[...] = total.astype(LOW)

    return kernel_call(
        kernel,
        (g_middle, part, arrived, state, gain, slopes, weights),
        [
            out((rows, depth), WIDE),
            out((rows, depth)),
            out((rows, hidden)),
            out((rows, depth)),
            out((8, depth), WIDE),
            out((8, hidden), WIDE),
        ], cost=3.8)

def turned(value):
    return value.astype(WIDE).T.astype(LOW)


def outer_feed(core, seconds, g_pres, lows, acts):
    depth = seconds[0].shape[1]
    size = acts[0].shape[1] // 2

    def kernel(core_ref, s0, s1, g0, g1, l0, l1, a0, a1, *out_refs):
        for index, (left_refs, right_refs) in enumerate((((s0, s1), (g0, g1)), ((l0, l1), (a0, a1)))):
            left = jnp.concatenate([turned(ref[...]) for ref in left_refs], axis=1)
            for which, out_ref in ((1, out_refs[0]), (0, out_refs[1])):
                start = jnp.where(core_ref[0] == which, 0, size)
                for at in range(0, size, 384):
                    columns = pl.ds(pl.multiple_of(start + at, 128), 384)
                    right = jnp.concatenate([ref[:, columns] for ref in right_refs])
                    base = index * size + at
                    out_ref[:, base : base + 384] = dot(left, right).astype(LOW)

    return kernel_call(
        kernel,
        (core, *seconds, *g_pres, *lows, *acts),
        [out((depth, 2 * size))] * 2,
        scalars=1,
        cost=3.4,
    )


def outer_heads(core, firsts, g_qkv, m_lows, mixeds, which):
    depth = firsts[0].shape[1]
    width = mixeds[0].shape[1]
    size = width // 2

    def kernel(core_ref, f0, f1, g_ref, l0, l1, m0, m1, out_ref):
        low = core_ref[0] == which

        def pick(value):
            return jnp.where(low, value[:, :size], value[:, size:])

        first = jnp.concatenate([turned(f0[...]), turned(f1[...])], axis=1)
        g = g_ref[...]
        right = jnp.concatenate(
            [pick(g[:, i * width : (i + 1) * width]) for i in range(3)], axis=1
        )
        m_low = jnp.concatenate([turned(l0[...]), turned(l1[...])], axis=1)
        mixed = jnp.concatenate([pick(m0[...]), pick(m1[...])])
        out_ref[...] = jnp.concatenate([dot(first, right), dot(m_low, mixed)], axis=1).astype(LOW)

    return kernel_call(
        kernel, (core, *firsts, g_qkv, *m_lows, *mixeds), [out((depth, 4 * size))], scalars=1, cost=1.8)[0]


def passing(blocks, owns, gots, step, count, moving):
    parts = len(owns)
    rows = owns[0].shape[0] // count
    half = rows // 2
    columns = sum(own.shape[1] for own in owns)
    first = moving is None
    last = step == 0
    partial_in = not first and moving[0].shape[0] == half

    def kernel(blocks_ref, *refs):
        if first:
            moving_refs, refs = (), refs
        else:
            moving_refs, refs = refs[:2], refs[2:]
        own_refs, got_refs = refs[:parts], refs[parts : 2 * parts]
        out_refs, held, sems = refs[2 * parts : -1 - 2 * parts], refs[-1 - 2 * parts : -1], refs[-1]
        if first:
            wanted = [(step, 0, half), (step, half, half)]
        elif last:
            wanted = [(0, 0, rows)]
        else:
            wanted = [(step, 0, rows), ((count - step) % count, 0, rows)]
        pairs = []
        for index, (block, offset, size) in enumerate(wanted):
            start = pl.multiple_of(blocks_ref[block] * rows + offset, 16)
            for ref, target in zip((*own_refs, *got_refs), held):
                pairs.append((ref.at[pl.ds(start, size), :], target.at[index, pl.ds(0, size), :]))
        copies = start_copies(pairs, sems)
        for copy in copies:
            copy.wait()

        def here(index, size=rows):
            return jnp.concatenate(
                [
                    held[k][index, :size].astype(WIDE) + held[parts + k][index, :size].astype(WIDE)
                    for k in range(parts)
                ],
                axis=1,
            )

        if first:
            out_refs[0][...] = here(0, half).astype(LOW)
            out_refs[1][...] = here(1, half).astype(LOW)
        elif last:
            total = here(0) + moving_refs[0][...].astype(WIDE) + moving_refs[1][...].astype(WIDE)
            out_refs[0][...] = total
        else:
            ahead, behind = here(0), here(1)
            a, b = moving_refs[0][...].astype(WIDE), moving_refs[1][...].astype(WIDE)
            if partial_in:
                out_refs[0][:half, :] = (ahead[:half] + a).astype(LOW)
                out_refs[0][half:, :] = ahead[half:].astype(LOW)
                out_refs[1][:half, :] = behind[:half].astype(LOW)
                out_refs[1][half:, :] = (behind[half:] + b).astype(LOW)
            else:
                out_refs[0][...] = (ahead + a).astype(LOW)
                out_refs[1][...] = (behind + b).astype(LOW)

    if last:
        outs = [out((rows, columns), WIDE)]
    else:
        outs = [out((half if first else rows, columns))] * 2
    operands = (blocks, *(() if first else moving), *owns, *gots)
    return kernel_call(
        kernel,
        operands,
        outs,
        [pltpu.VMEM((2, rows, own.shape[1]), LOW) for own in (*owns, *gots)]
        + [pltpu.SemaphoreType.DMA((4 * parts,))],
        scalars=1,
        cost=0.8,
        apart=2 * parts,
    )


def pack_near(weights):
    layers, rows, size = weights[0].shape

    def kernel(*refs):
        out_ref, held, sems = refs[4], refs[5:9], refs[9]
        copies = [
            pltpu.make_async_copy(refs[i], held[i], sems.at[i]) for i in range(4)
        ]
        for copy in copies:
            copy.start()
        for copy in copies:
            copy.wait()
        q_ref, k_ref, v_ref, o_ref = held
        for layer in range(layers):
            out_ref[layer] = jnp.concatenate(
                [q_ref[layer], k_ref[layer], v_ref[layer], turned(o_ref[layer])], axis=1
            )

    return pl.pallas_call(
        kernel,
        in_specs=[pl.BlockSpec(memory_space=pltpu.HBM)] * 4,
        out_specs=pl.BlockSpec(memory_space=pltpu.VMEM),
        out_shape=out((layers, rows, 4 * size)),
        scratch_shapes=[pltpu.VMEM(w.shape, LOW) for w in weights]
        + [pltpu.SemaphoreType.DMA((4,))],
        compiler_params=pltpu.CompilerParams(vmem_limit_bytes=8 << 20),
        cost_estimate=pl.CostEstimate(flops=1000, bytes_accessed=1024, transcendentals=0),
    )(*weights)


def weave_near(core, own, peer):
    layers, rows, columns = own.shape
    size = columns // 4

    def kernel(core_ref, own_ref, peer_ref, *out_refs):
        first = core_ref[0] == 0
        for layer, out_ref in enumerate(out_refs):
            a, b = own_ref[layer], peer_ref[layer]
            low, high = jnp.where(first, a, b), jnp.where(first, b, a)
            parts = []
            for i in range(4):
                parts += [low[:, i * size : (i + 1) * size], high[:, i * size : (i + 1) * size]]
            out_ref[...] = jnp.concatenate(parts, axis=1)

    return kernel_call(
        kernel, (core, own, peer), [out((rows, 2 * columns))] * layers, scalars=1
    )


def weave_far(core, own, peer):
    layers, rows, columns = own[0].shape

    def kernel(core_ref, u_own, d_own, u_peer, d_peer, *out_refs):
        first = core_ref[0] == 0
        for layer, out_ref in enumerate(out_refs):
            for index, (own_ref, peer_ref) in enumerate(((u_own, u_peer), (d_own, d_peer))):
                a, b = own_ref[layer], peer_ref[layer]
                low, high = index * columns, (2 + index) * columns
                out_ref[:, low : low + columns] = jnp.where(first, a, b)
                out_ref[:, high : high + columns] = jnp.where(first, b, a)

    return kernel_call(
        kernel, (core, *own, *peer), [out((rows, 4 * columns))] * layers, scalars=1
    )


def weave_bias(core, own, peer, size):
    layers = own.shape[0]
    rest = own.shape[1] - 2 * size

    def kernel(core_ref, own_ref, peer_ref, q_ref, v_ref, u_ref):
        first = core_ref[0] == 0
        a, b = own_ref[...], peer_ref[...]
        low, high = jnp.where(first, a, b), jnp.where(first, b, a)
        q_ref[...] = jnp.concatenate([low[:, :size], high[:, :size]], axis=1)
        v_ref[...] = jnp.concatenate([low[:, size : 2 * size], high[:, size : 2 * size]], axis=1)
        u_ref[...] = jnp.concatenate([low[:, 2 * size :], high[:, 2 * size :]], axis=1)

    return kernel_call(
        kernel,
        (core, own, peer),
        [
            out((layers, 2 * size), WIDE),
            out((layers, 2 * size), WIDE),
            out((layers, 2 * rest), WIDE),
        ],
        scalars=1,
    )


def mark_documents(core, segments, rows):
    def kernel(core_ref, segment_ref, *refs):
        core = core_ref[0]
        blocks = [core, 2 + core, 1 - core, 3 - core]
        lane = lax.broadcasted_iota(jnp.int32, (128, rows), 0)
        for index, block in enumerate(blocks):
            at = pl.ds(pl.multiple_of(block * rows, 128), rows)
            mark = jnp.where(lane == segment_ref[:, at] + 1, 1.0, 0.0).T
            refs[2 + index][...] = mark.astype(LOW)
            if index < 2:
                real = lax.broadcasted_iota(jnp.int32, (rows, 128), 1) < 9
                refs[index][...] = jnp.where(real & (mark == 0.0), NEVER, 0.0).astype(LOW)

    made = kernel_call(kernel, (core, segments), [out((rows, 128))] * 6, scalars=1)
    return made[:2], made[2:]


def seed_rows(side, own, other, marks):
    rows, depth = own.shape

    def kernel(side_ref, own_ref, other_ref, m0, m1, low0, low1, sums_ref):
        total = None
        for j, (mark, low) in enumerate(((m0, low0), (m1, low1))):
            mine = side_ref[0] == j
            value = jnp.where(mine, own_ref[...], other_ref[...])
            value = jnp.where(mark[:, 0:1] > 0, jnp.zeros_like(value), value)
            low[...] = value
            here = jnp.sum(value.astype(WIDE), axis=0, keepdims=True)
            here = jnp.where(mine, here, 0.0)
            total = here if total is None else total + here
        sums_ref[0:1, :] = total

    return kernel_call(
        kernel,
        (side, own, other, *marks),
        [out((rows, depth)), out((rows, depth)), out((8, depth), WIDE)],
        scalars=1,
    )


def project_first(side, own, other, embed, gain, shift, weights, q_bias, v_bias):
    rows, depth = own.shape
    width = q_bias.shape[1]
    scale = HEAD_DIM ** (-0.5)

    def kernel(side_ref, own_ref, other_ref, embed_ref, gain_ref, shift_ref, qb_ref, vb_ref, w_far, *refs):
        w_ref, sems = refs[8:]
        (copy,) = start_copies([(w_far.at[:, : 3 * width], w_ref)], sems)
        firsts = []
        for j in range(2):
            rows_in = jnp.where(side_ref[0] == j, own_ref[...], other_ref[...])
            state = rows_in.astype(WIDE) + embed_ref[...].astype(WIDE)
            refs[j][...] = state
            first = (norm_parts(state)[0] * gain_ref[0:1, :] + shift_ref[0:1, :]).astype(LOW)
            refs[2 + j][...] = first
            firsts.append(first)
        first = jnp.concatenate(firsts)
        copy.wait()
        query = (dot(first, w_ref[:, :width]) + qb_ref[0:1, :]).astype(LOW)
        query = query * jnp.asarray(scale, LOW)
        key = dot(first, w_ref[:, width : 2 * width]).astype(LOW)
        value = (dot(first, w_ref[:, 2 * width : 3 * width]) + vb_ref[0:1, :]).astype(LOW)
        for j in range(2):
            at = slice(j * rows, (j + 1) * rows)
            refs[4 + j][...] = query[at]
            refs[6 + j][:, :width] = key[at]
            refs[6 + j][:, width:] = value[at]

    made = kernel_call(
        kernel,
        (side, own, other, embed, gain, shift, q_bias, v_bias, weights),
        [out((rows, depth), WIDE)] * 2
        + [out((rows, depth))] * 2
        + [out((rows, width))] * 2
        + [out((rows, 2 * width))] * 2,
        scalars=1, scratch=[pltpu.VMEM((depth, 3 * width), LOW), pltpu.SemaphoreType.DMA((1,))],
        cost=1.8,
        apart=1,
    )
    return [made[2 * i : 2 * i + 2] for i in range(4)]


def last_branch(side, acts, weights):
    rows, hidden = acts[0].shape
    depth = weights.shape[0]
    size = hidden // 2

    def kernel(side_ref, a0, a1, w_far, away_ref, here_ref, w_ref, sems):
        copies = start_copies(
            [(w_far.at[:, (2 * i + 1) * size : (2 * i + 2) * size], w_ref.at[i]) for i in range(2)], sems
        )
        for copy in copies:
            copy.wait()
        for flip, ref in ((1, away_ref), (0, here_ref)):
            act = jnp.where(side_ref[0] == flip, a0[...], a1[...])
            total = dot_nt(act[:, :size], w_ref[0])
            total += dot_nt(act[:, size:], w_ref[1])
            ref[...] = total.astype(ref.dtype)

    return kernel_call(
        kernel,
        (side, *acts, weights),
        [out((rows, depth)), out((rows, depth), WIDE)],
        scalars=1, scratch=[pltpu.VMEM((2, depth, size), LOW), pltpu.SemaphoreType.DMA((2,))],
        cost=1.4,
        apart=1,
    )


def last_rows(side, middles, here, crossed, bias, layer):
    rows, depth = here.shape

    def kernel(side_ref, m0, m1, here_ref, crossed_ref, bias_ref, out_ref):
        middle = jnp.where(side_ref[0] == 0, m0[...], m1[...])
        total = here_ref[...] + crossed_ref[...].astype(WIDE)
        out_ref[...] = (middle + total + bias_ref[layer : layer + 1, :]).astype(LOW)

    return kernel_call(
        kernel, (side, *middles, here, crossed, bias), [out((rows, depth))], scalars=1
    )[0]


def project_back(side, dqs, owns, aways, weights, last):
    rows, width = dqs[0].shape
    depth = weights.shape[0]

    def kernel(side_ref, dq0, dq1, own0, own1, away0, away1, w_far, g_ref, part0, part1, sums_ref, w_ref, sems):
        (copy,) = start_copies([(w_far.at[:, : 3 * width], w_ref)], sems)
        pair = (
            own0[...].astype(WIDE)
            + own1[...].astype(WIDE)
            + (away0[...].astype(WIDE) + away1[...].astype(WIDE))
        ).astype(LOW)
        g_ref[:rows, :width] = dq0[...]
        g_ref[rows:, :width] = dq1[...]
        g_ref[:, width:] = pair
        g = g_ref[...]
        copy.wait()
        total = dot_nt(g, w_ref[...])
        low, high = total[:rows], total[rows:]
        if last:
            part0[...] = jnp.where(side_ref[0] == 0, high, low).astype(LOW)
            part1[...] = jnp.where(side_ref[0] == 0, low, high)
        else:
            part0[...] = low.astype(LOW)
            part1[...] = high.astype(LOW)
        sums_ref[0:1, :] = jnp.sum(g[:, :width].astype(WIDE), axis=0, keepdims=True)
        sums_ref[1:2, :] = jnp.sum(pair[:, width:].astype(WIDE), axis=0, keepdims=True)

    return kernel_call(
        kernel,
        (side, *dqs, *owns, *aways, weights),
        [
            out((2 * rows, 3 * width)),
            out((rows, depth)),
            out((rows, depth), WIDE if last else LOW),
            out((8, width), WIDE),
        ],
        scalars=1, scratch=[pltpu.VMEM((depth, 3 * width), LOW), pltpu.SemaphoreType.DMA((1,))],
        cost=1.6,
        apart=1,
    )


def first_rows(side, here, arrived, states, g_middles, gain):
    rows, depth = here.shape

    def kernel(side_ref, here_ref, arrived_ref, s0, s1, g0, g1, gain_ref, out_ref, sums_ref):
        low = side_ref[0] == 0
        incoming = here_ref[...] + arrived_ref[...].astype(WIDE)
        state = jnp.where(low, s0[...], s1[...])
        gain_grad, shift_grad, through = norm_backward(incoming, state, gain_ref[0:1, :])
        out_ref[...] = jnp.where(low, g0[...], g1[...]) + through
        sums_ref[0:1, :] = gain_grad
        sums_ref[1:2, :] = shift_grad

    return kernel_call(
        kernel,
        (side, here, arrived, *states, *g_middles, gain),
        [out((rows, depth), WIDE), out((8, depth), WIDE)],
        scalars=1,
    )


def vector_rows(place, entries, layers, depth):
    arrays = [array for _, _, group in entries for array in group]

    def kernel(place_ref, *refs):
        out_ref = refs[-1]
        place = place_ref[0]
        side = place // 2
        at = 0
        for row, (take, index), group in entries:
            here = refs[at : at + len(group)]
            at += len(group)
            if take == "own":
                value = jnp.where(side == 0, here[0][index : index + 1, :], here[1][index : index + 1, :])
                out_ref[row : row + 1, :] = value
            elif take == "one":
                out_ref[row : row + 1, :] = here[0][index : index + 1, :]
            elif take == "half":
                value = here[0][index : index + 1, :]
                zero = jnp.zeros_like(value)
                out_ref[row : row + 1, :] = jnp.concatenate(
                    [jnp.where(side == 0, value, zero), jnp.where(side == 0, zero, value)], axis=1
                )
            else:
                value = here[0][0:1, :] + here[1][0:1, :]
                for t in range(4):
                    here_row = value[:, t % 2 * depth : (t % 2 + 1) * depth]
                    out_ref[row + t : row + t + 1, :] = jnp.where(side == t // 2, here_row, 0.0)

    return kernel_call(
        kernel, (place, *arrays), [out((12 * layers, depth), WIDE)], scalars=1
    )[0]


def vector_outputs(place, total, layers, size):
    depth = total.shape[1]

    def kernel(place_ref, total_ref, qb, vb, ob, ub, db, fg, fs, sg, ss):
        place = place_ref[0]

        def pick(values):
            result = values[0]
            for t in range(1, 4):
                result = jnp.where(place == t, values[t], result)
            return result

        for layer in range(layers):
            at = slice(layer, layer + 1)
            row = lambda i: total_ref[12 * layer + i : 12 * layer + i + 1, :]
            for ref, i in ((fg, 0), (fs, 1), (sg, 2), (ss, 3), (ob, 4), (db, 5)):
                ref[at, :] = row(i)
            for ref, i in ((qb, 6), (vb, 7)):
                value = row(i)
                ref[at, :] = pick([value[:, t * size : (t + 1) * size] for t in range(4)])
            ub[at, :] = pick([row(8 + t) for t in range(4)])

    small, large = out((layers, size), WIDE), out((layers, depth), WIDE)
    return kernel_call(
        kernel, (place, total), [small, small] + [large] * 7, scalars=1
    )


def matrix_outputs(results, size, turn):
    layers = len(results)
    rows, columns = results[0].shape
    count = columns // size

    def kernel(*refs):
        for layer in range(layers):
            value = refs[layer][...].astype(WIDE)
            for i in range(count):
                part = value[:, i * size : (i + 1) * size]
                refs[layers + i][layer] = part.T if turn and i == count - 1 else part

    return kernel_call(
        kernel,
        results,
        [out((layers, rows, size), WIDE)] * (count - 1)
        + [out((layers, size, rows) if turn else (layers, rows, size), WIDE)],
    )


def head_lanes(half):
    lane = lax.broadcasted_iota(jnp.int32, (1, 128), 1)
    return (lane >= half * HEAD_DIM) & (lane < (half + 1) * HEAD_DIM)


def only(mask, value):
    return jnp.where(mask, value, jnp.zeros_like(value))


def fold(value, reduce):
    return reduce(value.reshape(value.shape[0] // 8, 8, value.shape[1]), axis=0)


def attend(query, q_marks, pairs, k_marks, weights):
    rows, width = query.shape
    heads = width // HEAD_DIM
    blocks = len(pairs)
    size = pairs[0].shape[0]

    def kernel(q_ref, qm_ref, *refs):
        kv_refs, km_refs = refs[:blocks], refs[blocks : 2 * blocks]
        w_far, mixed_ref, norm_ref, part_ref, held, w_ref, sems = refs[2 * blocks :]
        (copy,) = start_copies([(w_far.at[:, 3 * width :], w_ref)], sems)
        parts = []
        for pair in range(heads // 2):
            at = slice(pair * 128, pair * 128 + 128)
            to = slice(width + pair * 128, width + pair * 128 + 128)
            q = q_ref[:, at]
            values = [turned(kv[:, to]) for kv in kv_refs]
            for half in range(2):
                q_one = jnp.concatenate([only(head_lanes(half), q), qm_ref[...]], axis=1)
                top = None
                for b in range(blocks):
                    key = jnp.concatenate([kv_refs[b][:, at], km_refs[b][...]], axis=1)
                    scores = dot_nt(key, q_one)
                    held[b] = scores
                    here = fold(scores, jnp.max)
                    top = here if top is None else jnp.maximum(top, here)
                top = jnp.max(top, axis=0, keepdims=True)
                total, bulk = None, None
                for b in range(blocks):
                    grown = jnp.exp(held[b] - top)
                    here = fold(grown, jnp.sum)
                    bulk = here if bulk is None else bulk + here
                    value = values[b][half * HEAD_DIM : (half + 1) * HEAD_DIM]
                    part = dot(value, grown.astype(LOW))
                    total = part if total is None else total + part
                bulk = jnp.sum(bulk, axis=0, keepdims=True)
                parts.append(total * (1.0 / bulk))
                row = pair * 2 + half
                norm_ref[row : row + 1, :] = top + jnp.log(bulk)
        mixed = jnp.concatenate(parts).T.astype(LOW)
        mixed_ref[...] = mixed
        copy.wait()
        part_ref[...] = dot_nt(mixed, w_ref[...]).astype(LOW)

    return kernel_call(
        kernel,
        (query, q_marks, *pairs, *k_marks, weights),
        [out((rows, width)), out((8, rows), WIDE), out((rows, weights.shape[0]))],
        [
            pltpu.VMEM((blocks, size, rows), WIDE),
            pltpu.VMEM((weights.shape[0], width), LOW),
            pltpu.SemaphoreType.DMA((1,)),
        ], cost=4.0,
        apart=1,
    )


def attend_back(layer, grads, part, arrived, middle, gain, weights, query, q_marks, norms, pairs, k_marks):
    rows, width = query.shape
    depth = middle.shape[1]
    heads = width // HEAD_DIM
    blocks = len(pairs)
    size = pairs[0].shape[0]
    scale = HEAD_DIM ** (-0.5)
    near = blocks // 2

    def kernel(grads_ref, part_ref, arrived_ref, middle_ref, gain_ref, q_ref, qm_ref, norm_ref, *refs):
        kv_refs, km_refs = refs[:blocks], refs[blocks : 2 * blocks]
        w_far, *refs = refs[2 * blocks :]
        gm_ref, low_ref, sums_ref, dq_ref, own_ref, away_ref, *refs = refs
        p_wide, w_wide, p_all, s_all, weight_ref, sems = refs
        (copy,) = start_copies([(w_far.at[:, 3 * width :], weight_ref)], sems)
        incoming = part_ref[...].astype(WIDE) + arrived_ref[...].astype(WIDE)
        gain_grad, shift_grad, through = norm_backward(
            incoming, middle_ref[...], gain_ref[layer : layer + 1, :]
        )
        g_middle = grads_ref[...].astype(WIDE) + through
        low = g_middle.astype(LOW)
        gm_ref[...] = g_middle
        low_ref[...] = low
        sums_ref[0:1, :] = gain_grad
        sums_ref[1:2, :] = shift_grad
        sums_ref[2:3, :] = jnp.sum(g_middle, axis=0, keepdims=True)
        copy.wait()
        g_mixed = dot(low, weight_ref[...]).astype(LOW)
        dqs = []
        for pair in range(heads // 2):
            at = slice(pair * 128, pair * 128 + 128)
            to = slice(width + pair * 128, width + pair * 128 + 128)
            q, g = q_ref[:, at], g_mixed[:, at]
            keys = [turned(kv[:, at]) for kv in kv_refs]
            q_stack, g_stack = [], []
            for half in range(2):
                lanes = head_lanes(half)
                q_stack.append(only(lanes, q))
                g_stack.append(only(lanes, g))
                q_one = jnp.concatenate([q_stack[half], qm_ref[...]], axis=1)
                row = pair * 2 + half
                norm = norm_ref[row : row + 1, :]
                total = None
                for b in range(blocks):
                    key = jnp.concatenate([kv_refs[b][:, at], km_refs[b][...]], axis=1)
                    probs = jnp.exp(dot_nt(key, q_one) - norm)
                    weighed = probs * dot_nt(kv_refs[b][:, to], g_stack[half])
                    here = fold(weighed, jnp.sum)
                    total = here if total is None else total + here
                    p_wide[b] = probs
                    w_wide[b] = weighed
                    p_all[b * size : (b + 1) * size, half * rows : (half + 1) * rows] = probs.astype(LOW)
                total = jnp.sum(total, axis=0, keepdims=True)
                dq = None
                for b in range(blocks):
                    g_scores = (w_wide[b] - p_wide[b] * total).astype(LOW)
                    s_all[b * size : (b + 1) * size, half * rows : (half + 1) * rows] = g_scores
                    part = dot(keys[b][half * HEAD_DIM : (half + 1) * HEAD_DIM], g_scores)
                    dq = part if dq is None else dq + part
                dqs.append(dq)
            dk = dot(s_all[...], jnp.concatenate(q_stack)).astype(LOW)
            dv = dot(p_all[...], jnp.concatenate(g_stack)).astype(LOW)
            own_ref[:, at] = dk[: near * size]
            away_ref[:, at] = dk[near * size :]
            own_ref[:, to] = dv[: near * size]
            away_ref[:, to] = dv[near * size :]
        dq_ref[...] = (jnp.concatenate(dqs).T * scale).astype(LOW)

    half_rows = near * size
    length = blocks * size
    return kernel_call(
        kernel,
        (grads, part, arrived, middle, gain, query, q_marks, norms, *pairs, *k_marks, weights),
        [
            out((rows, depth), WIDE),
            out((rows, depth)),
            out((8, depth), WIDE),
            out((rows, width)),
            out((half_rows, 2 * width)),
            out((half_rows, 2 * width)),
        ],
        [
            pltpu.VMEM((blocks, size, rows), WIDE),
            pltpu.VMEM((blocks, size, rows), WIDE),
            pltpu.VMEM((length, 2 * rows), LOW),
            pltpu.VMEM((length, 2 * rows), LOW),
            pltpu.VMEM((depth, width), LOW),
            pltpu.SemaphoreType.DMA((1,)),
        ], cost=1.0,
        room=14,
        apart=1,
    )


def local(
    hidden_in,
    time_embed,
    segment_ids,
    cotangent,
    query_weight,
    key_weight,
    value_weight,
    output_weight,
    up_weight,
    down_weight,
    query_bias,
    value_bias,
    output_bias,
    up_bias,
    down_bias,
    first_gain,
    first_shift,
    second_gain,
    second_shift,
):
    rows, depth = hidden_in.shape
    layers, _, head_width = query_weight.shape
    hidden_width = up_weight.shape[2]
    place = lax.axis_index("tensor")
    core = (place % 2).reshape(1)
    side = (place // 2).reshape(1)
    place = place.reshape(1)
    ring = Ring()
    last = layers - 1

    near_own = pack_near((query_weight, key_weight, value_weight, output_weight))
    near_peer = swap_core(near_own)
    hidden_other = swap_y(hidden_in)
    pieces = weave_near(core, near_own, near_peer)
    near = [Gather(ring, pieces[0])]
    near[0].step()
    if ring.use:
        (_, query_bias, value_bias, up_bias, segment_ids, cotangent, up_weight, down_weight) = tie(
            near[0].current,
            query_bias,
            value_bias,
            up_bias,
            segment_ids,
            cotangent,
            up_weight,
            down_weight,
        )
    far_own = (up_weight, jnp.swapaxes(down_weight, 1, 2))
    far_pieces = weave_far(core, far_own, [swap_core(piece) for piece in far_own])
    near[0].step()
    near[0].step()
    token = near[0].current if ring.use else None
    cotangent_other = swap_y(tie(cotangent, token)[0] if ring.use else cotangent)
    near[0].finish()
    far = [Gather(ring, far_pieces[0])]
    far[0].step(token)
    biases = jnp.concatenate([query_bias, value_bias, up_bias], axis=1)
    q_bias, v_bias, u_bias = weave_bias(core, biases, swap_core(biases), head_width)
    q_marks, k_marks = mark_documents(core, segment_ids, rows)
    near.append(Gather(ring, pieces[1]))
    far.append(Gather(ring, far_pieces[1]))

    def exchange(parts):
        arrived = [swap_y(part) for part in parts]
        arrived[0], parts[1] = tie(arrived[0], parts[1])
        return arrived

    kept = []
    for layer in range(layers):
        w_near = near[layer].whole
        if layer == 0:
            states, firsts, queries, pairs = project_first(
                side, hidden_in, hidden_other, time_embed, first_gain, first_shift, w_near, q_bias, v_bias
            )
            seeds = None
        else:
            made = [
                project(
                    layer,
                    middles[j],
                    branches[j],
                    arrived[j],
                    down_bias,
                    first_gain,
                    first_shift,
                    w_near,
                    q_bias,
                    v_bias,
                )
                for j in range(2)
            ]
            states, firsts, queries, pairs = ([m[i] for m in made] for i in range(4))
        pairs = list(pairs) + [swap_core(pair) for pair in pairs]
        mixeds, norms, parts = [], [], []
        far[layer].step(queries[1])
        for j in range(2):
            mixed, norm, part = attend(queries[j], q_marks[j], pairs, k_marks, w_near)
            mixeds.append(mixed)
            norms.append(norm)
            parts.append(part)
        far[layer].step(parts[1])
        arrived = [swap_y(part) for part in parts]
        if layer == 0:
            token = far[0].current if ring.use else None
            near[1].step(token)
        far[layer].finish()
        if layer == 0:
            near[1].step(far[0].current)
        w_far = far[layer].whole
        arrived[0], w_far = tie(arrived[0], w_far)
        if layer == 0:
            seed0, seed1, seed_sums = seed_rows(side, cotangent, cotangent_other, k_marks[:2])
            seeds = [seed0, seed1]
        made = []
        for j in range(2):
            made.append(
                feed(
                    layer,
                    states[j],
                    parts[j],
                    arrived[j],
                    output_bias,
                    second_gain,
                    second_shift,
                    w_far,
                    u_bias,
                    seeds[j] if layer == last else None,
                )
            )
            if layer == 0 and j == 0:
                near[1].step(made[j][4])
        middles, seconds, acts, others, branches = ([m[i] for m in made] for i in range(5))
        kept.append((states, firsts, queries, pairs, norms, mixeds, middles, seconds, acts, others))
        if layer < last:
            arrived = [swap_y(branch) for branch in branches]
            arrived[0], branches[1] = tie(arrived[0], branches[1])
            token = near[1].current if ring.use else None
            near[1].finish()
            far[1].step(token)

    entries = [(12 * last + 5, ("one", 0), (seed_sums,))]
    up_sums = [m[5] for m in made]
    grads, lows, g_pres, parts = seeds, seeds, others, branches
    under_way, results = [], {}

    def advance(main):
        for scatter in under_way:
            main = scatter.step(main)
        return main

    for layer in reversed(range(layers)):
        (states, firsts, queries, pairs, norms, mixeds, middles, seconds, acts, slopes) = kept[layer]
        w_near = near[layer].whole
        w_far = far[layer].whole
        base = 12 * layer
        if layer < last:
            made = []
            for j in range(2):
                if j == 1:
                    arrived[1] = advance(arrived[1])
                made.append(feed_back(
                    layer + 1,
                    g_middles[j],
                    parts[j],
                    arrived[j],
                    above[j],
                    first_gain,
                    slopes[j],
                    w_far,
                ))
            grads, lows, g_pres, parts, sums, up_sums = ([m[i] for m in made] for i in range(6))
            entries += [
                (base + 12, ("own", 0), sums),
                (base + 13, ("own", 1), sums),
                (base + 5, ("own", 2), sums),
            ]
        entries.append((base + 8, ("up", 0), up_sums))
        arrived = exchange(parts)
        if layer < last:
            arrived[0] = advance(arrived[0])
            feed_away, feed_own = outer_feed(core, seconds, g_pres, lows, acts)
            arrived[0], feed_own = tie(arrived[0], feed_own)
            got = swap_core(feed_away)
        made = []
        for j in range(2):
            if j == 1:
                if layer == last:
                    feed_away, feed_own = outer_feed(core, seconds, g_pres, lows, acts)
                    got = swap_core(feed_away)
                arrived[1], feed_own, got = tie(arrived[1], feed_own, got)
                under_way.append(Scatter(ring, [feed_own], [got]))
                results[layer, "feed"] = under_way[-1]
                arrived[1] = advance(arrived[1])
                if layer == last:
                    acts_after, _ = tie(acts, arrived[1])
                    away_rows, here_rows = last_branch(side, acts_after, w_far)
            made.append(
                attend_back(
                    layer,
                    grads[j],
                    parts[j],
                    arrived[j],
                    middles[j],
                    second_gain,
                    w_near,
                    queries[j],
                    q_marks[j],
                    norms[j],
                    pairs,
                    k_marks,
                )
            )
            if j == 0:
                g_pres, _ = tie(g_pres, made[0][1])
        g_middles, m_lows, sums, dqs, owns, aways = ([m[i] for m in made] for i in range(6))
        entries += [
            (base + 2, ("own", 0), sums),
            (base + 3, ("own", 1), sums),
            (base + 4, ("own", 2), sums),
        ]
        aways = [swap_core(away) for away in aways]
        if layer == last:
            aways[1] = advance(aways[1])
            aways[1], away_rows = tie(aways[1], away_rows)
            crossed = swap_y(away_rows)
        g_qkv, part0, part1, sums = project_back(side, dqs, owns, aways, w_near, layer == 0)
        entries += [(base + 6, ("half", 0), (sums,)), (base + 7, ("half", 1), (sums,))]
        if layer > 0:
            parts = [part0, part1]
            arrived = exchange(parts)
            above = states
        else:
            arrived = swap_y(part0)
        near_away = outer_heads(core, firsts, g_qkv, m_lows, mixeds, 1)
        near_got = swap_core(near_away)
        near_own = outer_heads(core, firsts, g_qkv, m_lows, mixeds, 0)
        results[layer, "near"] = Scatter(ring, [near_own], [near_got])
        under_way.append(results[layer, "near"])
        if layer == last:
            arrived[0], near_own, near_got = tie(arrived[0], near_own, near_got)
            arrived[0] = advance(arrived[0])
        else:
            results[0, "near"].step()
            flight = results[0, "near"].flying[0] if ring.use else near_own
            results[0, "near"].step(token=flight)
            results[0, "feed"].step(token=results[0, "near"].made[0])
            arrived, _ = tie(arrived, flight)
        if layer == last:
            denoised = last_rows(side, middles, here_rows, crossed, down_bias, layer)
    input_grad, sums = first_rows(side, part1, arrived, states, g_middles, first_gain)
    entries += [(0, ("one", 0), (sums,)), (1, ("one", 1), (sums,))]
    total = vector_rows(place, entries, layers, depth)
    if ring.use:
        for move_by in exchanges(ring.count):
            total = total + move_by(total)
    else:
        total = lax.psum(total, ("fsdp", "tensor"))
    vectors = vector_outputs(place, total, layers, head_width)
    up_out, down_out = matrix_outputs(
        [results[layer, "feed"].finish() for layer in range(layers)], hidden_width, False
    )
    down_out = jnp.swapaxes(down_out, 1, 2)
    heads = matrix_outputs([results[layer, "near"].finish() for layer in range(layers)], head_width, True)
    return (denoised, input_grad, *heads, up_out, down_out, *vectors)


def solution(mesh):
    rows = P(("fsdp", "tensor"), None)
    inner = P(None, "fsdp", "tensor")
    outer = P(None, "tensor", "fsdp")
    cut = P(None, "tensor")
    in_specs = (
        rows,
        P("fsdp", None),
        P("fsdp", None),
        rows,
        inner,
        inner,
        inner,
        outer,
        inner,
        outer,
        cut,
        cut,
        P(),
        cut,
        P(),
        P(),
        P(),
        P(),
        P(),
    )
    out_specs = (
        rows,
        rows,
        inner,
        inner,
        inner,
        outer,
        inner,
        outer,
        cut,
        cut,
        P(),
        cut,
        P(),
        P(),
        P(),
        P(),
        P(),
    )
    return jax.shard_map(local, mesh=mesh, in_specs=in_specs, out_specs=out_specs, check_vma=False)
```

```python
import functools

import jax
import jax.numpy as jnp
from jax import lax
from jax.experimental import pallas as pl
from jax.experimental.pallas import tpu as pltpu
from jax.sharding import PartitionSpec as P

HEAD_DIM = 64
EPSILON = 1e-05
LOW = jnp.bfloat16
WIDE = jnp.float32
ROOT = 0.7978845608028654
CUBE = 0.044715

SWAP_CORE = [(0, 1), (1, 0), (2, 3), (3, 2)]
SWAP_Y = [(0, 2), (2, 0), (1, 3), (3, 1)]


def swap_core(value):
    return lax.ppermute(value, "tensor", SWAP_CORE)


def swap_y(value):
    return lax.ppermute(value, "tensor", SWAP_Y)


def dot(a, b):
    return jnp.dot(a, b, preferred_element_type=WIDE)


def dot_nt(a, b):
    return lax.dot_general(a, b, (((1,), (1,)), ((), ())), preferred_element_type=WIDE)


def dot_tn(a, b):
    return lax.dot_general(a, b, (((0,), (0,)), ((), ())), preferred_element_type=WIDE)


def tie(*values):
    return lax.optimization_barrier(values)


def ring_order(count):
    return list(range(0, count, 2)) + list(range(count - 1, 0, -2))


class Ring:
    def __init__(self):
        self.count = lax.axis_size("fsdp")
        self.use = self.count == 8
        self.core = lax.axis_index("tensor") % 2
        if self.use:
            here = lax.axis_index("fsdp")
            self.place = jnp.where(here % 2 == 0, here // 2, self.count - 1 - here // 2)
            self.way = 1 - 2 * self.core
            self.far = self.count // 2
            order = ring_order(self.count)
            self.pairs = [
                [(order[i], order[(i + way) % self.count]) for i in range(self.count)]
                for way in (1, -1)
            ]
            self.split = [
                (here * 4 + t, there * 4 + t)
                for t in range(4)
                for here, there in self.pairs[t % 2]
            ]
            self.blocks = jnp.stack([self.block_at(step) for step in range(self.count)])

    def split_send(self, value):
        return lax.ppermute(value, ("fsdp", "tensor"), self.split)

    def send_both(self, ahead, behind):
        return lax.ppermute(ahead, "fsdp", self.pairs[0]), lax.ppermute(behind, "fsdp", self.pairs[1])

    def block_at(self, steps):
        place = (self.place + steps + 2 * self.count) % self.count
        return jnp.where(place < self.count // 2, 2 * place, 2 * (self.count - 1 - place) + 1)


class Gather:
    def __init__(self, ring, piece):
        self.ring = ring
        self.rows, self.columns = piece.shape
        self.todo = []
        self.done = 0
        self.current = piece
        if ring.use:
            self.whole = jnp.zeros((ring.count * self.rows, self.columns), piece.dtype)
            self.put(piece, lax.axis_index("fsdp"))
        else:
            self.whole = lax.all_gather(piece, "fsdp", axis=0, tiled=True)

    def put(self, value, block, offset=0):
        start = block * self.rows + offset
        self.whole = lax.dynamic_update_slice(self.whole, value, (start, 0))

    def flush(self):
        ring = self.ring
        half = self.rows // 2
        for step, value in self.todo:
            if step < ring.far:
                self.put(value, ring.block_at(-ring.way * step))
                self.put(swap_core(value), ring.block_at(ring.way * step))
            else:
                block = ring.block_at(step)
                self.put(value, block, ring.core * half)
                self.put(swap_core(value), block, (1 - ring.core) * half)
        self.todo = []

    def step(self, token=None):
        ring = self.ring
        if not ring.use or self.done == ring.far:
            return
        self.flush()
        self.done += 1
        current = self.current
        if token is not None:
            current, _ = tie(current, token)
        if self.done == ring.far:
            half = self.rows // 2
            current = lax.dynamic_slice(current, (ring.core * half, 0), (half, self.columns))
        self.current = ring.split_send(current)
        self.todo.append((self.done, self.current))

    def finish(self):
        if self.ring.use:
            while self.done < self.ring.far:
                self.step()
            self.flush()


class Scatter:
    def __init__(self, ring, owns, gots):
        self.ring = ring
        self.owns, self.gots = owns, gots
        self.done = 0
        self.made = owns
        if ring.use:
            self.rows = owns[0].shape[0] // ring.count
        else:
            total = jnp.concatenate(
                [own.astype(WIDE) + got.astype(WIDE) for own, got in zip(owns, gots)], axis=1
            )
            self.result = lax.psum_scatter(total, "fsdp", scatter_dimension=0, tiled=True)

    def step(self, main=None, token=None):
        ring = self.ring
        if not ring.use or self.done > ring.far:
            return main
        moving = None
        if self.done:
            moving = self.flying
            if main is not None:
                main, *moving = tie(main, *moving)
        if self.done == ring.far:
            self.done += 1
            self.result = passing(ring.blocks, self.owns, self.gots, 0, ring.count, moving)[0]
            return main
        owns = self.owns
        if main is None and token is not None:
            owns, _ = tie(owns, token)
        made = passing(ring.blocks, owns, self.gots, ring.far - self.done, ring.count, moving)
        if main is not None:
            main, *made = tie(main, *made)
        self.made = made
        self.flying = ring.send_both(*made)
        self.done += 1
        return main

    def finish(self):
        if self.ring.use:
            while self.done <= self.ring.far:
                self.step()
        return self.result


def exchanges(count):
    moves = [swap_core, swap_y]
    bit = 1
    while bit < count:
        pairs = [(i, i ^ bit) for i in range(count)]
        moves.append(lambda value, pairs=pairs: lax.ppermute(value, "fsdp", pairs))
        bit *= 2
    return moves


NEVER = -1e30


def out(shape, dtype=LOW):
    return jax.ShapeDtypeStruct(shape, dtype)


def kernel_call(kernel, operands, outs, scratch=(), scalars=0, cost=1.0, room=8, apart=0):
    inside = pl.BlockSpec(memory_space=pltpu.VMEM)
    word = pl.BlockSpec(memory_space=pltpu.SMEM)
    return pl.pallas_call(
        kernel,
        in_specs=[word] * scalars
        + [inside] * (len(operands) - scalars - apart)
        + [pl.BlockSpec(memory_space=pl.ANY)] * apart,
        out_specs=[inside] * len(outs),
        out_shape=outs,
        scratch_shapes=scratch,
        compiler_params=pltpu.CompilerParams(vmem_limit_bytes=room << 20),
        cost_estimate=pl.CostEstimate(
            flops=int(cost * 1e9), bytes_accessed=1024, transcendentals=0
        ),
    )(*operands)


def start_copies(pairs, sems):
    copies = [
        pltpu.make_async_copy(source, target, sems.at[index])
        for index, (source, target) in enumerate(pairs)
    ]
    for copy in copies:
        copy.start()
    return copies


def norm_parts(rows):
    center = rows - jnp.mean(rows, axis=1, keepdims=True)
    factor = lax.rsqrt(jnp.mean(center * center, axis=1, keepdims=True) + EPSILON)
    return center * factor, factor


def norm_backward(grad, rows, gain):
    normed, factor = norm_parts(rows)
    scaled = grad * gain
    through = factor * (
        scaled
        - jnp.mean(scaled, axis=1, keepdims=True)
        - normed * jnp.mean(scaled * normed, axis=1, keepdims=True)
    )
    gain_grad = jnp.sum(grad * normed, axis=0, keepdims=True)
    return gain_grad, jnp.sum(grad, axis=0, keepdims=True), through


def gelu_both(pre):
    inner = jnp.tanh(ROOT * (pre + CUBE * pre * pre * pre))
    slope = 0.5 * (1.0 + inner) + 0.5 * pre * (1.0 - inner * inner) * (
        ROOT * (1.0 + 3.0 * CUBE * pre * pre)
    )
    return 0.5 * pre * (1.0 + inner), slope


def project(layer, base, part, arrived, bias, gain, shift, weights, q_bias, v_bias):
    rows, depth = base.shape
    width = q_bias.shape[1]
    scale = HEAD_DIM ** (-0.5)
    at = slice(layer, layer + 1)

    def kernel(base_ref, part_ref, arrived_ref, bias_ref, gain_ref, shift_ref, qb_ref, vb_ref, w_far,
               state_ref, first_ref, q_ref, kv_ref, w_ref, sems):
        (copy,) = start_copies([(w_far.at[:, : 3 * width], w_ref)], sems)
        state = base_ref[...] + (part_ref[...].astype(WIDE) + arrived_ref[...].astype(WIDE))
        state += bias_ref[layer - 1 : layer, :]
        first = (norm_parts(state)[0] * gain_ref[at, :] + shift_ref[at, :]).astype(LOW)
        state_ref[...] = state
        first_ref[...] = first
        copy.wait()
        query = (dot(first, w_ref[:, :width]) + qb_ref[at, :]).astype(LOW)
        q_ref[...] = query * jnp.asarray(scale, LOW)
        kv_ref[:, :width] = dot(first, w_ref[:, width : 2 * width]).astype(LOW)
        kv_ref[:, width:] = (dot(first, w_ref[:, 2 * width : 3 * width]) + vb_ref[at, :]).astype(LOW)

    return kernel_call(
        kernel,
        (base, part, arrived, bias, gain, shift, q_bias, v_bias, weights),
        [
            out((rows, depth), WIDE),
            out((rows, depth)),
            out((rows, width)),
            out((rows, 2 * width)),
        ], scratch=[pltpu.VMEM((depth, 3 * width), LOW), pltpu.SemaphoreType.DMA((1,))],
        cost=1.2,
        apart=1,
    )


def feed(layer, state, part, arrived, out_bias, gain, shift, weights, up_bias, lows=None):
    rows, depth = state.shape
    hidden = up_bias.shape[1]
    back = lows is not None
    half = hidden // 2
    tile = 384
    row = slice(layer, layer + 1)

    def kernel(*refs):
        state_ref, part_ref, arrived_ref, ob_ref, gain_ref, shift_ref, w_ref, ub_ref = refs[:8]
        refs = refs[8:]
        middle = (
            state_ref[...] + (part_ref[...].astype(WIDE) + arrived_ref[...].astype(WIDE)) + ob_ref[row, :]
        )
        second = (norm_parts(middle)[0] * gain_ref[row, :] + shift_ref[row, :]).astype(LOW)
        if back:
            lows_ref, middle_ref, second_ref, act_ref, other_ref, branch_ref, ubg_ref = refs
            low = lows_ref[...]
        else:
            middle_ref, second_ref, act_ref, other_ref, branch_ref = refs
        middle_ref[...] = middle
        second_ref[...] = second
        total = None
        for start in range(0, hidden, tile):
            at = slice(start, start + tile)
            inside = start + start // half * half
            up = w_ref[:, inside : inside + tile]
            down = w_ref[:, half + inside : half + inside + tile]
            act, slope = gelu_both(dot(second, up) + ub_ref[row, at])
            act = act.astype(LOW)
            act_ref[:, at] = act
            if back:
                other = (dot(low, down) * slope).astype(LOW)
                ubg_ref[0:1, at] = jnp.sum(other.astype(WIDE), axis=0, keepdims=True)
                here = dot_nt(other, up)
            else:
                other = slope.astype(LOW)
                here = dot_nt(act, down)
            other_ref[:, at] = other
            total = here if total is None else total + here
        branch_ref[...] = total.astype(LOW)

    operands = [state, part, arrived, out_bias, gain, shift, weights, up_bias]
    outs = [
        out((rows, depth), WIDE),
        out((rows, depth)),
        out((rows, hidden)),
        out((rows, hidden)),
        out((rows, depth)),
    ]
    if back:
        operands.append(lows)
        outs.append(out((8, hidden), WIDE))
    return kernel_call(kernel, operands, outs, cost=4.0)


def feed_back(layer, g_middle, part, arrived, state, gain, slopes, weights):
    rows, depth = state.shape
    hidden = slopes.shape[1]
    half = hidden // 2
    tile = 384

    def kernel(gm_ref, part_ref, arrived_ref, state_ref, gain_ref, slope_ref, w_ref,
               grad_ref, low_ref, gpre_ref, branch_ref, sums_ref, ubg_ref):
        incoming = part_ref[...].astype(WIDE) + arrived_ref[...].astype(WIDE)
        gain_grad, shift_grad, through = norm_backward(incoming, state_ref[...], gain_ref[layer : layer + 1, :])
        grad = gm_ref[...] + through
        low = grad.astype(LOW)
        grad_ref[...] = grad
        low_ref[...] = low
        sums_ref[0:1, :] = gain_grad
        sums_ref[1:2, :] = shift_grad
        sums_ref[2:3, :] = jnp.sum(grad, axis=0, keepdims=True)
        total = None
        for start in range(0, hidden, tile):
            at = slice(start, start + tile)
            inside = start + start // half * half
            up = w_ref[:, inside : inside + tile]
            down = w_ref[:, half + inside : half + inside + tile]
            gpre = (dot(low, down) * slope_ref[:, at].astype(WIDE)).astype(LOW)
            gpre_ref[:, at] = gpre
            ubg_ref[0:1, at] = jnp.sum(gpre.astype(WIDE), axis=0, keepdims=True)
            here = dot_nt(gpre, up)
            total = here if total is None else total + here
        branch_ref[...] = total.astype(LOW)

    return kernel_call(
        kernel,
        (g_middle, part, arrived, state, gain, slopes, weights),
        [
            out((rows, depth), WIDE),
            out((rows, depth)),
            out((rows, hidden)),
            out((rows, depth)),
            out((8, depth), WIDE),
            out((8, hidden), WIDE),
        ], cost=3.8)

def turned(value):
    return value.astype(WIDE).T.astype(LOW)


def outer_feed(core, seconds, g_pres, lows, acts):
    depth = seconds[0].shape[1]
    size = acts[0].shape[1] // 2

    def kernel(core_ref, s0, s1, g0, g1, l0, l1, a0, a1, *out_refs):
        for index, (left_refs, right_refs) in enumerate((((s0, s1), (g0, g1)), ((l0, l1), (a0, a1)))):
            left = jnp.concatenate([turned(ref[...]) for ref in left_refs], axis=1)
            for which, out_ref in ((1, out_refs[0]), (0, out_refs[1])):
                start = jnp.where(core_ref[0] == which, 0, size)
                for at in range(0, size, 384):
                    columns = pl.ds(pl.multiple_of(start + at, 128), 384)
                    right = jnp.concatenate([ref[:, columns] for ref in right_refs])
                    base = index * size + at
                    out_ref[:, base : base + 384] = dot(left, right).astype(LOW)

    return kernel_call(
        kernel,
        (core, *seconds, *g_pres, *lows, *acts),
        [out((depth, 2 * size))] * 2,
        scalars=1,
        cost=3.4,
    )


def outer_heads(core, firsts, g_qkv, m_lows, mixeds, which):
    depth = firsts[0].shape[1]
    width = mixeds[0].shape[1]
    size = width // 2

    def kernel(core_ref, f0, f1, g_ref, l0, l1, m0, m1, out_ref):
        low = core_ref[0] == which

        def pick(value):
            return jnp.where(low, value[:, :size], value[:, size:])

        first = jnp.concatenate([turned(f0[...]), turned(f1[...])], axis=1)
        g = g_ref[...]
        right = jnp.concatenate(
            [pick(g[:, i * width : (i + 1) * width]) for i in range(3)], axis=1
        )
        m_low = jnp.concatenate([turned(l0[...]), turned(l1[...])], axis=1)
        mixed = jnp.concatenate([pick(m0[...]), pick(m1[...])])
        out_ref[...] = jnp.concatenate([dot(first, right), dot(m_low, mixed)], axis=1).astype(LOW)

    return kernel_call(
        kernel, (core, *firsts, g_qkv, *m_lows, *mixeds), [out((depth, 4 * size))], scalars=1, cost=1.8)[0]


def passing(blocks, owns, gots, step, count, moving):
    parts = len(owns)
    rows = owns[0].shape[0] // count
    half = rows // 2
    columns = sum(own.shape[1] for own in owns)
    first = moving is None
    last = step == 0
    partial_in = not first and moving[0].shape[0] == half

    def kernel(blocks_ref, *refs):
        if first:
            moving_refs, refs = (), refs
        else:
            moving_refs, refs = refs[:2], refs[2:]
        own_refs, got_refs = refs[:parts], refs[parts : 2 * parts]
        out_refs, held, sems = refs[2 * parts : -1 - 2 * parts], refs[-1 - 2 * parts : -1], refs[-1]
        if first:
            wanted = [(step, 0, half), (step, half, half)]
        elif last:
            wanted = [(0, 0, rows)]
        else:
            wanted = [(step, 0, rows), ((count - step) % count, 0, rows)]
        pairs = []
        for index, (block, offset, size) in enumerate(wanted):
            start = pl.multiple_of(blocks_ref[block] * rows + offset, 16)
            for ref, target in zip((*own_refs, *got_refs), held):
                pairs.append((ref.at[pl.ds(start, size), :], target.at[index, pl.ds(0, size), :]))
        copies = start_copies(pairs, sems)
        for copy in copies:
            copy.wait()

        def here(index, size=rows):
            return jnp.concatenate(
                [
                    held[k][index, :size].astype(WIDE) + held[parts + k][index, :size].astype(WIDE)
                    for k in range(parts)
                ],
                axis=1,
            )

        if first:
            out_refs[0][...] = here(0, half).astype(LOW)
            out_refs[1][...] = here(1, half).astype(LOW)
        elif last:
            total = here(0) + moving_refs[0][...].astype(WIDE) + moving_refs[1][...].astype(WIDE)
            out_refs[0][...] = total
        else:
            ahead, behind = here(0), here(1)
            a, b = moving_refs[0][...].astype(WIDE), moving_refs[1][...].astype(WIDE)
            if partial_in:
                out_refs[0][:half, :] = (ahead[:half] + a).astype(LOW)
                out_refs[0][half:, :] = ahead[half:].astype(LOW)
                out_refs[1][:half, :] = behind[:half].astype(LOW)
                out_refs[1][half:, :] = (behind[half:] + b).astype(LOW)
            else:
                out_refs[0][...] = (ahead + a).astype(LOW)
                out_refs[1][...] = (behind + b).astype(LOW)

    if last:
        outs = [out((rows, columns), WIDE)]
    else:
        outs = [out((half if first else rows, columns))] * 2
    operands = (blocks, *(() if first else moving), *owns, *gots)
    return kernel_call(
        kernel,
        operands,
        outs,
        [pltpu.VMEM((2, rows, own.shape[1]), LOW) for own in (*owns, *gots)]
        + [pltpu.SemaphoreType.DMA((4 * parts,))],
        scalars=1,
        cost=0.8,
        apart=2 * parts,
    )


def pack_near(weights):
    layers, rows, size = weights[0].shape

    def kernel(*refs):
        out_ref, held, sems = refs[4], refs[5:9], refs[9]
        copies = [
            pltpu.make_async_copy(refs[i], held[i], sems.at[i]) for i in range(4)
        ]
        for copy in copies:
            copy.start()
        for copy in copies:
            copy.wait()
        q_ref, k_ref, v_ref, o_ref = held
        for layer in range(layers):
            out_ref[layer] = jnp.concatenate(
                [q_ref[layer], k_ref[layer], v_ref[layer], turned(o_ref[layer])], axis=1
            )

    return pl.pallas_call(
        kernel,
        in_specs=[pl.BlockSpec(memory_space=pltpu.HBM)] * 4,
        out_specs=pl.BlockSpec(memory_space=pltpu.VMEM),
        out_shape=out((layers, rows, 4 * size)),
        scratch_shapes=[pltpu.VMEM(w.shape, LOW) for w in weights]
        + [pltpu.SemaphoreType.DMA((4,))],
        compiler_params=pltpu.CompilerParams(vmem_limit_bytes=8 << 20),
        cost_estimate=pl.CostEstimate(flops=1000, bytes_accessed=1024, transcendentals=0),
    )(*weights)


def weave_near(core, own, peer):
    layers, rows, columns = own.shape
    size = columns // 4

    def kernel(core_ref, own_ref, peer_ref, *out_refs):
        first = core_ref[0] == 0
        for layer, out_ref in enumerate(out_refs):
            a, b = own_ref[layer], peer_ref[layer]
            low, high = jnp.where(first, a, b), jnp.where(first, b, a)
            parts = []
            for i in range(4):
                parts += [low[:, i * size : (i + 1) * size], high[:, i * size : (i + 1) * size]]
            out_ref[...] = jnp.concatenate(parts, axis=1)

    return kernel_call(
        kernel, (core, own, peer), [out((rows, 2 * columns))] * layers, scalars=1
    )


def weave_far(core, own, peer):
    layers, rows, columns = own[0].shape

    def kernel(core_ref, u_own, d_own, u_peer, d_peer, *out_refs):
        first = core_ref[0] == 0
        for layer, out_ref in enumerate(out_refs):
            for index, (own_ref, peer_ref) in enumerate(((u_own, u_peer), (d_own, d_peer))):
                a, b = own_ref[layer], peer_ref[layer]
                low, high = index * columns, (2 + index) * columns
                out_ref[:, low : low + columns] = jnp.where(first, a, b)
                out_ref[:, high : high + columns] = jnp.where(first, b, a)

    return kernel_call(
        kernel, (core, *own, *peer), [out((rows, 4 * columns))] * layers, scalars=1
    )


def weave_bias(core, own, peer, size):
    layers = own.shape[0]
    rest = own.shape[1] - 2 * size

    def kernel(core_ref, own_ref, peer_ref, q_ref, v_ref, u_ref):
        first = core_ref[0] == 0
        a, b = own_ref[...], peer_ref[...]
        low, high = jnp.where(first, a, b), jnp.where(first, b, a)
        q_ref[...] = jnp.concatenate([low[:, :size], high[:, :size]], axis=1)
        v_ref[...] = jnp.concatenate([low[:, size : 2 * size], high[:, size : 2 * size]], axis=1)
        u_ref[...] = jnp.concatenate([low[:, 2 * size :], high[:, 2 * size :]], axis=1)

    return kernel_call(
        kernel,
        (core, own, peer),
        [
            out((layers, 2 * size), WIDE),
            out((layers, 2 * size), WIDE),
            out((layers, 2 * rest), WIDE),
        ],
        scalars=1,
    )


def mark_documents(core, segments, rows):
    def kernel(core_ref, segment_ref, *refs):
        core = core_ref[0]
        blocks = [core, 2 + core, 1 - core, 3 - core]
        lane = lax.broadcasted_iota(jnp.int32, (128, rows), 0)
        for index, block in enumerate(blocks):
            at = pl.ds(pl.multiple_of(block * rows, 128), rows)
            mark = jnp.where(lane == segment_ref[:, at] + 1, 1.0, 0.0).T
            refs[2 + index][...] = mark.astype(LOW)
            if index < 2:
                real = lax.broadcasted_iota(jnp.int32, (rows, 128), 1) < 9
                refs[index][...] = jnp.where(real & (mark == 0.0), NEVER, 0.0).astype(LOW)

    made = kernel_call(kernel, (core, segments), [out((rows, 128))] * 6, scalars=1)
    return made[:2], made[2:]


def seed_rows(side, own, other, marks):
    rows, depth = own.shape

    def kernel(side_ref, own_ref, other_ref, m0, m1, low0, low1, sums_ref):
        total = None
        for j, (mark, low) in enumerate(((m0, low0), (m1, low1))):
            mine = side_ref[0] == j
            value = jnp.where(mine, own_ref[...], other_ref[...])
            value = jnp.where(mark[:, 0:1] > 0, jnp.zeros_like(value), value)
            low[...] = value
            here = jnp.sum(value.astype(WIDE), axis=0, keepdims=True)
            here = jnp.where(mine, here, 0.0)
            total = here if total is None else total + here
        sums_ref[0:1, :] = total

    return kernel_call(
        kernel,
        (side, own, other, *marks),
        [out((rows, depth)), out((rows, depth)), out((8, depth), WIDE)],
        scalars=1,
    )


def project_first(side, own, other, embed, gain, shift, weights, q_bias, v_bias):
    rows, depth = own.shape
    width = q_bias.shape[1]
    scale = HEAD_DIM ** (-0.5)

    def kernel(side_ref, own_ref, other_ref, embed_ref, gain_ref, shift_ref, qb_ref, vb_ref, w_far, *refs):
        w_ref, sems = refs[8:]
        (copy,) = start_copies([(w_far.at[:, : 3 * width], w_ref)], sems)
        firsts = []
        for j in range(2):
            rows_in = jnp.where(side_ref[0] == j, own_ref[...], other_ref[...])
            state = rows_in.astype(WIDE) + embed_ref[...].astype(WIDE)
            refs[j][...] = state
            first = (norm_parts(state)[0] * gain_ref[0:1, :] + shift_ref[0:1, :]).astype(LOW)
            refs[2 + j][...] = first
            firsts.append(first)
        first = jnp.concatenate(firsts)
        copy.wait()
        query = (dot(first, w_ref[:, :width]) + qb_ref[0:1, :]).astype(LOW)
        query = query * jnp.asarray(scale, LOW)
        key = dot(first, w_ref[:, width : 2 * width]).astype(LOW)
        value = (dot(first, w_ref[:, 2 * width : 3 * width]) + vb_ref[0:1, :]).astype(LOW)
        for j in range(2):
            at = slice(j * rows, (j + 1) * rows)
            refs[4 + j][...] = query[at]
            refs[6 + j][:, :width] = key[at]
            refs[6 + j][:, width:] = value[at]

    made = kernel_call(
        kernel,
        (side, own, other, embed, gain, shift, q_bias, v_bias, weights),
        [out((rows, depth), WIDE)] * 2
        + [out((rows, depth))] * 2
        + [out((rows, width))] * 2
        + [out((rows, 2 * width))] * 2,
        scalars=1, scratch=[pltpu.VMEM((depth, 3 * width), LOW), pltpu.SemaphoreType.DMA((1,))],
        cost=1.8,
        apart=1,
    )
    return [made[2 * i : 2 * i + 2] for i in range(4)]


def last_branch(side, acts, weights):
    rows, hidden = acts[0].shape
    depth = weights.shape[0]
    size = hidden // 2

    def kernel(side_ref, a0, a1, w_far, away_ref, here_ref, w_ref, sems):
        copies = start_copies(
            [(w_far.at[:, (2 * i + 1) * size : (2 * i + 2) * size], w_ref.at[i]) for i in range(2)], sems
        )
        for copy in copies:
            copy.wait()
        for flip, ref in ((1, away_ref), (0, here_ref)):
            act = jnp.where(side_ref[0] == flip, a0[...], a1[...])
            total = dot_nt(act[:, :size], w_ref[0])
            total += dot_nt(act[:, size:], w_ref[1])
            ref[...] = total.astype(ref.dtype)

    return kernel_call(
        kernel,
        (side, *acts, weights),
        [out((rows, depth)), out((rows, depth), WIDE)],
        scalars=1, scratch=[pltpu.VMEM((2, depth, size), LOW), pltpu.SemaphoreType.DMA((2,))],
        cost=1.4,
        apart=1,
    )


def last_rows(side, middles, here, crossed, bias, layer):
    rows, depth = here.shape

    def kernel(side_ref, m0, m1, here_ref, crossed_ref, bias_ref, out_ref):
        middle = jnp.where(side_ref[0] == 0, m0[...], m1[...])
        total = here_ref[...] + crossed_ref[...].astype(WIDE)
        out_ref[...] = (middle + total + bias_ref[layer : layer + 1, :]).astype(LOW)

    return kernel_call(
        kernel, (side, *middles, here, crossed, bias), [out((rows, depth))], scalars=1
    )[0]


def project_back(side, dqs, owns, aways, weights, last):
    rows, width = dqs[0].shape
    depth = weights.shape[0]

    def kernel(side_ref, dq0, dq1, own0, own1, away0, away1, w_far, g_ref, part0, part1, sums_ref, w_ref, sems):
        (copy,) = start_copies([(w_far.at[:, : 3 * width], w_ref)], sems)
        pair = (
            own0[...].astype(WIDE)
            + own1[...].astype(WIDE)
            + (away0[...].astype(WIDE) + away1[...].astype(WIDE))
        ).astype(LOW)
        g_ref[:rows, :width] = dq0[...]
        g_ref[rows:, :width] = dq1[...]
        g_ref[:, width:] = pair
        g = g_ref[...]
        copy.wait()
        total = dot_nt(g, w_ref[...])
        low, high = total[:rows], total[rows:]
        if last:
            part0[...] = jnp.where(side_ref[0] == 0, high, low).astype(LOW)
            part1[...] = jnp.where(side_ref[0] == 0, low, high)
        else:
            part0[...] = low.astype(LOW)
            part1[...] = high.astype(LOW)
        sums_ref[0:1, :] = jnp.sum(g[:, :width].astype(WIDE), axis=0, keepdims=True)
        sums_ref[1:2, :] = jnp.sum(pair[:, width:].astype(WIDE), axis=0, keepdims=True)

    return kernel_call(
        kernel,
        (side, *dqs, *owns, *aways, weights),
        [
            out((2 * rows, 3 * width)),
            out((rows, depth)),
            out((rows, depth), WIDE if last else LOW),
            out((8, width), WIDE),
        ],
        scalars=1, scratch=[pltpu.VMEM((depth, 3 * width), LOW), pltpu.SemaphoreType.DMA((1,))],
        cost=1.6,
        apart=1,
    )


def first_rows(side, here, arrived, states, g_middles, gain):
    rows, depth = here.shape

    def kernel(side_ref, here_ref, arrived_ref, s0, s1, g0, g1, gain_ref, out_ref, sums_ref):
        low = side_ref[0] == 0
        incoming = here_ref[...] + arrived_ref[...].astype(WIDE)
        state = jnp.where(low, s0[...], s1[...])
        gain_grad, shift_grad, through = norm_backward(incoming, state, gain_ref[0:1, :])
        out_ref[...] = jnp.where(low, g0[...], g1[...]) + through
        sums_ref[0:1, :] = gain_grad
        sums_ref[1:2, :] = shift_grad

    return kernel_call(
        kernel,
        (side, here, arrived, *states, *g_middles, gain),
        [out((rows, depth), WIDE), out((8, depth), WIDE)],
        scalars=1,
    )


def vector_rows(place, entries, layers, depth):
    arrays = [array for _, _, group in entries for array in group]

    def kernel(place_ref, *refs):
        out_ref = refs[-1]
        place = place_ref[0]
        side = place // 2
        at = 0
        for row, (take, index), group in entries:
            here = refs[at : at + len(group)]
            at += len(group)
            if take == "own":
                value = jnp.where(side == 0, here[0][index : index + 1, :], here[1][index : index + 1, :])
                out_ref[row : row + 1, :] = value
            elif take == "one":
                out_ref[row : row + 1, :] = here[0][index : index + 1, :]
            elif take == "half":
                value = here[0][index : index + 1, :]
                zero = jnp.zeros_like(value)
                out_ref[row : row + 1, :] = jnp.concatenate(
                    [jnp.where(side == 0, value, zero), jnp.where(side == 0, zero, value)], axis=1
                )
            else:
                value = here[0][0:1, :] + here[1][0:1, :]
                for t in range(4):
                    here_row = value[:, t % 2 * depth : (t % 2 + 1) * depth]
                    out_ref[row + t : row + t + 1, :] = jnp.where(side == t // 2, here_row, 0.0)

    return kernel_call(
        kernel, (place, *arrays), [out((12 * layers, depth), WIDE)], scalars=1
    )[0]


def vector_outputs(place, total, layers, size):
    depth = total.shape[1]

    def kernel(place_ref, total_ref, qb, vb, ob, ub, db, fg, fs, sg, ss):
        place = place_ref[0]

        def pick(values):
            result = values[0]
            for t in range(1, 4):
                result = jnp.where(place == t, values[t], result)
            return result

        for layer in range(layers):
            at = slice(layer, layer + 1)
            row = lambda i: total_ref[12 * layer + i : 12 * layer + i + 1, :]
            for ref, i in ((fg, 0), (fs, 1), (sg, 2), (ss, 3), (ob, 4), (db, 5)):
                ref[at, :] = row(i)
            for ref, i in ((qb, 6), (vb, 7)):
                value = row(i)
                ref[at, :] = pick([value[:, t * size : (t + 1) * size] for t in range(4)])
            ub[at, :] = pick([row(8 + t) for t in range(4)])

    small, large = out((layers, size), WIDE), out((layers, depth), WIDE)
    return kernel_call(
        kernel, (place, total), [small, small] + [large] * 7, scalars=1
    )


def matrix_outputs(results, size, turn):
    layers = len(results)
    rows, columns = results[0].shape
    count = columns // size

    def kernel(*refs):
        for layer in range(layers):
            value = refs[layer][...].astype(WIDE)
            for i in range(count):
                part = value[:, i * size : (i + 1) * size]
                refs[layers + i][layer] = part.T if turn and i == count - 1 else part

    return kernel_call(
        kernel,
        results,
        [out((layers, rows, size), WIDE)] * (count - 1)
        + [out((layers, size, rows) if turn else (layers, rows, size), WIDE)],
    )


def head_lanes(half):
    lane = lax.broadcasted_iota(jnp.int32, (1, 128), 1)
    return (lane >= half * HEAD_DIM) & (lane < (half + 1) * HEAD_DIM)


def only(mask, value):
    return jnp.where(mask, value, jnp.zeros_like(value))


def fold(value, reduce):
    return reduce(value.reshape(value.shape[0] // 8, 8, value.shape[1]), axis=0)


def attend(query, q_marks, pairs, k_marks, weights):
    rows, width = query.shape
    heads = width // HEAD_DIM
    blocks = len(pairs)
    size = pairs[0].shape[0]

    def kernel(q_ref, qm_ref, *refs):
        kv_refs, km_refs = refs[:blocks], refs[blocks : 2 * blocks]
        w_far, mixed_ref, norm_ref, part_ref, held, w_ref, sems = refs[2 * blocks :]
        (copy,) = start_copies([(w_far.at[:, 3 * width :], w_ref)], sems)
        parts = []
        for pair in range(heads // 2):
            at = slice(pair * 128, pair * 128 + 128)
            to = slice(width + pair * 128, width + pair * 128 + 128)
            q = q_ref[:, at]
            values = [turned(kv[:, to]) for kv in kv_refs]
            for half in range(2):
                q_one = jnp.concatenate([only(head_lanes(half), q), qm_ref[...]], axis=1)
                top = None
                for b in range(blocks):
                    key = jnp.concatenate([kv_refs[b][:, at], km_refs[b][...]], axis=1)
                    scores = dot_nt(key, q_one)
                    held[b] = scores
                    here = fold(scores, jnp.max)
                    top = here if top is None else jnp.maximum(top, here)
                top = jnp.max(top, axis=0, keepdims=True)
                total, bulk = None, None
                for b in range(blocks):
                    grown = jnp.exp(held[b] - top)
                    here = fold(grown, jnp.sum)
                    bulk = here if bulk is None else bulk + here
                    value = values[b][half * HEAD_DIM : (half + 1) * HEAD_DIM]
                    part = dot(value, grown.astype(LOW))
                    total = part if total is None else total + part
                bulk = jnp.sum(bulk, axis=0, keepdims=True)
                parts.append(total * (1.0 / bulk))
                row = pair * 2 + half
                norm_ref[row : row + 1, :] = top + jnp.log(bulk)
        mixed = jnp.concatenate(parts).T.astype(LOW)
        mixed_ref[...] = mixed
        copy.wait()
        part_ref[...] = dot_nt(mixed, w_ref[...]).astype(LOW)

    return kernel_call(
        kernel,
        (query, q_marks, *pairs, *k_marks, weights),
        [out((rows, width)), out((8, rows), WIDE), out((rows, weights.shape[0]))],
        [
            pltpu.VMEM((blocks, size, rows), WIDE),
            pltpu.VMEM((weights.shape[0], width), LOW),
            pltpu.SemaphoreType.DMA((1,)),
        ], cost=4.0,
        apart=1,
    )


def attend_back(layer, grads, part, arrived, middle, gain, weights, query, q_marks, norms, pairs, k_marks):
    rows, width = query.shape
    depth = middle.shape[1]
    heads = width // HEAD_DIM
    blocks = len(pairs)
    size = pairs[0].shape[0]
    scale = HEAD_DIM ** (-0.5)
    near = blocks // 2

    def kernel(grads_ref, part_ref, arrived_ref, middle_ref, gain_ref, q_ref, qm_ref, norm_ref, *refs):
        kv_refs, km_refs = refs[:blocks], refs[blocks : 2 * blocks]
        w_far, *refs = refs[2 * blocks :]
        gm_ref, low_ref, sums_ref, dq_ref, own_ref, away_ref, *refs = refs
        p_wide, w_wide, p_all, s_all, weight_ref, sems = refs
        (copy,) = start_copies([(w_far.at[:, 3 * width :], weight_ref)], sems)
        incoming = part_ref[...].astype(WIDE) + arrived_ref[...].astype(WIDE)
        gain_grad, shift_grad, through = norm_backward(
            incoming, middle_ref[...], gain_ref[layer : layer + 1, :]
        )
        g_middle = grads_ref[...].astype(WIDE) + through
        low = g_middle.astype(LOW)
        gm_ref[...] = g_middle
        low_ref[...] = low
        sums_ref[0:1, :] = gain_grad
        sums_ref[1:2, :] = shift_grad
        sums_ref[2:3, :] = jnp.sum(g_middle, axis=0, keepdims=True)
        copy.wait()
        g_mixed = dot(low, weight_ref[...]).astype(LOW)
        dqs = []
        for pair in range(heads // 2):
            at = slice(pair * 128, pair * 128 + 128)
            to = slice(width + pair * 128, width + pair * 128 + 128)
            q, g = q_ref[:, at], g_mixed[:, at]
            keys = [turned(kv[:, at]) for kv in kv_refs]
            q_stack, g_stack = [], []
            for half in range(2):
                lanes = head_lanes(half)
                q_stack.append(only(lanes, q))
                g_stack.append(only(lanes, g))
                q_one = jnp.concatenate([q_stack[half], qm_ref[...]], axis=1)
                row = pair * 2 + half
                norm = norm_ref[row : row + 1, :]
                total = None
                for b in range(blocks):
                    key = jnp.concatenate([kv_refs[b][:, at], km_refs[b][...]], axis=1)
                    probs = jnp.exp(dot_nt(key, q_one) - norm)
                    weighed = probs * dot_nt(kv_refs[b][:, to], g_stack[half])
                    here = fold(weighed, jnp.sum)
                    total = here if total is None else total + here
                    p_wide[b] = probs
                    w_wide[b] = weighed
                    p_all[b * size : (b + 1) * size, half * rows : (half + 1) * rows] = probs.astype(LOW)
                total = jnp.sum(total, axis=0, keepdims=True)
                dq = None
                for b in range(blocks):
                    g_scores = (w_wide[b] - p_wide[b] * total).astype(LOW)
                    s_all[b * size : (b + 1) * size, half * rows : (half + 1) * rows] = g_scores
                    part = dot(keys[b][half * HEAD_DIM : (half + 1) * HEAD_DIM], g_scores)
                    dq = part if dq is None else dq + part
                dqs.append(dq)
            dk = dot(s_all[...], jnp.concatenate(q_stack)).astype(LOW)
            dv = dot(p_all[...], jnp.concatenate(g_stack)).astype(LOW)
            own_ref[:, at] = dk[: near * size]
            away_ref[:, at] = dk[near * size :]
            own_ref[:, to] = dv[: near * size]
            away_ref[:, to] = dv[near * size :]
        dq_ref[...] = (jnp.concatenate(dqs).T * scale).astype(LOW)

    half_rows = near * size
    length = blocks * size
    return kernel_call(
        kernel,
        (grads, part, arrived, middle, gain, query, q_marks, norms, *pairs, *k_marks, weights),
        [
            out((rows, depth), WIDE),
            out((rows, depth)),
            out((8, depth), WIDE),
            out((rows, width)),
            out((half_rows, 2 * width)),
            out((half_rows, 2 * width)),
        ],
        [
            pltpu.VMEM((blocks, size, rows), WIDE),
            pltpu.VMEM((blocks, size, rows), WIDE),
            pltpu.VMEM((length, 2 * rows), LOW),
            pltpu.VMEM((length, 2 * rows), LOW),
            pltpu.VMEM((depth, width), LOW),
            pltpu.SemaphoreType.DMA((1,)),
        ], cost=1.0,
        room=14,
        apart=1,
    )


def local(
    hidden_in,
    time_embed,
    segment_ids,
    cotangent,
    query_weight,
    key_weight,
    value_weight,
    output_weight,
    up_weight,
    down_weight,
    query_bias,
    value_bias,
    output_bias,
    up_bias,
    down_bias,
    first_gain,
    first_shift,
    second_gain,
    second_shift,
):
    rows, depth = hidden_in.shape
    layers, _, head_width = query_weight.shape
    hidden_width = up_weight.shape[2]
    place = lax.axis_index("tensor")
    core = (place % 2).reshape(1)
    side = (place // 2).reshape(1)
    place = place.reshape(1)
    ring = Ring()
    last = layers - 1

    near_own = pack_near((query_weight, key_weight, value_weight, output_weight))
    near_peer = swap_core(near_own)
    hidden_other = swap_y(hidden_in)
    pieces = weave_near(core, near_own, near_peer)
    near = [Gather(ring, pieces[0])]
    near[0].step()
    if ring.use:
        (_, query_bias, value_bias, up_bias, segment_ids, cotangent, up_weight, down_weight) = tie(
            near[0].current,
            query_bias,
            value_bias,
            up_bias,
            segment_ids,
            cotangent,
            up_weight,
            down_weight,
        )
    far_own = (up_weight, jnp.swapaxes(down_weight, 1, 2))
    far_pieces = weave_far(core, far_own, [swap_core(piece) for piece in far_own])
    near[0].step()
    near[0].step()
    token = near[0].current if ring.use else None
    cotangent_other = swap_y(tie(cotangent, token)[0] if ring.use else cotangent)
    near[0].finish()
    far = [Gather(ring, far_pieces[0])]
    far[0].step(token)
    biases = jnp.concatenate([query_bias, value_bias, up_bias], axis=1)
    q_bias, v_bias, u_bias = weave_bias(core, biases, swap_core(biases), head_width)
    q_marks, k_marks = mark_documents(core, segment_ids, rows)
    near.append(Gather(ring, pieces[1]))
    far.append(Gather(ring, far_pieces[1]))

    def exchange(parts):
        arrived = [swap_y(part) for part in parts]
        arrived[0], parts[1] = tie(arrived[0], parts[1])
        return arrived

    kept = []
    for layer in range(layers):
        w_near = near[layer].whole
        if layer == 0:
            states, firsts, queries, pairs = project_first(
                side, hidden_in, hidden_other, time_embed, first_gain, first_shift, w_near, q_bias, v_bias
            )
            seeds = None
        else:
            made = [
                project(
                    layer,
                    middles[j],
                    branches[j],
                    arrived[j],
                    down_bias,
                    first_gain,
                    first_shift,
                    w_near,
                    q_bias,
                    v_bias,
                )
                for j in range(2)
            ]
            states, firsts, queries, pairs = ([m[i] for m in made] for i in range(4))
        pairs = list(pairs) + [swap_core(pair) for pair in pairs]
        mixeds, norms, parts = [], [], []
        far[layer].step(queries[1])
        for j in range(2):
            mixed, norm, part = attend(queries[j], q_marks[j], pairs, k_marks, w_near)
            mixeds.append(mixed)
            norms.append(norm)
            parts.append(part)
        far[layer].step(parts[1])
        arrived = [swap_y(part) for part in parts]
        if layer == 0:
            token = far[0].current if ring.use else None
            near[1].step(token)
        far[layer].finish()
        if layer == 0:
            near[1].step(far[0].current)
        w_far = far[layer].whole
        arrived[0], w_far = tie(arrived[0], w_far)
        if layer == 0:
            seed0, seed1, seed_sums = seed_rows(side, cotangent, cotangent_other, k_marks[:2])
            seeds = [seed0, seed1]
        made = []
        for j in range(2):
            made.append(
                feed(
                    layer,
                    states[j],
                    parts[j],
                    arrived[j],
                    output_bias,
                    second_gain,
                    second_shift,
                    w_far,
                    u_bias,
                    seeds[j] if layer == last else None,
                )
            )
            if layer == 0 and j == 0:
                near[1].step(made[j][4])
        middles, seconds, acts, others, branches = ([m[i] for m in made] for i in range(5))
        kept.append((states, firsts, queries, pairs, norms, mixeds, middles, seconds, acts, others))
        if layer < last:
            arrived = [swap_y(branch) for branch in branches]
            arrived[0], branches[1] = tie(arrived[0], branches[1])
            token = near[1].current if ring.use else None
            near[1].finish()
            far[1].step(token)

    entries = [(12 * last + 5, ("one", 0), (seed_sums,))]
    up_sums = [m[5] for m in made]
    grads, lows, g_pres, parts = seeds, seeds, others, branches
    under_way, results = [], {}

    def advance(main):
        for scatter in under_way:
            main = scatter.step(main)
        return main

    for layer in reversed(range(layers)):
        (states, firsts, queries, pairs, norms, mixeds, middles, seconds, acts, slopes) = kept[layer]
        w_near = near[layer].whole
        w_far = far[layer].whole
        base = 12 * layer
        if layer < last:
            made = []
            for j in range(2):
                if j == 1:
                    arrived[1] = advance(arrived[1])
                made.append(feed_back(
                    layer + 1,
                    g_middles[j],
                    parts[j],
                    arrived[j],
                    above[j],
                    first_gain,
                    slopes[j],
                    w_far,
                ))
            grads, lows, g_pres, parts, sums, up_sums = ([m[i] for m in made] for i in range(6))
            entries += [
                (base + 12, ("own", 0), sums),
                (base + 13, ("own", 1), sums),
                (base + 5, ("own", 2), sums),
            ]
        entries.append((base + 8, ("up", 0), up_sums))
        arrived = exchange(parts)
        if layer < last:
            arrived[0] = advance(arrived[0])
            feed_away, feed_own = outer_feed(core, seconds, g_pres, lows, acts)
            arrived[0], feed_own = tie(arrived[0], feed_own)
            got = swap_core(feed_away)
        made = []
        for j in range(2):
            if j == 1:
                if layer == last:
                    feed_away, feed_own = outer_feed(core, seconds, g_pres, lows, acts)
                    got = swap_core(feed_away)
                arrived[1], feed_own, got = tie(arrived[1], feed_own, got)
                under_way.append(Scatter(ring, [feed_own], [got]))
                results[layer, "feed"] = under_way[-1]
                arrived[1] = advance(arrived[1])
                if layer == last:
                    acts_after, _ = tie(acts, arrived[1])
                    away_rows, here_rows = last_branch(side, acts_after, w_far)
            made.append(
                attend_back(
                    layer,
                    grads[j],
                    parts[j],
                    arrived[j],
                    middles[j],
                    second_gain,
                    w_near,
                    queries[j],
                    q_marks[j],
                    norms[j],
                    pairs,
                    k_marks,
                )
            )
            if j == 0:
                g_pres, _ = tie(g_pres, made[0][1])
        g_middles, m_lows, sums, dqs, owns, aways = ([m[i] for m in made] for i in range(6))
        entries += [
            (base + 2, ("own", 0), sums),
            (base + 3, ("own", 1), sums),
            (base + 4, ("own", 2), sums),
        ]
        aways = [swap_core(away) for away in aways]
        if layer == last:
            aways[1], away_rows = tie(aways[1], away_rows)
            crossed = swap_y(away_rows)
        g_qkv, part0, part1, sums = project_back(side, dqs, owns, aways, w_near, layer == 0)
        entries += [(base + 6, ("half", 0), (sums,)), (base + 7, ("half", 1), (sums,))]
        if layer > 0:
            parts = [part0, part1]
            arrived = exchange(parts)
            above = states
        else:
            arrived = swap_y(part0)
        near_away = outer_heads(core, firsts, g_qkv, m_lows, mixeds, 1)
        near_got = swap_core(near_away)
        near_own = outer_heads(core, firsts, g_qkv, m_lows, mixeds, 0)
        results[layer, "near"] = Scatter(ring, [near_own], [near_got])
        under_way.append(results[layer, "near"])
        if layer == last:
            arrived[0], near_own, near_got = tie(arrived[0], near_own, near_got)
            arrived[0] = advance(arrived[0])
        else:
            results[0, "near"].step()
            flight = results[0, "near"].flying[0] if ring.use else near_own
            results[0, "near"].step(token=flight)
            results[0, "feed"].step(token=results[0, "near"].made[0])
            arrived, _ = tie(arrived, flight)
        if layer == last:
            denoised = last_rows(side, middles, here_rows, crossed, down_bias, layer)
    input_grad, sums = first_rows(side, part1, arrived, states, g_middles, first_gain)
    entries += [(0, ("one", 0), (sums,)), (1, ("one", 1), (sums,))]
    total = vector_rows(place, entries, layers, depth)
    if ring.use:
        for move_by in exchanges(ring.count):
            total = total + move_by(total)
    else:
        total = lax.psum(total, ("fsdp", "tensor"))
    vectors = vector_outputs(place, total, layers, head_width)
    up_out, down_out = matrix_outputs(
        [results[layer, "feed"].finish() for layer in range(layers)], hidden_width, False
    )
    down_out = jnp.swapaxes(down_out, 1, 2)
    heads = matrix_outputs([results[layer, "near"].finish() for layer in range(layers)], head_width, True)
    return (denoised, input_grad, *heads, up_out, down_out, *vectors)


def solution(mesh):
    rows = P(("fsdp", "tensor"), None)
    inner = P(None, "fsdp", "tensor")
    outer = P(None, "tensor", "fsdp")
    cut = P(None, "tensor")
    in_specs = (
        rows,
        P("fsdp", None),
        P("fsdp", None),
        rows,
        inner,
        inner,
        inner,
        outer,
        inner,
        outer,
        cut,
        cut,
        P(),
        cut,
        P(),
        P(),
        P(),
        P(),
        P(),
    )
    out_specs = (
        rows,
        rows,
        inner,
        inner,
        inner,
        outer,
        inner,
        outer,
        cut,
        cut,
        P(),
        cut,
        P(),
        P(),
        P(),
        P(),
        P(),
    )
    return jax.shard_map(local, mesh=mesh, in_specs=in_specs, out_specs=out_specs, check_vma=False)
```
